512 devices in a mesh: samples: 128 (over y, z, core), genes: 4 (over x).
Axes of the slice: x: 4, y: 4, z: 16, core: 2. Of those that a mesh axis runs over, the one named last changes fastest.
Arguments:
- probes: float32 [64, 524288], P(None, ('samples', 'genes')), may hold values from -6 to 6
- dosages: bfloat16 [20480, 128, 128], P(('samples', 'genes')), may hold values from 0 to 2
- weights: float32 [10240, 128], P(('samples', 'genes')), may hold values from 0.02 to 0.1
- send_rows: int32 [512, 512, 24], P(('samples', 'genes')), may hold values from 0 to 1023
- tile_src: int32 [20480, 128], P(('samples', 'genes')), may hold values from 0 to 12288, as said below
- tile_gene: int32 [20480], P(('samples', 'genes')), may hold values from 0 to 19, as said below
Outputs:
- projected: float32 [64, 524288], P(None, ('samples', 'genes'))
- moments: float32 [2, 64, 10240], P(None, None, ('samples', 'genes'))
The draws below stay inside these ranges and needn't reach their ends.
Inputs may be any that keep to these rules, and one draw needn't show every extreme that they name: send_rows[o, r, j] is a row among device o's own 1024 samples, sent to device r in slot j. tile_src[t, c] is o * 24 + j, slot j of the rows device o sends to the holder of tile t, or 12288 for an empty slot. tile_gene[t] is a gene slot of the device holding tile t; it never falls along a device's tiles.
All inputs are finite; a program needn't handle non-finite values.
Results may differ from the reference program's by a relative error of at most 0.0003.
Values sent between devices are 32-bit elements; how exact they have to be, the bound alone decides.
No kernel may reach another device: no remote copies, remote signals or barrier semaphores. Data moves between devices by JAX's collectives and lax.ppermute only.
A program may use at most 64 MiB of HBM per device.

```python
import math
import jax
import jax.numpy as jnp
from jax import lax

RADEMACHER_COUNT = 64
VT = 128
TILE = 128
TILE_CAP = 40
GENE_CAP = 20
SLOT_CAP = 24
LOCAL_SUBJECTS = 1024
COHORT_SUBJECTS = 524288
GENES = 10240
TILES = 20480
DEVICES = 512


def tile_layout(key):
    base = jax.random.fold_in(key, 41)
    key_count, key_top, key_start, key_fill = jax.random.split(base, 4)
    counts = jax.random.randint(key_count, (DEVICES,), TILE_CAP // 4, TILE_CAP + 1)
    fullest = jax.random.randint(key_top, (), 0, DEVICES)
    counts = jnp.where(jnp.arange(DEVICES) == fullest, TILE_CAP, counts)
    starts = jax.random.randint(key_start, (DEVICES, TILE_CAP), 0, 5) < 2
    starts = starts.at[:, 0].set(True)
    fills = jax.random.randint(key_fill, (DEVICES, TILE_CAP), TILE // 8, TILE + 1)
    return (counts, starts, fills)


def draw_tile_gene(key, part):
    counts, starts, fills = tile_layout(key)
    slots = jnp.minimum(jnp.cumsum(starts.astype(jnp.int32), axis=1) - 1, GENE_CAP - 1)
    return slots.reshape(DEVICES * TILE_CAP).astype(jnp.int32)


def one_order(order_key):
    return jax.random.permutation(order_key, DEVICES * SLOT_CAP)


def draw_tile_src(key, part):
    counts, starts, fills = tile_layout(key)
    subject_indices = DEVICES * SLOT_CAP
    closing = jnp.concatenate([starts[:, 1:], jnp.ones((DEVICES, 1), dtype=bool)], axis=1)
    used_slots = jnp.where(closing, fills, TILE)
    live_tile = jnp.arange(TILE_CAP)[None, :] < counts[:, None]
    live = live_tile[:, :, None] & (jnp.arange(TILE)[None, None, :] < used_slots[:, :, None])
    order_keys = jax.random.split(jax.random.fold_in(key, 43), DEVICES)
    orders = jax.vmap(one_order)(order_keys)
    flat_index = jnp.arange(TILE_CAP * TILE) % subject_indices
    picked = orders[:, flat_index].reshape(DEVICES, TILE_CAP, TILE)
    return jnp.where(live, picked, subject_indices).reshape(DEVICES * TILE_CAP, TILE).astype(jnp.int32)


def touch_ends(entries, own_key, smallest, largest):
    spot = [jax.random.randint(jax.random.fold_in(own_key, axis), (), 0, length) for axis, length in enumerate(entries.shape)]
    main_axis = entries.shape.index(max(entries.shape))
    beside = spot[:main_axis] + [(spot[main_axis] + 1) % entries.shape[main_axis]] + spot[main_axis + 1:]
    return entries.at[tuple(spot)].set(smallest).at[tuple(beside)].set(largest)


def steps_of(key, extent, cuts, low, high):
    def one(position, blocks):
        draws = jax.random.uniform(jax.random.fold_in(jax.random.fold_in(key, 6), position), (blocks,), jnp.float32, low / len(cuts), high / len(cuts))
        return jnp.repeat(jnp.exp(draws), extent[position] // blocks).reshape((-1,) + (1,) * (len(extent) - position - 1))

    factor_of = one(*cuts[0])
    for cut in cuts[1:]:
        factor_of = factor_of * one(*cut)
    return factor_of


def noise(own_key, shape, deviation, most, cuts=(), kind=jnp.bfloat16):
    entries = jax.random.normal(own_key, shape, jnp.float32) * deviation
    if len(cuts) > 0:
        entries = steps_of(own_key, shape, cuts, -0.22, 0.18) * entries
    return jnp.clip(entries, min=-most, max=most).astype(kind)


def setup_inputs(seed: int = 0) -> dict:
    streams_of = jax.random.split(jax.random.key(seed), 7)
    probes = noise(streams_of[0], (RADEMACHER_COUNT, COHORT_SUBJECTS), 1.0, 6.0, ((1, 512),), jnp.float32)
    dosages = jnp.clip(2.0 * jax.random.uniform(streams_of[1], (TILES, VT, TILE), jnp.float32) ** steps_of(streams_of[1], (TILES, VT, TILE), ((0, 512),), -0.2, 0.2), 0.0, 2.0).astype(jnp.bfloat16)
    weights = jnp.clip(jnp.exp(math.log(0.1) - 1.609438 * jax.random.uniform(streams_of[2], (GENES, VT), jnp.float32) ** steps_of(streams_of[2], (GENES, VT), ((0, 512),), -0.2, 0.2)), 0.02, 0.1)
    send_rows = touch_ends(jax.random.randint(streams_of[3], (DEVICES, DEVICES, SLOT_CAP), 0, LOCAL_SUBJECTS), jax.random.fold_in(streams_of[3], 1), 0, LOCAL_SUBJECTS - 1).astype(jnp.int32)
    tile_src = draw_tile_src(jax.random.fold_in(streams_of[6], 71), 0)
    tile_gene = draw_tile_gene(jax.random.fold_in(streams_of[6], 71), 0)
    return {"probes": probes, "dosages": dosages, "weights": weights, "send_rows": send_rows, "tile_src": tile_src, "tile_gene": tile_gene}


def device_terms(random_vector_slab, dose_tiles, gene_weights, gene_slots):
    dense = dose_tiles.astype(jnp.float32)
    tile_scores = jnp.einsum("tcb,tvc->tbv", random_vector_slab, dense, precision=lax.Precision.HIGHEST)
    member = (gene_slots[None, :] == jnp.arange(GENE_CAP, dtype=jnp.int32)[:, None]).astype(jnp.float32)
    scores = jnp.einsum("gt,tbv->gbv", member, tile_scores, precision=lax.Precision.HIGHEST) * gene_weights[:, None, :]
    moment_one = jnp.sum(scores * scores, axis=2) / VT
    weighted = jnp.einsum("gt,gbv->tbv", member, scores * gene_weights[:, None, :], precision=lax.Precision.HIGHEST)
    arriving_product = jnp.einsum("tbv,tvc->tcb", weighted, dense, precision=lax.Precision.HIGHEST)
    moment_two = jnp.dot(member, jnp.sum(arriving_product * arriving_product, axis=1), precision=lax.Precision.HIGHEST) / TILE
    return moment_one, moment_two, arriving_product


def reference(probes, dosages, weights, send_rows, tile_src, tile_gene):
    subject_indices = DEVICES * SLOT_CAP
    random_test_vectors = jnp.concatenate([probes.T, jnp.zeros((1, RADEMACHER_COUNT), jnp.float32)], axis=0)
    source_map = tile_src.reshape(DEVICES, TILE_CAP, TILE)
    dose_tiles = dosages.reshape(DEVICES, TILE_CAP, VT, TILE)
    gene_weights = weights.reshape(DEVICES, GENE_CAP, VT)
    gene_slots = tile_gene.reshape(DEVICES, TILE_CAP)

    def device_step(accumulated_moment, inputs):
        device_rank, present_sender, dose_now, weight_now, slot_now = inputs
        keeper_devices_list = jnp.minimum(present_sender // SLOT_CAP, DEVICES - 1).astype(jnp.int32)
        slot_index = (present_sender % SLOT_CAP).astype(jnp.int32)
        local_subject_entries = send_rows[keeper_devices_list, device_rank, slot_index]
        allele_holder_patch = jnp.where(present_sender < subject_indices, keeper_devices_list * LOCAL_SUBJECTS + local_subject_entries, COHORT_SUBJECTS).astype(jnp.int32)
        random_vector_slab = random_test_vectors[allele_holder_patch]
        moment_one, moment_two, arriving_product = device_terms(random_vector_slab, dose_now, weight_now, slot_now)
        accumulated_moment = accumulated_moment.at[allele_holder_patch.reshape(-1)].add(arriving_product.reshape(-1, RADEMACHER_COUNT))
        return accumulated_moment, jnp.stack([moment_one, moment_two])

    start_total = jnp.zeros((COHORT_SUBJECTS + 1, RADEMACHER_COUNT), jnp.float32)
    accumulated_moment, stacked = lax.scan(device_step, start_total, (jnp.arange(DEVICES, dtype=jnp.int32), source_map, dose_tiles, gene_weights, gene_slots))
    projected = accumulated_moment[:COHORT_SUBJECTS].T
    moments = stacked.transpose(1, 3, 0, 2).reshape(2, RADEMACHER_COUNT, DEVICES * GENE_CAP)
    return projected, moments
```

```python
import jax
import jax.numpy as jnp
from jax import lax
from jax.experimental import pallas as pl
from jax.experimental.pallas import tpu as pltpu
from jax.sharding import Mesh, PartitionSpec as P

NY, NZ, NC, NX = 4, 16, 2, 4
PLANE = NY * NC * NX
DEV = NY * NZ * NC * NX
SLOTS = 24
LANE = 32
SRC = DEV * SLOTS
TILES = 40
TILE = 128
VT = 128
GENES = 20
PROBES = 64
ROWS = 1024
ZB = 128
ZCAP = 2 * (ZB - 1)
PB = 96
PCAP = 2 * (PB - 1)
ZBUF = 280
PBUF = 216
HOLD = PLANE * 2 * PB
F32 = jnp.float32
BF16 = jnp.bfloat16
I32 = jnp.int32
ALL = ("y", "z", "c", "x")
FLAT = ("y", "c", "x")


def iota(shape, dim):
    return lax.broadcasted_iota(I32, shape, dim)


def dot(a, b, ca=1, cb=0, **kw):
    return lax.dot_general(a, b, (((ca,), (cb,)), ((), ())), preferred_element_type=F32, **kw)


def ones_where(mask):
    return jnp.where(mask, 1.0, 0.0).astype(BF16)


def lanes64(shape):
    return iota(shape, 1) < PROBES


def fold(v):
    return v + pltpu.roll(v, PROBES, 1)


def split(v):
    high = v.astype(BF16).astype(F32)
    return jnp.where(lanes64(v.shape), high, v - high).astype(BF16)


def both(block):
    turned = pltpu.roll(block, PROBES, 1)
    left = lanes64(block.shape)
    return jnp.where(left, block, turned), jnp.where(left, turned, block)


def source_parts(ref, t, n):
    highs, lows, empties = [], [], []
    for i in range(n):
        p = ref[pl.ds(t * n + i, 1), :]
        o = (p * 43691) >> 20
        highs.append(o >> 2)
        lows.append((o & 3) * LANE + p - o * SLOTS)
        empties.append(p >= SRC)
    return highs, lows, empties


def one_hots(rows):
    return jnp.concatenate([ones_where(iota((128, 128), 0) == r) for r in rows], axis=1)


def used_kernel(src_ref, count_ref):
    count_ref[...] = jnp.zeros_like(count_ref)

    def step(t, carry):
        highs, lows, _ = source_parts(src_ref, t, 8)
        count_ref[...] += dot(one_hots(highs), one_hots(lows), 1, 1)
        return carry

    lax.fori_loop(0, TILES // 8, step, 0)


def place_kernel(src_ref, count_ref, addr_ref, again_ref):
    count = count_ref[...]
    again_ref[0, 0] = jnp.where(jnp.max(count) > 1.5, 1, 0)
    used = ones_where(count > 0.5)
    row, col = iota((128, 128), 0), iota((128, 128), 1)
    same = (row >> 5) == (col >> 5)
    before = dot(used, ones_where(same & (row < col)))
    number = dot(used, ones_where(same)).astype(BF16)
    earlier = ((row >> 5) == (col >> 5)) & ((row & 1) == (col & 1)) & (col < row)
    rank = jnp.minimum((dot(ones_where(earlier), number) + before).astype(I32), PCAP)
    relay = ((row >> 5) * NC + (row & 1)) * NX + (col >> 5)
    place = relay * (2 * PB) + rank + jnp.where(rank >= PB - 1, 1, 0)
    turned = jnp.transpose(place)
    high = turned >> 6
    table = jnp.concatenate([high, turned - (high << 6)], axis=0).astype(F32).astype(BF16)

    def step(t, carry):
        highs, lows, empties = source_parts(src_ref, t, 8)
        found = dot(table, one_hots(highs))
        for i in range(8):
            part = found[:, i * 128 : (i + 1) * 128]
            value = part[:128] * 64.0 + part[128:]
            value = jnp.sum(jnp.where(row == lows[i], value, 0.0), axis=0, keepdims=True)
            addr_ref[pl.ds(t * 8 + i, 1), :] = jnp.where(empties[i], HOLD, value.astype(I32))
        return carry

    lax.fori_loop(0, TILES // 8, step, 0)


def choose(index, lane):
    return jnp.concatenate(
        [ones_where(index == (lane + (128 * k + 1)).astype(F32)) for k in range(ROWS // 128)], axis=1
    )


def send_kernel(used_ref, rows_ref, probes_ref, out_ref, index_ref, place_ref, head_ref, value_ref):
    used = used_ref[...]
    flag = ones_where(used > 0.5)
    row, col = iota((128, 128), 0), iota((128, 128), 1)
    number = dot(flag, jnp.ones((128, 128), BF16))
    zrow, zcol = (row >> 1) & (NZ - 1), (col >> 1) & (NZ - 1)
    start = dot(ones_where((zrow == zcol) & (col < row)), number.astype(BF16))
    place = start + dot(flag, ones_where(row < col))
    place_ref[...] = jnp.where(used > 0.5, place.astype(I32), -1)
    value_ref[...] = (rows_ref[...] + 1).astype(F32)
    picked = dot(place, jnp.where(row == (col & 3) * LANE, 1.0, 0.0), precision=lax.Precision.HIGHEST)
    picked = jnp.where((col >> 2) == (row >> 5) * NC + (row & 1), picked, 0.0)
    zpick = jnp.where(iota((NZ, 128), 0) == ((iota((NZ, 128), 1) >> 1) & (NZ - 1)), 1.0, 0.0)
    starts = dot(zpick, picked, precision=lax.Precision.HIGHEST)
    total = dot(zpick, number, precision=lax.Precision.HIGHEST)
    head_ref[...] = jnp.where(iota((NZ, 128), 1) < PLANE, starts, total)
    high = probes_ref[...].astype(BF16)
    low = (probes_ref[...] - high.astype(F32)).astype(BF16)
    parts = jnp.concatenate([high, low], axis=0)
    at = iota((2 * ZB, 128), 0)
    want = jnp.where(at < ZB, at, at - 1)
    want = jnp.where((at & (ZB - 1)) == ZB - 1, -2, want)
    lane = iota((2 * ZB, 128), 1)
    ones = jnp.ones((128, 128), BF16)

    def step(z, carry):
        total = jnp.zeros((2 * ZB, 128), F32)
        for y in range(NY):
            for c in range(NC):
                i = y * (NZ * NC) + z * NC + c
                total += jnp.where(want == place_ref[pl.ds(i, 1), :], value_ref[pl.ds(i, 1), :], 0.0)
        top = jnp.floor(total * (1.0 / 32.0))
        index = dot(top.astype(BF16), ones) * 32.0 + dot((total - top * 32.0).astype(BF16), ones)
        index_ref[z] = index
        rows = fold(dot(choose(index, lane), parts, 1, 1))
        out_ref[z] = jnp.where(lanes64((ZB, 128)), rows[:ZB], rows[ZB:])
        out_ref[z, pl.ds(ZB - 1, 1), :] = head_ref[pl.ds(z, 1), :]
        return carry

    lax.fori_loop(0, NZ, step, 0)


def relay_kernel(in_ref, out_ref, head_out_ref, zbuf, pbuf, head_vmem, head):
    for z in range(NZ):
        left, right = both(in_ref[z])
        zbuf[pl.ds(z * ZBUF, ZB), :] = left
        zbuf[pl.ds(z * ZBUF + ZB - 1, ZB), :] = right
        head_vmem[pl.ds(z, 1), :] = in_ref[z, pl.ds(ZB - 1, 1), :].astype(I32)
    head_out_ref[...] = head_vmem[...]
    pltpu.sync_copy(head_vmem, head)

    def step(r, over):
        to = jnp.int32(0)
        for z in range(NZ):
            start = head[z, r]
            at = jnp.minimum(start, ZCAP)
            pbuf[pl.ds(r * PBUF + to, SLOTS), :] = zbuf[pl.ds(z * ZBUF + at, SLOTS), :]
            end = head[z, r + 1]
            to = jnp.minimum(to + end - start, PCAP + 1)
            over = jnp.maximum(over, jnp.where(end > ZCAP, 1, 0))
        return jnp.maximum(over, jnp.where(to > PCAP, 1, 0))

    over = lax.fori_loop(0, PLANE, step, jnp.int32(0))
    mark = jnp.full((1, 128), over, I32).astype(F32)
    left = lanes64((PB, 128))
    for r in range(PLANE):
        out_ref[r] = jnp.where(left, pbuf[pl.ds(r * PBUF, PB), :], pbuf[pl.ds(r * PBUF + PB - 1, PB), :])
        out_ref[r, pl.ds(PB - 1, 1), :] = mark


def back_kernel(head, in_ref, out_ref, zbuf, pbuf):
    mark = jnp.zeros((1, 128), F32)
    for r in range(PLANE):
        left, right = both(in_ref[r])
        pbuf[pl.ds(r * PBUF, PB), :] = left
        pbuf[pl.ds(r * PBUF + PB - 1, PB), :] = right
        mark = jnp.maximum(mark, in_ref[r, pl.ds(PB - 1, 1), :])

    def step(r, carry):
        at = jnp.int32(0)
        for z in range(NZ):
            start = head[z, r]
            to = jnp.minimum(start, ZCAP)
            zbuf[pl.ds(z * ZBUF + to, SLOTS), :] = pbuf[pl.ds(r * PBUF + at, SLOTS), :]
            at = jnp.minimum(at + head[z, r + 1] - start, PCAP + 1)
        return carry

    lax.fori_loop(0, PLANE, step, 0)
    left = lanes64((ZB, 128))
    for z in range(NZ):
        out_ref[z] = jnp.where(left, zbuf[pl.ds(z * ZBUF, ZB), :], zbuf[pl.ds(z * ZBUF + ZB - 1, ZB), :])
        out_ref[z, pl.ds(ZB - 1, 1), :] = mark


def gene_kernel(
    addr, again, gene, in_ref, dose_ref, weight_ref, out_ref, one_ref, two_ref, held, total, weighted, work
):
    mark = jnp.zeros((1, 128), F32)
    for m in range(PLANE):
        left, right = both(in_ref[m])
        held[pl.ds(m * 2 * PB, PB), :] = left
        held[pl.ds(m * 2 * PB + PB, PB), :] = right
        mark = jnp.maximum(mark, in_ref[m, pl.ds(PB - 1, 1), :])
    held[pl.ds(HOLD, 8), :] = jnp.zeros((8, 128), F32)
    total[...] = jnp.zeros_like(total)
    two_ref[...] = jnp.zeros_like(two_ref)

    def gather(t, carry):
        for c in range(TILE):
            work[pl.ds(c, 1), :] = held[pl.ds(addr[t, c], 1), :]
        total[gene[t]] += dot(dose_ref[t], split(work[...]))
        return carry

    lax.fori_loop(0, TILES, gather, 0)
    for k in range(GENES):
        weight = weight_ref[:, pl.ds(k, 1)]
        scores = fold(total[k]) * weight
        one_ref[pl.ds(k, 1), :] = jnp.sum(scores * scores, axis=0, keepdims=True) * (1.0 / VT)
        weighted[k] = split(scores * weight)

    def returned(t):
        rows = fold(dot(dose_ref[t], weighted[gene[t]], 0, 0))
        two_ref[pl.ds(gene[t], 1), :] += jnp.sum(rows * rows, axis=0, keepdims=True) * (1.0 / TILE)
        work[...] = rows

    @pl.when(again[0, 0] == 0)
    def _():
        def scatter(t, carry):
            returned(t)
            for c in range(TILE):
                held[pl.ds(addr[t, c], 1), :] = work[pl.ds(c, 1), :]
            return carry

        lax.fori_loop(0, TILES, scatter, 0)

    @pl.when(again[0, 0] != 0)
    def _():
        held[...] = jnp.zeros_like(held)

        def scatter(t, carry):
            returned(t)

            def add(c, inner):
                held[pl.ds(addr[t, c], 1), :] += work[pl.ds(c, 1), :]
                return inner

            lax.fori_loop(0, TILE, add, 0)
            return carry

        lax.fori_loop(0, TILES, scatter, 0)

    left = lanes64((PB, 128))
    for m in range(PLANE):
        out_ref[m] = jnp.where(left, held[pl.ds(m * 2 * PB, PB), :], held[pl.ds(m * 2 * PB + PB, PB), :])
        out_ref[m, pl.ds(PB - 1, 1), :] = mark


def sum_kernel(in_ref, index_ref, out_ref, mark_ref, total):
    total[...] = jnp.zeros_like(total)
    lane = iota((2 * ZB, 128), 1)

    def step(z, mark):
        left, right = both(in_ref[z])
        index = index_ref[z]
        rows = jnp.where(index > 0.5, jnp.concatenate([left, right], axis=0), 0.0)
        total[...] += dot(split(rows), choose(index, lane), 0, 0)
        return jnp.maximum(mark, in_ref[z, pl.ds(ZB - 1, 1), :])

    mark_ref[...] = lax.fori_loop(0, NZ, step, jnp.zeros((1, 128), F32))
    out_ref[...] = total[pl.ds(0, PROBES), :] + total[pl.ds(PROBES, PROBES), :]


VMEM = pl.BlockSpec(memory_space=pltpu.VMEM)
SMEM = pl.BlockSpec(memory_space=pltpu.SMEM)


def call(kernel, outs, ins, scratch=(), out_specs=None, cost=2_000_000):
    shapes = [jax.ShapeDtypeStruct(*o) for o in outs]
    return pl.pallas_call(
        kernel,
        out_shape=shapes,
        in_specs=ins,
        out_specs=[VMEM] * len(shapes) if out_specs is None else out_specs,
        scratch_shapes=list(scratch),
        cost_estimate=pl.CostEstimate(flops=cost * 100, bytes_accessed=cost, transcendentals=0),
    )


def packed(probes, dosages, weights, send_rows, tile_src, tile_gene):
    (count,) = call(used_kernel, [((128, 128), F32)], [VMEM])(tile_src)
    asked = jnp.minimum(count, 1.0).reshape(DEV * LANE)
    asked = lax.all_to_all(asked, ALL, 0, 0, tiled=True).reshape(128, 128)
    addr, again = call(
        place_kernel, [((TILES, TILE), I32), ((1, 1), I32)], [VMEM, VMEM], out_specs=[VMEM, SMEM]
    )(tile_src, count)
    rows = jnp.pad(send_rows[0], ((0, 0), (0, LANE - SLOTS))).reshape(128, 128)
    block, index = call(
        send_kernel,
        [((NZ, ZB, 128), F32), ((NZ, 2 * ZB, 128), F32)],
        [VMEM] * 3,
        [pltpu.VMEM((128, 128), I32), pltpu.VMEM((NZ, 128), F32), pltpu.VMEM((128, 128), F32)],
    )(asked, rows, probes)
    block = lax.all_to_all(block, "z", 0, 0, tiled=True)
    buffers = [pltpu.VMEM((NZ * ZBUF, 128), F32), pltpu.VMEM((PLANE * PBUF, 128), F32)]
    block, head = call(
        relay_kernel,
        [((PLANE, PB, 128), F32), ((NZ, 128), I32)],
        [VMEM],
        buffers + [pltpu.VMEM((NZ, 128), I32), pltpu.SMEM((NZ, 128), I32)],
    )(block)
    block = lax.all_to_all(block, FLAT, 0, 0, tiled=True)
    block, one, two = call(
        gene_kernel,
        [((PLANE, PB, 128), F32), ((GENES, 128), F32), ((GENES, 128), F32)],
        [SMEM] * 3 + [VMEM] * 3,
        [
            pltpu.VMEM((HOLD + 8, 128), F32),
            pltpu.VMEM((GENES, VT, 128), F32),
            pltpu.VMEM((GENES, VT, 128), BF16),
            pltpu.VMEM((TILE, 128), F32),
        ],
    )(addr, again, tile_gene, block, dosages, weights.T)
    block = lax.all_to_all(block, FLAT, 0, 0, tiled=True)
    (block,) = call(back_kernel, [((NZ, ZB, 128), F32)], [SMEM, VMEM], buffers)(head, block)
    block = lax.all_to_all(block, "z", 0, 0, tiled=True)
    projected, mark = call(
        sum_kernel,
        [((PROBES, ROWS), F32), ((1, 128), F32)],
        [VMEM] * 2,
        [pltpu.VMEM((2 * PROBES, ROWS), F32)],
    )(block, index)
    moments = jnp.stack([one[:, :PROBES], two[:, :PROBES]]).transpose(0, 2, 1)
    return projected, moments, mark[0, 0]


def exchange(rows):
    return lax.all_to_all(rows, ALL, 0, 0, tiled=True)


def whole(probes, dosages, weights, send_rows, tile_src, tile_gene):
    rows_sent = send_rows[0]
    high = lax.Precision.HIGHEST
    outgoing = probes.T[rows_sent].reshape(DEV, SLOTS * PROBES // 128, 128)
    incoming = exchange(outgoing).reshape(SRC, PROBES)
    fetched = jnp.concatenate([incoming, jnp.zeros((1, PROBES), F32)], axis=0)
    slab = fetched[tile_src]
    tile_scores = jnp.einsum("tcb,tvc->tbv", slab, dosages, precision=high, preferred_element_type=F32)
    member = (tile_gene[None, :] == jnp.arange(GENES, dtype=I32)[:, None]).astype(F32)
    scores = jnp.einsum("gt,tbv->gbv", member, tile_scores, precision=high) * weights[:, None, :]
    one = jnp.sum(scores * scores, axis=2) / VT
    weighted = jnp.einsum("gt,gbv->tbv", member, scores * weights[:, None, :], precision=high)
    returned = jnp.einsum("tbv,tvc->tcb", weighted, dosages, precision=high, preferred_element_type=F32)
    two = jnp.dot(member, jnp.sum(returned * returned, axis=1), precision=high) / TILE
    sums = jax.ops.segment_sum(returned.reshape(-1, PROBES), tile_src.reshape(-1), num_segments=SRC + 1)
    arrived = exchange(sums[:SRC].reshape(DEV, SLOTS * PROBES // 128, 128))
    projected = jax.ops.segment_sum(
        arrived.reshape(SRC, PROBES), rows_sent.reshape(-1), num_segments=ROWS
    ).T
    return projected, jnp.stack([one, two]).transpose(0, 2, 1)


def shards(*args):
    projected, moments, mark = packed(*args)
    return lax.cond(mark > 0.5, lambda: whole(*args), lambda: (projected, moments))


def solution(mesh):
    fine = Mesh(mesh.devices.reshape(NY, NZ, NC, NX), ALL)
    placed = (P(None, ALL), P(ALL, None, None), P(ALL, None), P(ALL, None, None), P(ALL, None), P(ALL))
    return jax.shard_map(
        shards,
        mesh=fine,
        in_specs=placed,
        out_specs=(P(None, ALL), P(None, None, ALL)),
        check_vma=False,
    )
```

```python
import jax
import jax.numpy as jnp
from jax import lax
from jax.experimental import pallas as pl
from jax.experimental.pallas import tpu as pltpu
from jax.sharding import Mesh, PartitionSpec as P

NY, NZ, NC, NX = 4, 16, 2, 4
PLANE = NY * NC * NX
DEV = NY * NZ * NC * NX
SLOTS = 24
LANE = 32
SRC = DEV * SLOTS
TILES = 40
TILE = 128
VT = 128
GENES = 20
PROBES = 64
ROWS = 1024
ZB = 128
ZCAP = 2 * (ZB - 1)
PB = 96
PCAP = 2 * (PB - 1)
ZBUF = 280
PBUF = 216
HOLD = PLANE * 2 * PB
F32 = jnp.float32
BF16 = jnp.bfloat16
I32 = jnp.int32
ALL = ("y", "z", "c", "x")
FLAT = ("y", "c", "x")


def iota(shape, dim):
    return lax.broadcasted_iota(I32, shape, dim)


def dot(a, b, ca=1, cb=0, **kw):
    return lax.dot_general(a, b, (((ca,), (cb,)), ((), ())), preferred_element_type=F32, **kw)


def ones_where(mask):
    return jnp.where(mask, 1.0, 0.0).astype(BF16)


def lanes64(shape):
    return iota(shape, 1) < PROBES


def fold(v):
    return v + pltpu.roll(v, PROBES, 1)


def split(v):
    high = v.astype(BF16).astype(F32)
    return jnp.where(lanes64(v.shape), high, v - high).astype(BF16)


def both(block):
    turned = pltpu.roll(block, PROBES, 1)
    left = lanes64(block.shape)
    return jnp.where(left, block, turned), jnp.where(left, turned, block)


def source_parts(ref, t, n):
    highs, lows, empties = [], [], []
    for i in range(n):
        p = ref[pl.ds(t * n + i, 1), :]
        o = (p * 43691) >> 20
        highs.append(((o >> 7) * (NC * NX) + (o & 7)) * 4 + ((o >> 5) & 3))
        lows.append(((o >> 3) & 3) * LANE + p - o * SLOTS)
        empties.append(p >= SRC)
    return highs, lows, empties


def one_hots(rows):
    return jnp.concatenate([ones_where(iota((128, 128), 0) == r) for r in rows], axis=1)


def used_kernel(src_ref, used_ref, count_ref):
    count_ref[...] = jnp.zeros_like(count_ref)

    def step(t, carry):
        highs, lows, _ = source_parts(src_ref, t, 8)
        count_ref[...] += dot(one_hots(highs), one_hots(lows), 1, 1)
        return carry

    lax.fori_loop(0, TILES // 8, step, 0)
    used_ref[...] = jnp.minimum(count_ref[...], 1.0)


def place_kernel(src_ref, count_ref, addr_ref, again_ref):
    count = count_ref[...]
    again_ref[0, 0] = jnp.where(jnp.max(count) > 1.5, 1, 0)
    used = ones_where(count > 0.5)
    row, col = iota((128, 128), 0), iota((128, 128), 1)
    before = dot(used, ones_where(row < col))
    number = dot(used, jnp.ones((128, 128), BF16)).astype(BF16)
    earlier = ones_where(((row >> 2) == (col >> 2)) & (col < row))
    rank = jnp.minimum((dot(earlier, number) + before).astype(I32), PCAP)
    place = (row >> 2) * (2 * PB) + rank + jnp.where(rank >= PB - 1, 1, 0)
    turned = jnp.transpose(place)
    high = turned >> 6
    table = jnp.concatenate([high, turned - (high << 6)], axis=0).astype(F32).astype(BF16)

    def step(t, carry):
        highs, lows, empties = source_parts(src_ref, t, 8)
        found = dot(table, one_hots(highs))
        for i in range(8):
            part = found[:, i * 128 : (i + 1) * 128]
            value = part[:128] * 64.0 + part[128:]
            value = jnp.sum(jnp.where(row == lows[i], value, 0.0), axis=0, keepdims=True)
            addr_ref[pl.ds(t * 8 + i, 1), :] = jnp.where(empties[i], HOLD, value.astype(I32))
        return carry

    lax.fori_loop(0, TILES // 8, step, 0)


def meet_kernel(in_ref, out_ref):
    block = iota((8, 128), 1) >> 5
    for high in range(4):
        parts = [in_ref[pl.ds(x * 4 + high, 8, stride=16), :] for x in range(NX)]
        for low in range(4):
            turned = [pltpu.roll(parts[x], ((x - low) * LANE) % 128, 1) for x in range(NX)]
            result = turned[0]
            for x in range(1, NX):
                result = jnp.where(block == x, turned[x], result)
            out_ref[high * 4 + low] = result


def table_kernel(in_ref, table_ref, mark_ref):
    used = ones_where(in_ref[...] > 0.5)
    row, col = iota((128, 128), 0), iota((128, 128), 1)
    segment = dot(used, ones_where((row >> 5) == (col >> 5)))
    whole_row = dot(used, jnp.ones((128, 128), BF16))
    before = dot(used, ones_where((row >> 5) < (col >> 5)))
    owner = dot(ones_where(((row & 3) == (col & 3)) & (col < row)), segment.astype(BF16))
    holder = before + dot(ones_where(((row >> 2) == (col >> 2)) & (col < row)), whole_row.astype(BF16))
    over = jnp.maximum(
        jnp.where(owner + segment > ZCAP, 1.0, 0.0), jnp.where(holder + segment > PCAP, 1.0, 0.0)
    )
    mark_ref[...] = jnp.broadcast_to(jnp.max(over), (1, 128))
    owner, holder = jnp.minimum(owner, float(ZCAP)), jnp.minimum(holder, float(PCAP + 1))
    table_ref[...] = jnp.where((col & 1) == 0, owner, holder).astype(I32)


def rows_kernel(rows_ref, probes_ref, out_ref, turned_ref, parts_ref):
    turned_ref[...] = jnp.transpose(rows_ref[...])
    high = probes_ref[...].astype(BF16).astype(F32)
    parts = jnp.concatenate([high, probes_ref[...] - high], axis=0)
    parts_ref[...] = jnp.transpose(parts).astype(BF16)
    lane = iota((128, 128), 1)

    def step(i, carry):
        for n in range(4):
            which = pltpu.roll(turned_ref[...], lax.rem(128 - (i * 4 + n), 128), 1)[:, :1]
            which = jnp.broadcast_to(which, (128, 128))
            picks = [ones_where(which == lane + 128 * k) for k in range(ROWS // 128)]
            out_ref[i * 4 + n] = dot(jnp.concatenate(picks, axis=1), parts_ref[...]).astype(BF16)
        return carry

    lax.fori_loop(0, 32, step, 0)


def send_kernel(used_ref, rows_ref, parts_ref, out_ref, index_ref, place_ref, digit_ref):
    used = used_ref[...]
    flag = ones_where(used > 0.5)
    row, col = iota((128, 128), 0), iota((128, 128), 1)
    number = dot(flag, jnp.ones((128, 128), BF16))
    start = dot(ones_where(((row >> 3) == (col >> 3)) & (col < row)), number.astype(BF16))
    place = start + dot(flag, ones_where(row < col))
    place_ref[...] = jnp.where(used > 0.5, place.astype(I32), -1)
    value = rows_ref[...] + 1
    digit_ref[0] = (value >> 5).astype(F32)
    digit_ref[1] = (value & 31).astype(F32)
    at = iota((2 * ZB, 128), 0)
    at = jnp.where((at & (ZB - 1)) == ZB - 1, -2, jnp.where(at < ZB, at, at - 1))
    first = iota((8, 128), 0) == 0

    def step(z, carry):
        picks, parts, digits = [], [], []
        for y in range(NY):
            for c in range(NC):
                i = y * (NZ * NC) + z * NC + c
                picks.append(ones_where(at == place_ref[pl.ds(z * (NY * NC) + y * NC + c, 1), :]))
                parts.append(parts_ref[i])
                digits.append(jnp.where(first, digit_ref[0, pl.ds(i, 1), :], digit_ref[1, pl.ds(i, 1), :]))
        picks = jnp.concatenate(picks, axis=1)
        rows = fold(dot(picks, jnp.concatenate(parts, axis=0)))
        out_ref[z] = jnp.where(lanes64((ZB, 128)), rows[:ZB], rows[ZB:])
        index = dot(jnp.concatenate(digits, axis=1).astype(BF16), picks, 1, 1)
        index_ref[pl.ds(z, 1), :] = index[:1] * 32.0 + index[1:2]
        return carry

    lax.fori_loop(0, NZ, step, 0)


def relay_kernel(table, mark_ref, in_ref, out_ref, zbuf, pbuf):
    for z in range(NZ):
        left, right = both(in_ref[z])
        zbuf[pl.ds(z * ZBUF, ZB), :] = left
        zbuf[pl.ds(z * ZBUF + ZB - 1, ZB), :] = right

    def step(r, carry):
        for z in range(NZ):
            row, col = r * 4 + z // 4, (z % 4) * LANE
            pbuf[pl.ds(r * PBUF + table[row, col + 1], SLOTS), :] = zbuf[
                pl.ds(z * ZBUF + table[row, col], SLOTS), :
            ]
        return carry

    lax.fori_loop(0, PLANE, step, 0)
    left = lanes64((PB, 128))
    for r in range(PLANE):
        out_ref[r] = jnp.where(left, pbuf[pl.ds(r * PBUF, PB), :], pbuf[pl.ds(r * PBUF + PB - 1, PB), :])
        out_ref[r, pl.ds(PB - 1, 1), :] = mark_ref[...]


def back_kernel(table, in_ref, out_ref, zbuf, pbuf):
    mark = jnp.zeros((1, 128), F32)
    for r in range(PLANE):
        left, right = both(in_ref[r])
        pbuf[pl.ds(r * PBUF, PB), :] = left
        pbuf[pl.ds(r * PBUF + PB - 1, PB), :] = right
        mark = jnp.maximum(mark, in_ref[r, pl.ds(PB - 1, 1), :])

    def step(r, carry):
        for z in range(NZ):
            row, col = r * 4 + z // 4, (z % 4) * LANE
            zbuf[pl.ds(z * ZBUF + table[row, col], SLOTS), :] = pbuf[
                pl.ds(r * PBUF + table[row, col + 1], SLOTS), :
            ]
        return carry

    lax.fori_loop(0, PLANE, step, 0)
    left = lanes64((ZB, 128))
    for z in range(NZ):
        out_ref[z] = jnp.where(left, zbuf[pl.ds(z * ZBUF, ZB), :], zbuf[pl.ds(z * ZBUF + ZB - 1, ZB), :])
        out_ref[z, pl.ds(ZB - 1, 1), :] = mark


def gene_kernel(
    addr, again, gene, in_ref, dose_ref, weight_ref, out_ref, one_ref, two_ref, held, total, weighted, work
):
    mark = jnp.zeros((1, 128), F32)
    for m in range(PLANE):
        left, right = both(in_ref[m])
        held[pl.ds(m * 2 * PB, PB), :] = left
        held[pl.ds(m * 2 * PB + PB, PB), :] = right
        mark = jnp.maximum(mark, in_ref[m, pl.ds(PB - 1, 1), :])
    held[pl.ds(HOLD, 8), :] = jnp.zeros((8, 128), F32)
    total[...] = jnp.zeros_like(total)
    two_ref[...] = jnp.zeros_like(two_ref)

    def gather(t, carry):
        for c in range(TILE):
            work[pl.ds(c, 1), :] = held[pl.ds(addr[t, c], 1), :]
        total[gene[t]] += dot(dose_ref[t], split(work[...]))
        return carry

    lax.fori_loop(0, TILES, gather, 0)
    for k in range(GENES):
        weight = weight_ref[:, pl.ds(k, 1)]
        scores = fold(total[k]) * weight
        one_ref[pl.ds(k, 1), :] = jnp.sum(scores * scores, axis=0, keepdims=True) * (1.0 / VT)
        weighted[k] = split(scores * weight)

    def returned(t):
        rows = fold(dot(dose_ref[t], weighted[gene[t]], 0, 0))
        two_ref[pl.ds(gene[t], 1), :] += jnp.sum(rows * rows, axis=0, keepdims=True) * (1.0 / TILE)
        work[...] = rows

    @pl.when(again[0, 0] == 0)
    def _():
        def scatter(t, carry):
            returned(t)
            for c in range(TILE):
                held[pl.ds(addr[t, c], 1), :] = work[pl.ds(c, 1), :]
            return carry

        lax.fori_loop(0, TILES, scatter, 0)

    @pl.when(again[0, 0] != 0)
    def _():
        held[...] = jnp.zeros_like(held)

        def scatter(t, carry):
            returned(t)

            def add(c, inner):
                held[pl.ds(addr[t, c], 1), :] += work[pl.ds(c, 1), :]
                return inner

            lax.fori_loop(0, TILE, add, 0)
            return carry

        lax.fori_loop(0, TILES, scatter, 0)

    left = lanes64((PB, 128))
    for m in range(PLANE):
        out_ref[m] = jnp.where(left, held[pl.ds(m * 2 * PB, PB), :], held[pl.ds(m * 2 * PB + PB, PB), :])
        out_ref[m, pl.ds(PB - 1, 1), :] = mark


def sum_kernel(in_ref, index_ref, out_ref, mark_ref, total):
    total[...] = jnp.zeros_like(total)
    at = (iota((ROWS, 2 * ZB), 0) + 1).astype(F32)

    def step(z, mark):
        block = in_ref[z]
        index = index_ref[pl.ds(z, 1), :]
        turned = jnp.transpose(block)
        rows = jnp.concatenate([turned[:PROBES], turned[PROBES:]], axis=1)
        rows = jnp.where(index > 0.5, rows, 0.0)
        high = rows.astype(BF16).astype(F32)
        parts = jnp.concatenate([high, rows - high], axis=0).astype(BF16)
        total[...] += dot(parts, ones_where(at == index), 1, 1)
        return jnp.maximum(mark, in_ref[z, pl.ds(ZB - 1, 1), :])

    mark_ref[...] = lax.fori_loop(0, NZ, step, jnp.zeros((1, 128), F32))
    out_ref[...] = total[pl.ds(0, PROBES), :] + total[pl.ds(PROBES, PROBES), :]


VMEM = pl.BlockSpec(memory_space=pltpu.VMEM)
SMEM = pl.BlockSpec(memory_space=pltpu.SMEM)


def call(kernel, outs, ins, scratch=(), out_specs=None, cost=2_000_000, limit=24):
    shapes = [jax.ShapeDtypeStruct(*o) for o in outs]
    return pl.pallas_call(
        kernel,
        out_shape=shapes,
        in_specs=ins,
        out_specs=[VMEM] * len(shapes) if out_specs is None else out_specs,
        scratch_shapes=list(scratch),
        cost_estimate=pl.CostEstimate(flops=cost * 100, bytes_accessed=cost, transcendentals=0),
        compiler_params=pltpu.CompilerParams(vmem_limit_bytes=limit << 20),
    )


def packed(probes, dosages, weights, send_rows, tile_src, tile_gene):
    used, count = call(used_kernel, [((128, 128), F32)] * 2, [VMEM])(tile_src)
    asked = lax.all_to_all(used.reshape(PLANE, 4, 128), FLAT, 0, 0, tiled=True).reshape(128, 128)
    (met,) = call(meet_kernel, [((NZ, 8, 128), F32)], [VMEM])(asked)
    met = lax.all_to_all(met, "z", 0, 0, tiled=True).reshape(128, 128)
    table, mark = call(table_kernel, [((128, 128), I32), ((1, 128), F32)], [VMEM])(asked)
    addr, again = call(
        place_kernel, [((TILES, TILE), I32), ((1, 1), I32)], [VMEM, VMEM], out_specs=[VMEM, SMEM]
    )(tile_src, count)
    rows = jnp.pad(send_rows[0], ((0, 0), (0, LANE - SLOTS))).reshape(128, 128)
    (parts,) = call(
        rows_kernel,
        [((128, 128, 128), BF16)],
        [VMEM] * 2,
        [pltpu.VMEM((128, 128), I32), pltpu.VMEM((ROWS, 128), BF16)],
    )(rows, probes)
    block, index = call(
        send_kernel,
        [((NZ, ZB, 128), F32), ((NZ, 2 * ZB), F32)],
        [VMEM] * 3,
        [pltpu.VMEM((128, 128), I32), pltpu.VMEM((2, 128, 128), F32)],
    )(met, rows, parts)
    block = lax.all_to_all(block, "z", 0, 0, tiled=True)
    buffers = [pltpu.VMEM((NZ * ZBUF, 128), F32), pltpu.VMEM((PLANE * PBUF, 128), F32)]
    (block,) = call(relay_kernel, [((PLANE, PB, 128), F32)], [SMEM, VMEM, VMEM], buffers)(table, mark, block)
    block = lax.all_to_all(block, FLAT, 0, 0, tiled=True)
    block, one, two = call(
        gene_kernel,
        [((PLANE, PB, 128), F32), ((GENES, 128), F32), ((GENES, 128), F32)],
        [SMEM] * 3 + [VMEM] * 3,
        [
            pltpu.VMEM((HOLD + 8, 128), F32),
            pltpu.VMEM((GENES, VT, 128), F32),
            pltpu.VMEM((GENES, VT, 128), BF16),
            pltpu.VMEM((TILE, 128), F32),
        ],
    )(addr, again, tile_gene, block, dosages, weights.T)
    block = lax.all_to_all(block, FLAT, 0, 0, tiled=True)
    (block,) = call(back_kernel, [((NZ, ZB, 128), F32)], [SMEM, VMEM], buffers)(table, block)
    block = lax.all_to_all(block, "z", 0, 0, tiled=True)
    projected, mark = call(
        sum_kernel,
        [((PROBES, ROWS), F32), ((1, 128), F32)],
        [VMEM] * 2,
        [pltpu.VMEM((2 * PROBES, ROWS), F32)],
    )(block, index)
    moments = jnp.stack([one[:, :PROBES], two[:, :PROBES]]).transpose(0, 2, 1)
    return projected, moments, mark[0, 0]


def exchange(rows):
    return lax.all_to_all(rows, ALL, 0, 0, tiled=True)


def whole(probes, dosages, weights, send_rows, tile_src, tile_gene):
    rows_sent = send_rows[0]
    high = lax.Precision.HIGHEST
    outgoing = probes.T[rows_sent].reshape(DEV, SLOTS * PROBES // 128, 128)
    incoming = exchange(outgoing).reshape(SRC, PROBES)
    fetched = jnp.concatenate([incoming, jnp.zeros((1, PROBES), F32)], axis=0)
    slab = fetched[tile_src]
    tile_scores = jnp.einsum("tcb,tvc->tbv", slab, dosages, precision=high, preferred_element_type=F32)
    member = (tile_gene[None, :] == jnp.arange(GENES, dtype=I32)[:, None]).astype(F32)
    scores = jnp.einsum("gt,tbv->gbv", member, tile_scores, precision=high) * weights[:, None, :]
    one = jnp.sum(scores * scores, axis=2) / VT
    weighted = jnp.einsum("gt,gbv->tbv", member, scores * weights[:, None, :], precision=high)
    returned = jnp.einsum("tbv,tvc->tcb", weighted, dosages, precision=high, preferred_element_type=F32)
    two = jnp.dot(member, jnp.sum(returned * returned, axis=1), precision=high) / TILE
    sums = jax.ops.segment_sum(returned.reshape(-1, PROBES), tile_src.reshape(-1), num_segments=SRC + 1)
    arrived = exchange(sums[:SRC].reshape(DEV, SLOTS * PROBES // 128, 128))
    projected = jax.ops.segment_sum(
        arrived.reshape(SRC, PROBES), rows_sent.reshape(-1), num_segments=ROWS
    ).T
    return projected, jnp.stack([one, two]).transpose(0, 2, 1)


def shards(*args):
    projected, moments, mark = packed(*args)
    return lax.cond(mark > 0.5, lambda: whole(*args), lambda: (projected, moments))


def solution(mesh):
    fine = Mesh(mesh.devices.reshape(NY, NZ, NC, NX), ALL)
    placed = (P(None, ALL), P(ALL, None, None), P(ALL, None), P(ALL, None, None), P(ALL, None), P(ALL))
    return jax.shard_map(
        shards,
        mesh=fine,
        in_specs=placed,
        out_specs=(P(None, ALL), P(None, None, ALL)),
        check_vma=False,
    )
```

```python
import jax
import jax.numpy as jnp
from jax import lax
from jax.experimental import pallas as pl
from jax.experimental.pallas import tpu as pltpu
from jax.sharding import Mesh, PartitionSpec as P

NY, NZ, NC, NX = 4, 16, 2, 4
PLANE = NY * NC * NX
DEV = NY * NZ * NC * NX
SLOTS = 24
LANE = 32
SRC = DEV * SLOTS
TILES = 40
TILE = 128
VT = 128
GENES = 20
PROBES = 64
ROWS = 1024
ZB = 128
ZCAP = 2 * (ZB - 1)
PB = 96
PCAP = 2 * (PB - 1)
ZBUF = 280
PBUF = 216
HOLD = PLANE * 2 * PB
F32 = jnp.float32
BF16 = jnp.bfloat16
I32 = jnp.int32
ALL = ("y", "z", "c", "x")
FLAT = ("y", "c", "x")


def iota(shape, dim):
    return lax.broadcasted_iota(I32, shape, dim)


def dot(a, b, ca=1, cb=0, **kw):
    return lax.dot_general(a, b, (((ca,), (cb,)), ((), ())), preferred_element_type=F32, **kw)


def ones_where(mask):
    return jnp.where(mask, 1.0, 0.0).astype(BF16)


def lanes64(shape):
    return iota(shape, 1) < PROBES


def fold(v):
    return v + pltpu.roll(v, PROBES, 1)


def split(v):
    high = v.astype(BF16).astype(F32)
    return jnp.where(lanes64(v.shape), high, v - high).astype(BF16)


def both(block):
    turned = pltpu.roll(block, PROBES, 1)
    left = lanes64(block.shape)
    return jnp.where(left, block, turned), jnp.where(left, turned, block)


def source_parts(ref, t, n):
    highs, lows, empties = [], [], []
    for i in range(n):
        p = ref[pl.ds(t * n + i, 1), :]
        o = (p * 43691) >> 20
        highs.append(((o >> 7) * (NC * NX) + (o & 7)) * 4 + ((o >> 5) & 3))
        lows.append(((o >> 3) & 3) * LANE + p - o * SLOTS)
        empties.append(p >= SRC)
    return highs, lows, empties


def one_hots(rows):
    return jnp.concatenate([ones_where(iota((128, 128), 0) == r) for r in rows], axis=1)


def used_kernel(src_ref, used_ref, count_ref):
    count_ref[...] = jnp.zeros_like(count_ref)

    def step(t, carry):
        highs, lows, _ = source_parts(src_ref, t, 8)
        count_ref[...] += dot(one_hots(highs), one_hots(lows), 1, 1)
        return carry

    lax.fori_loop(0, TILES // 8, step, 0)
    used_ref[...] = jnp.minimum(count_ref[...], 1.0)


def place_kernel(src_ref, count_ref, addr_ref, again_ref):
    count = count_ref[...]
    again_ref[0, 0] = jnp.where(jnp.max(count) > 1.5, 1, 0)
    used = ones_where(count > 0.5)
    row, col = iota((128, 128), 0), iota((128, 128), 1)
    before = dot(used, ones_where(row < col))
    number = dot(used, jnp.ones((128, 128), BF16)).astype(BF16)
    earlier = ones_where(((row >> 2) == (col >> 2)) & (col < row))
    rank = jnp.minimum((dot(earlier, number) + before).astype(I32), PCAP)
    place = (row >> 2) * (2 * PB) + rank + jnp.where(rank >= PB - 1, 1, 0)
    turned = jnp.transpose(place)
    high = turned >> 6
    table = jnp.concatenate([high, turned - (high << 6)], axis=0).astype(F32).astype(BF16)

    def step(t, carry):
        highs, lows, empties = source_parts(src_ref, t, 8)
        found = dot(table, one_hots(highs))
        for i in range(8):
            part = found[:, i * 128 : (i + 1) * 128]
            value = part[:128] * 64.0 + part[128:]
            value = jnp.sum(jnp.where(row == lows[i], value, 0.0), axis=0, keepdims=True)
            addr_ref[pl.ds(t * 8 + i, 1), :] = jnp.where(empties[i], HOLD, value.astype(I32))
        return carry

    lax.fori_loop(0, TILES // 8, step, 0)


def meet_kernel(in_ref, out_ref):
    block = iota((8, 128), 1) >> 5
    for high in range(4):
        parts = [in_ref[pl.ds(x * 4 + high, 8, stride=16), :] for x in range(NX)]
        for low in range(4):
            turned = [pltpu.roll(parts[x], ((x - low) * LANE) % 128, 1) for x in range(NX)]
            result = turned[0]
            for x in range(1, NX):
                result = jnp.where(block == x, turned[x], result)
            out_ref[high * 4 + low] = result


def table_kernel(in_ref, table_ref, mark_ref):
    used = ones_where(in_ref[...] > 0.5)
    row, col = iota((128, 128), 0), iota((128, 128), 1)
    segment = dot(used, ones_where((row >> 5) == (col >> 5)))
    whole_row = dot(used, jnp.ones((128, 128), BF16))
    before = dot(used, ones_where((row >> 5) < (col >> 5)))
    owner = dot(ones_where(((row & 3) == (col & 3)) & (col < row)), segment.astype(BF16))
    holder = before + dot(ones_where(((row >> 2) == (col >> 2)) & (col < row)), whole_row.astype(BF16))
    over = jnp.maximum(
        jnp.where(owner + segment > ZCAP, 1.0, 0.0), jnp.where(holder + segment > PCAP, 1.0, 0.0)
    )
    mark_ref[...] = jnp.broadcast_to(jnp.max(over), (1, 128))
    owner, holder = jnp.minimum(owner, float(ZCAP)), jnp.minimum(holder, float(PCAP + 1))
    table_ref[...] = jnp.where((col & 1) == 0, owner, holder).astype(I32)


def send_kernel(used_ref, rows_ref, probes_ref, out_ref, index_ref, high_ref, low_ref, parts_ref):
    used = used_ref[...]
    flag = ones_where(used > 0.5)
    row, col = iota((128, 128), 0), iota((128, 128), 1)
    number = dot(flag, jnp.ones((128, 128), BF16))
    start = dot(ones_where(((row >> 3) == (col >> 3)) & (col < row)), number.astype(BF16))
    place = (start + dot(flag, ones_where(row < col))).astype(I32)
    place = place + jnp.where(place >= ZB - 1, 1, 0)
    high_ref[...] = jnp.where(used > 0.5, place >> 7, -1)
    low_ref[...] = place & (ZB - 1)
    high = probes_ref[...].astype(BF16).astype(F32)
    parts_ref[...] = jnp.concatenate([high, probes_ref[...] - high], axis=0).astype(BF16)
    which = iota((8, 128), 0)
    at = iota((ZB, 128), 0)
    subject = (iota((ROWS, 2 * ZB), 0) + 1).astype(F32)

    def step(z, carry):
        values, places = [], []
        for y in range(NY):
            for c in range(NC):
                i = z * (NY * NC) + y * NC + c
                value = rows_ref[pl.ds(y * (NZ * NC) + z * NC + c, 1), :] + 1
                digit = jnp.where(which < 2, value >> 5, value & 31)
                match = ((which & 1) == high_ref[pl.ds(i, 1), :]) & (which < 4)
                values.append(jnp.where(match, digit, 0).astype(F32).astype(BF16))
                places.append(ones_where(at == low_ref[pl.ds(i, 1), :]))
        listed = dot(jnp.concatenate(values, axis=1), jnp.concatenate(places, axis=1), 1, 1)
        index = listed[:2] * 32.0 + listed[2:4]
        index = jnp.concatenate([index[:1], index[1:]], axis=1)
        index_ref[pl.ds(z, 1), :] = index
        rows = dot(parts_ref[...], ones_where(subject == index))
        rows = rows[:PROBES] + rows[PROBES:]
        out_ref[z] = jnp.transpose(jnp.concatenate([rows[:, :ZB], rows[:, ZB:]], axis=0))
        return carry

    lax.fori_loop(0, NZ, step, 0)


def relay_kernel(table, mark_ref, in_ref, out_ref, zbuf, pbuf):
    for z in range(NZ):
        left, right = both(in_ref[z])
        zbuf[pl.ds(z * ZBUF, ZB), :] = left
        zbuf[pl.ds(z * ZBUF + ZB - 1, ZB), :] = right

    def step(r, carry):
        for z in range(NZ):
            row, col = r * 4 + z // 4, (z % 4) * LANE
            pbuf[pl.ds(r * PBUF + table[row, col + 1], SLOTS), :] = zbuf[
                pl.ds(z * ZBUF + table[row, col], SLOTS), :
            ]
        return carry

    lax.fori_loop(0, PLANE, step, 0)
    left = lanes64((PB, 128))
    for r in range(PLANE):
        out_ref[r] = jnp.where(left, pbuf[pl.ds(r * PBUF, PB), :], pbuf[pl.ds(r * PBUF + PB - 1, PB), :])
        out_ref[r, pl.ds(PB - 1, 1), :] = mark_ref[...]


def back_kernel(table, in_ref, out_ref, zbuf, pbuf):
    mark = jnp.zeros((1, 128), F32)
    for r in range(PLANE):
        left, right = both(in_ref[r])
        pbuf[pl.ds(r * PBUF, PB), :] = left
        pbuf[pl.ds(r * PBUF + PB - 1, PB), :] = right
        mark = jnp.maximum(mark, in_ref[r, pl.ds(PB - 1, 1), :])

    def step(r, carry):
        for z in range(NZ):
            row, col = r * 4 + z // 4, (z % 4) * LANE
            zbuf[pl.ds(z * ZBUF + table[row, col], SLOTS), :] = pbuf[
                pl.ds(r * PBUF + table[row, col + 1], SLOTS), :
            ]
        return carry

    lax.fori_loop(0, PLANE, step, 0)
    left = lanes64((ZB, 128))
    for z in range(NZ):
        out_ref[z] = jnp.where(left, zbuf[pl.ds(z * ZBUF, ZB), :], zbuf[pl.ds(z * ZBUF + ZB - 1, ZB), :])
        out_ref[z, pl.ds(ZB - 1, 1), :] = mark


def gene_kernel(
    addr, again, gene, in_ref, dose_ref, weight_ref, out_ref, one_ref, two_ref, held, total, weighted, work
):
    mark = jnp.zeros((1, 128), F32)
    for m in range(PLANE):
        left, right = both(in_ref[m])
        held[pl.ds(m * 2 * PB, PB), :] = left
        held[pl.ds(m * 2 * PB + PB, PB), :] = right
        mark = jnp.maximum(mark, in_ref[m, pl.ds(PB - 1, 1), :])
    held[pl.ds(HOLD, 8), :] = jnp.zeros((8, 128), F32)
    total[...] = jnp.zeros_like(total)
    two_ref[...] = jnp.zeros_like(two_ref)

    def gather(t, slot):
        for c in range(TILE):
            work[slot, pl.ds(c, 1), :] = held[pl.ds(addr[t, c], 1), :]

    def score(t, slot):
        total[gene[t]] += dot(dose_ref[t], split(work[slot]))

    def scored(t, carry):
        gather(t * 2 + 1, 1)
        score(t * 2, 0)
        gather(jnp.minimum(t * 2 + 2, TILES - 1), 0)
        score(t * 2 + 1, 1)
        return carry

    gather(0, 0)
    lax.fori_loop(0, TILES // 2, scored, 0)
    for k in range(GENES):
        weight = weight_ref[:, pl.ds(k, 1)]
        scores = fold(total[k]) * weight
        one_ref[pl.ds(k, 1), :] = jnp.sum(scores * scores, axis=0, keepdims=True) * (1.0 / VT)
        weighted[k] = split(scores * weight)

    def returned(t, slot):
        rows = fold(dot(dose_ref[t], weighted[gene[t]], 0, 0))
        two_ref[pl.ds(gene[t], 1), :] += jnp.sum(rows * rows, axis=0, keepdims=True) * (1.0 / TILE)
        work[slot] = rows

    def scatter(t, slot):
        for c in range(TILE):
            held[pl.ds(addr[t, c], 1), :] = work[slot, pl.ds(c, 1), :]

    @pl.when(again[0, 0] == 0)
    def _():
        def sent(t, carry):
            returned(t * 2 + 1, 1)
            scatter(t * 2, 0)
            returned(t * 2 + 2, 0)
            scatter(t * 2 + 1, 1)
            return carry

        returned(0, 0)
        lax.fori_loop(0, TILES // 2 - 1, sent, 0)
        returned(TILES - 1, 1)
        scatter(TILES - 2, 0)
        scatter(TILES - 1, 1)

    @pl.when(again[0, 0] != 0)
    def _():
        held[...] = jnp.zeros_like(held)

        def summed(t, carry):
            returned(t, 0)

            def add(c, inner):
                held[pl.ds(addr[t, c], 1), :] += work[0, pl.ds(c, 1), :]
                return inner

            lax.fori_loop(0, TILE, add, 0)
            return carry

        lax.fori_loop(0, TILES, summed, 0)

    left = lanes64((PB, 128))
    for m in range(PLANE):
        out_ref[m] = jnp.where(left, held[pl.ds(m * 2 * PB, PB), :], held[pl.ds(m * 2 * PB + PB, PB), :])
        out_ref[m, pl.ds(PB - 1, 1), :] = mark


def sum_kernel(in_ref, index_ref, out_ref, mark_ref, total):
    total[...] = jnp.zeros_like(total)
    at = (iota((ROWS, 2 * ZB), 0) + 1).astype(F32)

    def step(z, mark):
        block = in_ref[z]
        index = index_ref[pl.ds(z, 1), :]
        turned = jnp.transpose(block)
        rows = jnp.concatenate([turned[:PROBES], turned[PROBES:]], axis=1)
        rows = jnp.where(index > 0.5, rows, 0.0)
        high = rows.astype(BF16).astype(F32)
        parts = jnp.concatenate([high, rows - high], axis=0).astype(BF16)
        total[...] += dot(parts, ones_where(at == index), 1, 1)
        return jnp.maximum(mark, in_ref[z, pl.ds(ZB - 1, 1), :])

    mark_ref[...] = lax.fori_loop(0, NZ, step, jnp.zeros((1, 128), F32))
    out_ref[...] = total[pl.ds(0, PROBES), :] + total[pl.ds(PROBES, PROBES), :]


VMEM = pl.BlockSpec(memory_space=pltpu.VMEM)
SMEM = pl.BlockSpec(memory_space=pltpu.SMEM)


def call(kernel, outs, ins, scratch=(), out_specs=None, cost=2_000_000, limit=24):
    shapes = [jax.ShapeDtypeStruct(*o) for o in outs]
    return pl.pallas_call(
        kernel,
        out_shape=shapes,
        in_specs=ins,
        out_specs=[VMEM] * len(shapes) if out_specs is None else out_specs,
        scratch_shapes=list(scratch),
        cost_estimate=pl.CostEstimate(flops=cost * 100, bytes_accessed=cost, transcendentals=0),
        compiler_params=pltpu.CompilerParams(vmem_limit_bytes=limit << 20),
    )


def packed(probes, dosages, weights, send_rows, tile_src, tile_gene):
    used, count = call(used_kernel, [((128, 128), F32)] * 2, [VMEM])(tile_src)
    asked = lax.all_to_all(used.reshape(PLANE, 4, 128), FLAT, 0, 0, tiled=True).reshape(128, 128)
    (met,) = call(meet_kernel, [((NZ, 8, 128), F32)], [VMEM])(asked)
    met = lax.all_to_all(met, "z", 0, 0, tiled=True).reshape(128, 128)
    table, mark = call(table_kernel, [((128, 128), I32), ((1, 128), F32)], [VMEM])(asked)
    addr, again = call(
        place_kernel, [((TILES, TILE), I32), ((1, 1), I32)], [VMEM, VMEM], out_specs=[VMEM, SMEM]
    )(tile_src, count)
    rows = jnp.pad(send_rows[0], ((0, 0), (0, LANE - SLOTS))).reshape(128, 128)
    block, index = call(
        send_kernel,
        [((NZ, ZB, 128), F32), ((NZ, 2 * ZB), F32)],
        [VMEM] * 3,
        [pltpu.VMEM((128, 128), I32), pltpu.VMEM((128, 128), I32), pltpu.VMEM((2 * PROBES, ROWS), BF16)],
    )(met, rows, probes)
    block = lax.all_to_all(block, "z", 0, 0, tiled=True)
    buffers = [pltpu.VMEM((NZ * ZBUF, 128), F32), pltpu.VMEM((PLANE * PBUF, 128), F32)]
    (block,) = call(relay_kernel, [((PLANE, PB, 128), F32)], [SMEM, VMEM, VMEM], buffers)(table, mark, block)
    block = lax.all_to_all(block, FLAT, 0, 0, tiled=True)
    block, one, two = call(
        gene_kernel,
        [((PLANE, PB, 128), F32), ((GENES, 128), F32), ((GENES, 128), F32)],
        [SMEM] * 3 + [VMEM] * 3,
        [
            pltpu.VMEM((HOLD + 8, 128), F32),
            pltpu.VMEM((GENES, VT, 128), F32),
            pltpu.VMEM((GENES, VT, 128), BF16),
            pltpu.VMEM((2, TILE, 128), F32),
        ],
    )(addr, again, tile_gene, block, dosages, weights.T)
    block = lax.all_to_all(block, FLAT, 0, 0, tiled=True)
    (block,) = call(back_kernel, [((NZ, ZB, 128), F32)], [SMEM, VMEM], buffers)(table, block)
    block = lax.all_to_all(block, "z", 0, 0, tiled=True)
    projected, mark = call(
        sum_kernel,
        [((PROBES, ROWS), F32), ((1, 128), F32)],
        [VMEM] * 2,
        [pltpu.VMEM((2 * PROBES, ROWS), F32)],
    )(block, index)
    moments = jnp.stack([one[:, :PROBES], two[:, :PROBES]]).transpose(0, 2, 1)
    return projected, moments, mark[0, 0]


def exchange(rows):
    return lax.all_to_all(rows, ALL, 0, 0, tiled=True)


def whole(probes, dosages, weights, send_rows, tile_src, tile_gene):
    rows_sent = send_rows[0]
    high = lax.Precision.HIGHEST
    outgoing = probes.T[rows_sent].reshape(DEV, SLOTS * PROBES // 128, 128)
    incoming = exchange(outgoing).reshape(SRC, PROBES)
    fetched = jnp.concatenate([incoming, jnp.zeros((1, PROBES), F32)], axis=0)
    slab = fetched[tile_src]
    tile_scores = jnp.einsum("tcb,tvc->tbv", slab, dosages, precision=high, preferred_element_type=F32)
    member = (tile_gene[None, :] == jnp.arange(GENES, dtype=I32)[:, None]).astype(F32)
    scores = jnp.einsum("gt,tbv->gbv", member, tile_scores, precision=high) * weights[:, None, :]
    one = jnp.sum(scores * scores, axis=2) / VT
    weighted = jnp.einsum("gt,gbv->tbv", member, scores * weights[:, None, :], precision=high)
    returned = jnp.einsum("tbv,tvc->tcb", weighted, dosages, precision=high, preferred_element_type=F32)
    two = jnp.dot(member, jnp.sum(returned * returned, axis=1), precision=high) / TILE
    sums = jax.ops.segment_sum(returned.reshape(-1, PROBES), tile_src.reshape(-1), num_segments=SRC + 1)
    arrived = exchange(sums[:SRC].reshape(DEV, SLOTS * PROBES // 128, 128))
    projected = jax.ops.segment_sum(
        arrived.reshape(SRC, PROBES), rows_sent.reshape(-1), num_segments=ROWS
    ).T
    return projected, jnp.stack([one, two]).transpose(0, 2, 1)


def shards(*args):
    projected, moments, mark = packed(*args)
    return lax.cond(mark > 0.5, lambda: whole(*args), lambda: (projected, moments))


def solution(mesh):
    fine = Mesh(mesh.devices.reshape(NY, NZ, NC, NX), ALL)
    placed = (P(None, ALL), P(ALL, None, None), P(ALL, None), P(ALL, None, None), P(ALL, None), P(ALL))
    return jax.shard_map(
        shards,
        mesh=fine,
        in_specs=placed,
        out_specs=(P(None, ALL), P(None, None, ALL)),
        check_vma=False,
    )
```

```python
import jax
import jax.numpy as jnp
from jax import lax
from jax.experimental import pallas as pl
from jax.experimental.pallas import tpu as pltpu
from jax.sharding import Mesh, PartitionSpec as P

NY, NZ, NC, NX = 4, 16, 2, 4
PLANE = NY * NC * NX
DEV = NY * NZ * NC * NX
SLOTS = 24
LANE = 32
SRC = DEV * SLOTS
TILES = 40
TILE = 128
VT = 128
GENES = 20
GROUP = 4
GROUPS = TILES // GROUP
PROBES = 64
ROWS = 1024
ZB = 128
ZCAP = 2 * (ZB - 1)
PB = 96
PCAP = 2 * (PB - 1)
ZBUF = 280
PBUF = 216
HOLD = PLANE * 2 * PB
F32 = jnp.float32
BF16 = jnp.bfloat16
I32 = jnp.int32
ALL = ("y", "z", "c", "x")
FLAT = ("y", "c", "x")


def iota(shape, dim):
    return lax.broadcasted_iota(I32, shape, dim)


def dot(a, b, ca=1, cb=0, **kw):
    return lax.dot_general(a, b, (((ca,), (cb,)), ((), ())), preferred_element_type=F32, **kw)


def ones_where(mask):
    return jnp.where(mask, 1.0, 0.0).astype(BF16)


def ones16(mask):
    return jnp.where(mask, jnp.ones((), BF16), jnp.zeros((), BF16))


def short(v):
    return v.astype(I32).astype(jnp.int16)


def lanes64(shape):
    return iota(shape, 1) < PROBES


def fold(v):
    return v + pltpu.roll(v, PROBES, 1)


def split(v):
    high = v.astype(BF16).astype(F32)
    return jnp.where(lanes64(v.shape), high, v - high).astype(BF16)


def both(block):
    turned = pltpu.roll(block, PROBES, 1)
    left = lanes64(block.shape)
    return jnp.where(left, block, turned), jnp.where(left, turned, block)


def source_parts(ref, t, n):
    highs, lows, empties = [], [], []
    for i in range(n):
        p = ref[pl.ds(t * n + i, 1), :]
        o = (p * 43691) >> 20
        highs.append(((o >> 7) * (NC * NX) + (o & 7)) * 4 + ((o >> 5) & 3))
        lows.append(((o >> 3) & 3) * LANE + p - o * SLOTS)
        empties.append(p >= SRC)
    return highs, lows, empties


def one_hots(rows):
    return jnp.concatenate([ones_where(iota((128, 128), 0) == r) for r in rows], axis=1)


def used_kernel(src_ref, used_ref, count_ref):
    count_ref[...] = jnp.zeros_like(count_ref)

    def step(t, carry):
        highs, lows, _ = source_parts(src_ref, t, 8)
        count_ref[...] += dot(one_hots(highs), one_hots(lows), 1, 1)
        return carry

    lax.fori_loop(0, TILES // 8, step, 0)
    used_ref[...] = jnp.minimum(count_ref[...], 1.0)


def place_kernel(src_ref, count_ref, addr_ref, again_ref):
    count = count_ref[...]
    again_ref[0, 0] = jnp.where(jnp.max(count) > 1.5, 1, 0)
    used = ones_where(count > 0.5)
    row, col = iota((128, 128), 0), iota((128, 128), 1)
    before = dot(used, ones_where(row < col))
    number = dot(used, jnp.ones((128, 128), BF16)).astype(BF16)
    earlier = ones_where(((row >> 2) == (col >> 2)) & (col < row))
    rank = jnp.minimum((dot(earlier, number) + before).astype(I32), PCAP)
    place = (row >> 2) * (2 * PB) + rank + jnp.where(rank >= PB - 1, 1, 0)
    turned = jnp.transpose(place)
    high = turned >> 6
    table = jnp.concatenate([high, turned - (high << 6)], axis=0).astype(F32).astype(BF16)

    def step(t, carry):
        highs, lows, empties = source_parts(src_ref, t, 8)
        found = dot(table, one_hots(highs))
        for i in range(8):
            part = found[:, i * 128 : (i + 1) * 128]
            value = part[:128] * 64.0 + part[128:]
            value = jnp.sum(jnp.where(row == lows[i], value, 0.0), axis=0, keepdims=True)
            addr_ref[pl.ds(t * 8 + i, 1), :] = jnp.where(empties[i], HOLD, value.astype(I32))
        return carry

    lax.fori_loop(0, TILES // 8, step, 0)


def meet_kernel(in_ref, out_ref):
    block = iota((8, 128), 1) >> 5
    for high in range(4):
        parts = [in_ref[pl.ds(x * 4 + high, 8, stride=16), :] for x in range(NX)]
        for low in range(4):
            turned = [pltpu.roll(parts[x], ((x - low) * LANE) % 128, 1) for x in range(NX)]
            result = turned[0]
            for x in range(1, NX):
                result = jnp.where(block == x, turned[x], result)
            out_ref[high * 4 + low] = result


def table_kernel(in_ref, table_ref, mark_ref):
    used = ones_where(in_ref[...] > 0.5)
    row, col = iota((128, 128), 0), iota((128, 128), 1)
    segment = dot(used, ones_where((row >> 5) == (col >> 5)))
    whole_row = dot(used, jnp.ones((128, 128), BF16))
    before = dot(used, ones_where((row >> 5) < (col >> 5)))
    owner = dot(ones_where(((row & 3) == (col & 3)) & (col < row)), segment.astype(BF16))
    holder = before + dot(ones_where(((row >> 2) == (col >> 2)) & (col < row)), whole_row.astype(BF16))
    over = jnp.maximum(
        jnp.where(owner + segment > ZCAP, 1.0, 0.0), jnp.where(holder + segment > PCAP, 1.0, 0.0)
    )
    mark_ref[...] = jnp.broadcast_to(jnp.max(over), (1, 128))
    owner, holder = jnp.minimum(owner, float(ZCAP)), jnp.minimum(holder, float(PCAP + 1))
    table_ref[...] = jnp.where((col & 1) == 0, owner, holder).astype(I32)


def send_kernel(
    used_ref, rows_ref, probes_ref, out_ref, index_ref, high_ref, low_ref, value_ref, turned_ref, parts_ref
):
    used = used_ref[...]
    flag = ones_where(used > 0.5)
    row, col = iota((128, 128), 0), iota((128, 128), 1)
    number = dot(flag, jnp.ones((128, 128), BF16))
    start = dot(ones_where(((row >> 3) == (col >> 3)) & (col < row)), number.astype(BF16))
    place = (start + dot(flag, ones_where(row < col))).astype(I32)
    place = place + jnp.where(place >= ZB - 1, 1, 0)
    high_ref[...] = jnp.where(used > 0.5, place >> 7, -1)
    low_ref[...] = place & (ZB - 1)
    high = probes_ref[...].astype(BF16).astype(F32)
    parts_ref[...] = jnp.concatenate([high, probes_ref[...] - high], axis=0).astype(BF16)
    turned_ref[...] = jnp.zeros_like(turned_ref)
    for k in range(DEV // 128):
        turned_ref[pl.ds(k * 128, 128), pl.ds(0, SLOTS)] = jnp.transpose(rows_ref[:, pl.ds(k * 128, 128)])
    value = turned_ref[pl.ds(0, 128, stride=NX), :]
    for x in range(1, NX):
        turned = pltpu.roll(turned_ref[pl.ds(x, 128, stride=NX), :], x * LANE, 1)
        value = jnp.where((col >> 5) == x, turned, value)
    value_ref[...] = value + 1
    which = iota((8, 128), 0)
    at = iota((ZB, 128), 0).astype(jnp.int16)
    subject = (iota((ROWS, 4 * ZB), 0) + 1).astype(jnp.int16)

    def list_of(z):
        values, places = [], []
        for y in range(NY):
            for c in range(NC):
                i = z * (NY * NC) + y * NC + c
                value = value_ref[pl.ds(y * (NZ * NC) + z * NC + c, 1), :]
                digit = jnp.where(which < 2, value >> 5, value & 31)
                match = ((which & 1) == high_ref[pl.ds(i, 1), :]) & (which < 4)
                values.append(jnp.where(match, digit, 0).astype(F32).astype(BF16))
                places.append(ones16(at == low_ref[pl.ds(i, 1), :].astype(jnp.int16)))
        listed = dot(jnp.concatenate(values, axis=1), jnp.concatenate(places, axis=1), 1, 1)
        index = listed[:2] * 32.0 + listed[2:4]
        index = jnp.concatenate([index[:1], index[1:]], axis=1)
        index_ref[pl.ds(z, 1), :] = index
        return index

    def lists_of(i):
        return jnp.concatenate([list_of(2 * i), list_of(2 * i + 1)], axis=1)

    def step(i, index):
        later = lists_of(jnp.minimum(i + 1, NZ // 2 - 1))
        rows = dot(parts_ref[...], ones16(subject == short(index)))
        rows = rows[:PROBES] + rows[PROBES:]
        for n in range(2):
            left, right = rows[:, 2 * n * ZB : (2 * n + 1) * ZB], rows[:, (2 * n + 1) * ZB : (2 * n + 2) * ZB]
            out_ref[2 * i + n] = jnp.transpose(jnp.concatenate([left, right], axis=0))
        return later

    lax.fori_loop(0, NZ // 2, step, lists_of(0))


def relay_kernel(table, mark_ref, in_ref, out_ref, zbuf, pbuf):
    for z in range(NZ):
        left, right = both(in_ref[z])
        zbuf[pl.ds(z * ZBUF, ZB), :] = left
        zbuf[pl.ds(z * ZBUF + ZB - 1, ZB), :] = right

    def step(r, carry):
        for z in range(NZ):
            row, col = r * 4 + z // 4, (z % 4) * LANE
            pbuf[pl.ds(r * PBUF + table[row, col + 1], SLOTS), :] = zbuf[
                pl.ds(z * ZBUF + table[row, col], SLOTS), :
            ]
        return carry

    lax.fori_loop(0, PLANE, step, 0)
    left = lanes64((PB, 128))
    for r in range(PLANE):
        out_ref[r] = jnp.where(left, pbuf[pl.ds(r * PBUF, PB), :], pbuf[pl.ds(r * PBUF + PB - 1, PB), :])
        out_ref[r, pl.ds(PB - 1, 1), :] = mark_ref[...]


def back_kernel(table, in_ref, out_ref, zbuf, pbuf):
    mark = jnp.zeros((1, 128), F32)
    for r in range(PLANE):
        left, right = both(in_ref[r])
        pbuf[pl.ds(r * PBUF, PB), :] = left
        pbuf[pl.ds(r * PBUF + PB - 1, PB), :] = right
        mark = jnp.maximum(mark, in_ref[r, pl.ds(PB - 1, 1), :])

    def step(r, carry):
        for z in range(NZ):
            row, col = r * 4 + z // 4, (z % 4) * LANE
            zbuf[pl.ds(z * ZBUF + table[row, col], SLOTS), :] = pbuf[
                pl.ds(r * PBUF + table[row, col + 1], SLOTS), :
            ]
        return carry

    lax.fori_loop(0, PLANE, step, 0)
    left = lanes64((ZB, 128))
    for z in range(NZ):
        out_ref[z] = jnp.where(left, zbuf[pl.ds(z * ZBUF, ZB), :], zbuf[pl.ds(z * ZBUF + ZB - 1, ZB), :])
        out_ref[z, pl.ds(ZB - 1, 1), :] = mark


def gene_kernel(
    addr,
    again,
    gene,
    addr_ref,
    in_ref,
    dose_ref,
    weight_ref,
    out_ref,
    one_ref,
    two_ref,
    held,
    total,
    weighted,
    work,
    near,
    sem,
):
    def fetch(group, slot):
        return pltpu.make_async_copy(
            addr_ref.at[pl.ds(lax.rem(group, GROUPS) * GROUP, GROUP), :], near.at[slot], sem.at[slot]
        )

    fetch(0, 0).start()
    fetch(1, 1).start()
    mark = jnp.zeros((1, 128), F32)
    for m in range(PLANE):
        left, right = both(in_ref[m])
        held[pl.ds(m * 2 * PB, PB), :] = left
        held[pl.ds(m * 2 * PB + PB, PB), :] = right
        mark = jnp.maximum(mark, in_ref[m, pl.ds(PB - 1, 1), :])
    held[pl.ds(HOLD, 8), :] = jnp.zeros((8, 128), F32)
    total[...] = jnp.zeros_like(total)
    two_ref[...] = jnp.zeros_like(two_ref)

    def gather(slot, k):
        for c in range(TILE):
            work[k % 2, pl.ds(c, 1), :] = held[pl.ds(near[slot, k, c], 1), :]

    def score(t, k):
        total[gene[t]] += dot(dose_ref[t], split(work[k % 2]))

    def scored(i, carry):
        for slot in range(2):
            group = i * 2 + slot
            fetch(group, slot).wait()
            for k in range(GROUP):
                gather(slot, k)
                if k > 0:
                    score(group * GROUP + k - 1, k - 1)
            fetch(group + 2, slot).start()
            score(group * GROUP + GROUP - 1, GROUP - 1)
        return carry

    lax.fori_loop(0, GROUPS // 2, scored, 0)
    for k in range(GENES):
        weight = weight_ref[:, pl.ds(k, 1)]
        scores = fold(total[k]) * weight
        one_ref[pl.ds(k, 1), :] = jnp.sum(scores * scores, axis=0, keepdims=True) * (1.0 / VT)
        weighted[k] = split(scores * weight)

    def returned(t, slot):
        rows = fold(dot(dose_ref[t], weighted[gene[t]], 0, 0))
        two_ref[pl.ds(gene[t], 1), :] += jnp.sum(rows * rows, axis=0, keepdims=True) * (1.0 / TILE)
        work[slot] = rows

    def scatter(slot, k):
        for c in range(TILE):
            held[pl.ds(near[slot, k, c], 1), :] = work[k % 2, pl.ds(c, 1), :]

    @pl.when(again[0, 0] == 0)
    def _():
        def sent(i, carry):
            for slot in range(2):
                group = i * 2 + slot
                fetch(group, slot).wait()
                returned(group * GROUP, 0)
                for k in range(GROUP):
                    if k + 1 < GROUP:
                        returned(group * GROUP + k + 1, (k + 1) % 2)
                    scatter(slot, k)
                fetch(group + 2, slot).start()
            return carry

        lax.fori_loop(0, GROUPS // 2, sent, 0)

    @pl.when(again[0, 0] != 0)
    def _():
        held[...] = jnp.zeros_like(held)

        def summed(t, carry):
            returned(t, 0)

            def add(c, inner):
                held[pl.ds(addr[t, c], 1), :] += work[0, pl.ds(c, 1), :]
                return inner

            lax.fori_loop(0, TILE, add, 0)
            return carry

        lax.fori_loop(0, TILES, summed, 0)

    fetch(0, 0).wait()
    fetch(1, 1).wait()
    left = lanes64((PB, 128))
    for m in range(PLANE):
        out_ref[m] = jnp.where(left, held[pl.ds(m * 2 * PB, PB), :], held[pl.ds(m * 2 * PB + PB, PB), :])
        out_ref[m, pl.ds(PB - 1, 1), :] = mark


def sum_kernel(in_ref, index_ref, out_ref, mark_ref, total):
    total[...] = jnp.zeros_like(total)
    at = (iota((ROWS, 8 * ZB), 0) + 1).astype(jnp.int16)

    def step(i, mark):
        rows, indices = [], []
        for n in range(4):
            z = i * 4 + n
            turned = jnp.transpose(in_ref[z])
            rows += [turned[:PROBES], turned[PROBES:]]
            indices.append(index_ref[pl.ds(z, 1), :])
            mark = jnp.maximum(mark, in_ref[z, pl.ds(ZB - 1, 1), :])
        index = jnp.concatenate(indices, axis=1)
        rows = jnp.where(index > 0.5, jnp.concatenate(rows, axis=1), 0.0)
        high = rows.astype(BF16).astype(F32)
        parts = jnp.concatenate([high, rows - high], axis=0).astype(BF16)
        total[...] += dot(parts, ones16(at == short(index)), 1, 1)
        return mark

    mark_ref[...] = lax.fori_loop(0, NZ // 4, step, jnp.zeros((1, 128), F32))
    out_ref[...] = total[pl.ds(0, PROBES), :] + total[pl.ds(PROBES, PROBES), :]


VMEM = pl.BlockSpec(memory_space=pltpu.VMEM)
SMEM = pl.BlockSpec(memory_space=pltpu.SMEM)


def call(kernel, outs, ins, scratch=(), out_specs=None, cost=2_000_000, limit=24):
    shapes = [jax.ShapeDtypeStruct(*o) for o in outs]
    return pl.pallas_call(
        kernel,
        out_shape=shapes,
        in_specs=ins,
        out_specs=[VMEM] * len(shapes) if out_specs is None else out_specs,
        scratch_shapes=list(scratch),
        cost_estimate=pl.CostEstimate(flops=cost * 100, bytes_accessed=cost, transcendentals=0),
        compiler_params=pltpu.CompilerParams(vmem_limit_bytes=limit << 20),
    )


def packed(probes, dosages, weights, send_rows, tile_src, tile_gene):
    used, count = call(used_kernel, [((128, 128), F32)] * 2, [VMEM])(tile_src)
    asked = lax.all_to_all(used.reshape(PLANE, 4, 128), FLAT, 0, 0, tiled=True).reshape(128, 128)
    (met,) = call(meet_kernel, [((NZ, 8, 128), F32)], [VMEM])(asked)
    met = lax.all_to_all(met, "z", 0, 0, tiled=True).reshape(128, 128)
    asked, count, met = lax.optimization_barrier((asked, count, met))
    table, mark = call(table_kernel, [((128, 128), I32), ((1, 128), F32)], [VMEM])(asked)
    addr, again = call(
        place_kernel, [((TILES, TILE), I32), ((1, 1), I32)], [VMEM, VMEM], out_specs=[VMEM, SMEM]
    )(tile_src, count)
    block, index = call(
        send_kernel,
        [((NZ, ZB, 128), F32), ((NZ, 2 * ZB), F32)],
        [VMEM] * 3,
        [pltpu.VMEM((128, 128), I32)] * 3
        + [pltpu.VMEM((DEV, 128), I32), pltpu.VMEM((2 * PROBES, ROWS), BF16)],
    )(met, send_rows[0].T, probes)
    block = lax.all_to_all(block, "z", 0, 0, tiled=True)
    buffers = [pltpu.VMEM((NZ * ZBUF, 128), F32), pltpu.VMEM((PLANE * PBUF, 128), F32)]
    (block,) = call(relay_kernel, [((PLANE, PB, 128), F32)], [SMEM, VMEM, VMEM], buffers)(table, mark, block)
    block = lax.all_to_all(block, FLAT, 0, 0, tiled=True)
    block, one, two = call(
        gene_kernel,
        [((PLANE, PB, 128), F32), ((GENES, 128), F32), ((GENES, 128), F32)],
        [SMEM] * 3 + [VMEM] * 4,
        [
            pltpu.VMEM((HOLD + 8, 128), F32),
            pltpu.VMEM((GENES, VT, 128), F32),
            pltpu.VMEM((GENES, VT, 128), BF16),
            pltpu.VMEM((2, TILE, 128), F32),
            pltpu.SMEM((2, GROUP, TILE), I32),
            pltpu.SemaphoreType.DMA((2,)),
        ],
    )(addr, again, tile_gene, addr, block, dosages, weights.T)
    block = lax.all_to_all(block, FLAT, 0, 0, tiled=True)
    (block,) = call(back_kernel, [((NZ, ZB, 128), F32)], [SMEM, VMEM], buffers)(table, block)
    block = lax.all_to_all(block, "z", 0, 0, tiled=True)
    projected, mark = call(
        sum_kernel,
        [((PROBES, ROWS), F32), ((1, 128), F32)],
        [VMEM] * 2,
        [pltpu.VMEM((2 * PROBES, ROWS), F32)],
    )(block, index)
    moments = jnp.stack([one[:, :PROBES], two[:, :PROBES]]).transpose(0, 2, 1)
    return projected, moments, mark[0, 0]


def exchange(rows):
    return lax.all_to_all(rows, ALL, 0, 0, tiled=True)


def whole(probes, dosages, weights, send_rows, tile_src, tile_gene):
    rows_sent = send_rows[0]
    high = lax.Precision.HIGHEST
    outgoing = probes.T[rows_sent].reshape(DEV, SLOTS * PROBES // 128, 128)
    incoming = exchange(outgoing).reshape(SRC, PROBES)
    fetched = jnp.concatenate([incoming, jnp.zeros((1, PROBES), F32)], axis=0)
    slab = fetched[tile_src]
    tile_scores = jnp.einsum("tcb,tvc->tbv", slab, dosages, precision=high, preferred_element_type=F32)
    member = (tile_gene[None, :] == jnp.arange(GENES, dtype=I32)[:, None]).astype(F32)
    scores = jnp.einsum("gt,tbv->gbv", member, tile_scores, precision=high) * weights[:, None, :]
    one = jnp.sum(scores * scores, axis=2) / VT
    weighted = jnp.einsum("gt,gbv->tbv", member, scores * weights[:, None, :], precision=high)
    returned = jnp.einsum("tbv,tvc->tcb", weighted, dosages, precision=high, preferred_element_type=F32)
    two = jnp.dot(member, jnp.sum(returned * returned, axis=1), precision=high) / TILE
    sums = jax.ops.segment_sum(returned.reshape(-1, PROBES), tile_src.reshape(-1), num_segments=SRC + 1)
    arrived = exchange(sums[:SRC].reshape(DEV, SLOTS * PROBES // 128, 128))
    projected = jax.ops.segment_sum(
        arrived.reshape(SRC, PROBES), rows_sent.reshape(-1), num_segments=ROWS
    ).T
    return projected, jnp.stack([one, two]).transpose(0, 2, 1)


def shards(*args):
    projected, moments, mark = packed(*args)
    return lax.cond(mark > 0.5, lambda: whole(*args), lambda: (projected, moments))


def solution(mesh):
    fine = Mesh(mesh.devices.reshape(NY, NZ, NC, NX), ALL)
    placed = (P(None, ALL), P(ALL, None, None), P(ALL, None), P(ALL, None, None), P(ALL, None), P(ALL))
    return jax.shard_map(
        shards,
        mesh=fine,
        in_specs=placed,
        out_specs=(P(None, ALL), P(None, None, ALL)),
        check_vma=False,
    )
```

```python
import jax
import jax.numpy as jnp
from jax import lax
from jax.experimental import pallas as pl
from jax.experimental.pallas import tpu as pltpu
from jax.sharding import Mesh, PartitionSpec as P

NY, NZ, NC, NX = 4, 16, 2, 4
PLANE = NY * NC * NX
DEV = NY * NZ * NC * NX
SLOTS = 24
LANE = 32
SRC = DEV * SLOTS
TILES = 40
TILE = 128
VT = 128
GENES = 20
GROUP = 4
GROUPS = TILES // GROUP
PROBES = 64
ROWS = 1024
ZB = 128
ZCAP = 2 * (ZB - 1)
PB = 96
PCAP = 2 * (PB - 1)
ZBUF = 280
PBUF = 216
HOLD = PLANE * 2 * PB
F32 = jnp.float32
BF16 = jnp.bfloat16
I32 = jnp.int32
ALL = ("y", "z", "c", "x")
FLAT = ("y", "c", "x")


def iota(shape, dim):
    return lax.broadcasted_iota(I32, shape, dim)


def dot(a, b, ca=1, cb=0, **kw):
    return lax.dot_general(a, b, (((ca,), (cb,)), ((), ())), preferred_element_type=F32, **kw)


def ones_where(mask):
    return jnp.where(mask, 1.0, 0.0).astype(BF16)


def ones16(mask):
    return jnp.where(mask, jnp.ones((), BF16), jnp.zeros((), BF16))


def short(v):
    return v.astype(I32).astype(jnp.int16)


def lanes64(shape):
    return iota(shape, 1) < PROBES


def fold(v):
    return v + pltpu.roll(v, PROBES, 1)


def split(v):
    high = v.astype(BF16).astype(F32)
    return jnp.where(lanes64(v.shape), high, v - high).astype(BF16)


def both(block):
    turned = pltpu.roll(block, PROBES, 1)
    left = lanes64(block.shape)
    return jnp.where(left, block, turned), jnp.where(left, turned, block)


def source_parts(ref, t, n):
    highs, lows, empties = [], [], []
    for i in range(n):
        p = ref[pl.ds(t * n + i, 1), :]
        o = (p * 43691) >> 20
        highs.append(((o >> 7) * (NC * NX) + (o & 7)) * 4 + ((o >> 5) & 3))
        lows.append(((o >> 3) & 3) * LANE + p - o * SLOTS)
        empties.append(p >= SRC)
    return highs, lows, empties


def one_hots(rows):
    return jnp.concatenate([ones16(iota((128, 128), 0).astype(jnp.int16) == r.astype(jnp.int16)) for r in rows], axis=1)


def used_kernel(src_ref, used_ref, count_ref):
    count_ref[...] = jnp.zeros_like(count_ref)

    def step(t, carry):
        highs, lows, _ = source_parts(src_ref, t, 8)
        count_ref[...] += dot(one_hots(highs), one_hots(lows), 1, 1)
        return carry

    lax.fori_loop(0, TILES // 8, step, 0)
    used_ref[...] = jnp.minimum(count_ref[...], 1.0)


def place_kernel(src_ref, count_ref, addr_ref, again_ref):
    count = count_ref[...]
    again_ref[0, 0] = jnp.where(jnp.max(count) > 1.5, 1, 0)
    used = ones_where(count > 0.5)
    row, col = iota((128, 128), 0), iota((128, 128), 1)
    before = dot(used, ones_where(row < col))
    number = dot(used, jnp.ones((128, 128), BF16)).astype(BF16)
    earlier = ones_where(((row >> 2) == (col >> 2)) & (col < row))
    rank = jnp.minimum((dot(earlier, number) + before).astype(I32), PCAP)
    place = (row >> 2) * (2 * PB) + rank + jnp.where(rank >= PB - 1, 1, 0)
    turned = jnp.transpose(place)
    high = turned >> 6
    table = jnp.concatenate([high, turned - (high << 6)], axis=0).astype(F32).astype(BF16)

    def step(t, carry):
        highs, lows, empties = source_parts(src_ref, t, 8)
        found = dot(table, one_hots(highs))
        for i in range(8):
            part = found[:, i * 128 : (i + 1) * 128]
            value = part[:128] * 64.0 + part[128:]
            value = jnp.sum(jnp.where(row == lows[i], value, 0.0), axis=0, keepdims=True)
            addr_ref[pl.ds(t * 8 + i, 1), :] = jnp.where(empties[i], HOLD, value.astype(I32))
        return carry

    lax.fori_loop(0, TILES // 8, step, 0)


def meet_kernel(in_ref, out_ref):
    block = iota((8, 128), 1) >> 5
    for high in range(4):
        parts = [in_ref[pl.ds(x * 4 + high, 8, stride=16), :] for x in range(NX)]
        for low in range(4):
            turned = [pltpu.roll(parts[x], ((x - low) * LANE) % 128, 1) for x in range(NX)]
            result = turned[0]
            for x in range(1, NX):
                result = jnp.where(block == x, turned[x], result)
            out_ref[high * 4 + low] = result


def table_kernel(in_ref, table_ref, mark_ref):
    used = ones_where(in_ref[...] > 0.5)
    row, col = iota((128, 128), 0), iota((128, 128), 1)
    segment = dot(used, ones_where((row >> 5) == (col >> 5)))
    whole_row = dot(used, jnp.ones((128, 128), BF16))
    before = dot(used, ones_where((row >> 5) < (col >> 5)))
    owner = dot(ones_where(((row & 3) == (col & 3)) & (col < row)), segment.astype(BF16))
    holder = before + dot(ones_where(((row >> 2) == (col >> 2)) & (col < row)), whole_row.astype(BF16))
    over = jnp.maximum(
        jnp.where(owner + segment > ZCAP, 1.0, 0.0), jnp.where(holder + segment > PCAP, 1.0, 0.0)
    )
    mark_ref[...] = jnp.broadcast_to(jnp.max(over), (1, 128))
    owner = jnp.minimum(owner, float(ZCAP)).astype(I32) + ((row & 3) * 4 + (col >> 5)) * ZBUF
    holder = jnp.minimum(holder, float(PCAP + 1)).astype(I32) + (row >> 2) * PBUF
    table_ref[...] = jnp.where((col & 1) == 0, owner, holder)


def ready_kernel(rows_ref, probes_ref, value_ref, parts_ref, turned_ref):
    col = iota((128, 128), 1)
    high = probes_ref[...].astype(BF16).astype(F32)
    parts_ref[...] = jnp.concatenate([high, probes_ref[...] - high], axis=0).astype(BF16)
    turned_ref[...] = jnp.zeros_like(turned_ref)
    for k in range(DEV // 128):
        turned_ref[pl.ds(k * 128, 128), pl.ds(0, SLOTS)] = jnp.transpose(rows_ref[:, pl.ds(k * 128, 128)])
    value = turned_ref[pl.ds(0, 128, stride=NX), :]
    for x in range(1, NX):
        turned = pltpu.roll(turned_ref[pl.ds(x, 128, stride=NX), :], x * LANE, 1)
        value = jnp.where((col >> 5) == x, turned, value)
    value_ref[...] = value + 1


def send_kernel(used_ref, value_ref, parts_ref, out_ref, index_ref, high_ref, low_ref, done, sem):
    used = used_ref[...]
    flag = ones_where(used > 0.5)
    row, col = iota((128, 128), 0), iota((128, 128), 1)
    number = dot(flag, jnp.ones((128, 128), BF16))
    start = dot(ones_where(((row >> 3) == (col >> 3)) & (col < row)), number.astype(BF16))
    place = (start + dot(flag, ones_where(row < col))).astype(I32)
    place = place + jnp.where(place >= ZB - 1, 1, 0)
    high_ref[...] = jnp.where(used > 0.5, place >> 7, -1)
    low_ref[...] = place & (ZB - 1)
    which = iota((8, 128), 0)
    at = iota((ZB, 128), 0).astype(jnp.int16)
    subject = (iota((ROWS, 4 * ZB), 0) + 1).astype(jnp.int16)

    def list_of(z):
        values, places = [], []
        for y in range(NY):
            for c in range(NC):
                i = z * (NY * NC) + y * NC + c
                value = value_ref[pl.ds(y * (NZ * NC) + z * NC + c, 1), :]
                digit = jnp.where(which < 2, value >> 5, value & 31)
                match = ((which & 1) == high_ref[pl.ds(i, 1), :]) & (which < 4)
                values.append(jnp.where(match, digit, 0).astype(F32).astype(BF16))
                places.append(ones16(at == low_ref[pl.ds(i, 1), :].astype(jnp.int16)))
        listed = dot(jnp.concatenate(values, axis=1), jnp.concatenate(places, axis=1), 1, 1)
        index = listed[:2] * 32.0 + listed[2:4]
        index = jnp.concatenate([index[:1], index[1:]], axis=1)
        index_ref[pl.ds(z, 1), :] = index
        return index

    def lists_of(i):
        return jnp.concatenate([list_of(2 * i), list_of(2 * i + 1)], axis=1)

    def step(i, index):
        later = lists_of(jnp.minimum(i + 1, NZ // 2 - 1))
        rows = dot(parts_ref[...], ones16(subject == short(index)))
        rows = rows[:PROBES] + rows[PROBES:]
        for n in range(2):
            left, right = rows[:, 2 * n * ZB : (2 * n + 1) * ZB], rows[:, (2 * n + 1) * ZB : (2 * n + 2) * ZB]
            done[2 * i + n] = jnp.transpose(jnp.concatenate([left, right], axis=0))
        leave(i).start()
        return later

    def leave(i):
        part = pl.ds(2 * i, 2)
        return pltpu.make_async_copy(done.at[part], out_ref.at[part], sem.at[i])

    lax.fori_loop(0, NZ // 2, step, lists_of(0))
    for i in range(NZ // 2):
        leave(i).wait()


def relay_kernel(table, mark_ref, in_ref, out_ref, zbuf, pbuf, done, sem):
    for z in range(NZ):
        left, right = both(in_ref[z])
        zbuf[pl.ds(z * ZBUF, ZB), :] = left
        zbuf[pl.ds(z * ZBUF + ZB - 1, ZB), :] = right
    left = lanes64((PB, 128))
    copies = []
    for r in range(PLANE):
        for z in range(NZ):
            row, col = r * 4 + z // 4, (z % 4) * LANE
            pbuf[pl.ds(table[row, col + 1], SLOTS), :] = zbuf[pl.ds(table[row, col], SLOTS), :]
        done[r] = jnp.where(left, pbuf[pl.ds(r * PBUF, PB), :], pbuf[pl.ds(r * PBUF + PB - 1, PB), :])
        done[r, pl.ds(PB - 1, 1), :] = mark_ref[...]
        if r % 8 == 7:
            part = pl.ds(r - 7, 8)
            copies.append(pltpu.make_async_copy(done.at[part], out_ref.at[part], sem.at[r // 8]))
            copies[-1].start()
    for copy in copies:
        copy.wait()


def back_kernel(table, in_ref, out_ref, zbuf, pbuf, done, sem):
    mark = jnp.zeros((1, 128), F32)
    for r in range(PLANE):
        left, right = both(in_ref[r])
        pbuf[pl.ds(r * PBUF, PB), :] = left
        pbuf[pl.ds(r * PBUF + PB - 1, PB), :] = right
        mark = jnp.maximum(mark, in_ref[r, pl.ds(PB - 1, 1), :])
    left = lanes64((ZB, 128))
    copies = []
    for z in range(NZ):
        for r in range(PLANE):
            row, col = r * 4 + z // 4, (z % 4) * LANE
            zbuf[pl.ds(table[row, col], SLOTS), :] = pbuf[pl.ds(table[row, col + 1], SLOTS), :]
        done[z] = jnp.where(left, zbuf[pl.ds(z * ZBUF, ZB), :], zbuf[pl.ds(z * ZBUF + ZB - 1, ZB), :])
        done[z, pl.ds(ZB - 1, 1), :] = mark
        if z % 4 == 3:
            part = pl.ds(z - 3, 4)
            copies.append(pltpu.make_async_copy(done.at[part], out_ref.at[part], sem.at[z // 4]))
            copies[-1].start()
    for copy in copies:
        copy.wait()


def gene_kernel(
    addr,
    again,
    gene,
    addr_ref,
    in_ref,
    dose_ref,
    weight_ref,
    out_ref,
    one_ref,
    two_ref,
    held,
    total,
    weighted,
    work,
    near,
    done,
    sem,
    out_sem,
):
    def fetch(group, slot):
        return pltpu.make_async_copy(
            addr_ref.at[pl.ds(lax.rem(group, GROUPS) * GROUP, GROUP), :], near.at[slot], sem.at[slot]
        )

    fetch(0, 0).start()
    fetch(1, 1).start()
    mark = jnp.zeros((1, 128), F32)
    for m in range(PLANE):
        left, right = both(in_ref[m])
        held[pl.ds(m * 2 * PB, PB), :] = left
        held[pl.ds(m * 2 * PB + PB, PB), :] = right
        mark = jnp.maximum(mark, in_ref[m, pl.ds(PB - 1, 1), :])
    held[pl.ds(HOLD, 8), :] = jnp.zeros((8, 128), F32)
    total[...] = jnp.zeros_like(total)
    two_ref[...] = jnp.zeros_like(two_ref)

    def gather(slot, k):
        for c in range(TILE):
            work[k % 2, pl.ds(c, 1), :] = held[pl.ds(near[slot, k, c], 1), :]

    def score(t, k):
        total[gene[t]] += dot(dose_ref[t], split(work[k % 2]))

    def scored(i, carry):
        for slot in range(2):
            group = i * 2 + slot
            fetch(group, slot).wait()
            for k in range(GROUP):
                gather(slot, k)
                score(jnp.maximum(group * GROUP + k - 1, 0), k + 1)
            fetch(group + 2, slot).start()
        return carry

    work[1] = jnp.zeros((TILE, 128), F32)
    lax.fori_loop(0, GROUPS // 2, scored, 0)
    score(TILES - 1, 1)
    for k in range(GENES):
        weight = weight_ref[:, pl.ds(k, 1)]
        scores = fold(total[k]) * weight
        one_ref[pl.ds(k, 1), :] = jnp.sum(scores * scores, axis=0, keepdims=True) * (1.0 / VT)
        weighted[k] = split(scores * weight)

    def returned(t, slot):
        scale = jnp.where(t < TILES, 1.0 / TILE, 0.0)
        t = jnp.minimum(t, TILES - 1)
        rows = fold(dot(dose_ref[t], weighted[gene[t]], 0, 0))
        two_ref[pl.ds(gene[t], 1), :] += jnp.sum(rows * rows, axis=0, keepdims=True) * scale
        work[slot] = rows

    def scatter(slot, k):
        for c in range(TILE):
            held[pl.ds(near[slot, k, c], 1), :] = work[k % 2, pl.ds(c, 1), :]

    @pl.when(again[0, 0] == 0)
    def _():
        def sent(i, carry):
            for slot in range(2):
                group = i * 2 + slot
                fetch(group, slot).wait()
                for k in range(GROUP):
                    returned(group * GROUP + k + 1, (k + 1) % 2)
                    scatter(slot, k)
                fetch(group + 2, slot).start()
            return carry

        returned(0, 0)
        lax.fori_loop(0, GROUPS // 2, sent, 0)

    @pl.when(again[0, 0] != 0)
    def _():
        held[...] = jnp.zeros_like(held)

        def summed(t, carry):
            returned(t, 0)

            def add(c, inner):
                held[pl.ds(addr[t, c], 1), :] += work[0, pl.ds(c, 1), :]
                return inner

            lax.fori_loop(0, TILE, add, 0)
            return carry

        lax.fori_loop(0, TILES, summed, 0)

    fetch(0, 0).wait()
    fetch(1, 1).wait()
    left = lanes64((PB, 128))
    copies = []
    for m in range(PLANE):
        done[m] = jnp.where(left, held[pl.ds(m * 2 * PB, PB), :], held[pl.ds(m * 2 * PB + PB, PB), :])
        done[m, pl.ds(PB - 1, 1), :] = mark
        if m % 8 == 7:
            part = pl.ds(m - 7, 8)
            copies.append(pltpu.make_async_copy(done.at[part], out_ref.at[part], out_sem.at[m // 8]))
            copies[-1].start()
    for copy in copies:
        copy.wait()


def sum_kernel(in_ref, index_ref, out_ref, mark_ref, total):
    total[...] = jnp.zeros_like(total)
    at = (iota((ROWS, 8 * ZB), 0) + 1).astype(jnp.int16)

    def step(i, mark):
        rows, indices = [], []
        for n in range(4):
            z = i * 4 + n
            turned = jnp.transpose(in_ref[z])
            rows += [turned[:PROBES], turned[PROBES:]]
            indices.append(index_ref[pl.ds(z, 1), :])
            mark = jnp.maximum(mark, in_ref[z, pl.ds(ZB - 1, 1), :])
        index = jnp.concatenate(indices, axis=1)
        rows = jnp.where(index > 0.5, jnp.concatenate(rows, axis=1), 0.0)
        high = rows.astype(BF16).astype(F32)
        parts = jnp.concatenate([high, rows - high], axis=0).astype(BF16)
        total[...] += dot(parts, ones16(at == short(index)), 1, 1)
        return mark

    mark_ref[...] = lax.fori_loop(0, NZ // 4, step, jnp.zeros((1, 128), F32))
    out_ref[...] = total[pl.ds(0, PROBES), :] + total[pl.ds(PROBES, PROBES), :]


VMEM = pl.BlockSpec(memory_space=pltpu.VMEM)
SMEM = pl.BlockSpec(memory_space=pltpu.SMEM)
HBM = pl.BlockSpec(memory_space=pl.ANY)


def call(kernel, outs, ins, scratch=(), out_specs=None, cost=2_000_000, limit=24):
    shapes = [jax.ShapeDtypeStruct(*o) for o in outs]
    return pl.pallas_call(
        kernel,
        out_shape=shapes,
        in_specs=ins,
        out_specs=[VMEM] * len(shapes) if out_specs is None else out_specs,
        scratch_shapes=list(scratch),
        cost_estimate=pl.CostEstimate(flops=cost * 100, bytes_accessed=cost, transcendentals=0),
        compiler_params=pltpu.CompilerParams(vmem_limit_bytes=limit << 20),
    )


def packed(probes, dosages, weights, send_rows, tile_src, tile_gene):
    zdone, pdone = [pltpu.VMEM((NZ, ZB, 128), F32)], [pltpu.VMEM((PLANE, PB, 128), F32)]
    four = [pltpu.SemaphoreType.DMA((4,))]
    used, count = call(used_kernel, [((128, 128), F32)] * 2, [VMEM])(tile_src)
    asked = lax.all_to_all(used.reshape(PLANE, 4, 128), FLAT, 0, 0, tiled=True).reshape(128, 128)
    (met,) = call(meet_kernel, [((NZ, 8, 128), F32)], [VMEM])(asked)
    met = lax.all_to_all(met, "z", 0, 0, tiled=True).reshape(128, 128)
    value, parts = call(
        ready_kernel,
        [((128, 128), I32), ((2 * PROBES, ROWS), BF16)],
        [VMEM] * 2,
        [pltpu.VMEM((DEV, 128), I32)],
    )(send_rows[0].T, probes)
    asked, count, met = lax.optimization_barrier((asked, count, met))
    table, mark = call(table_kernel, [((128, 128), I32), ((1, 128), F32)], [VMEM])(asked)
    addr, again = call(
        place_kernel, [((TILES, TILE), I32), ((1, 1), I32)], [VMEM, VMEM], out_specs=[VMEM, SMEM]
    )(tile_src, count)
    block, index = call(
        send_kernel,
        [((NZ, ZB, 128), F32), ((NZ, 2 * ZB), F32)],
        [VMEM] * 3,
        [pltpu.VMEM((128, 128), I32)] * 2 + zdone + [pltpu.SemaphoreType.DMA((NZ // 2,))],
        out_specs=[HBM, VMEM],
    )(met, value, parts)
    block = lax.all_to_all(block, "z", 0, 0, tiled=True)
    buffers = [pltpu.VMEM((NZ * ZBUF, 128), F32), pltpu.VMEM((PLANE * PBUF, 128), F32)]
    (block,) = call(relay_kernel, [((PLANE, PB, 128), F32)], [SMEM, VMEM, VMEM], buffers + pdone + four, out_specs=[HBM])(
        table, mark, block
    )
    block = lax.all_to_all(block, FLAT, 0, 0, tiled=True)
    block, one, two = call(
        gene_kernel,
        [((PLANE, PB, 128), F32), ((GENES, 128), F32), ((GENES, 128), F32)],
        [SMEM] * 3 + [VMEM] * 4,
        [
            pltpu.VMEM((HOLD + 8, 128), F32),
            pltpu.VMEM((GENES, VT, 128), F32),
            pltpu.VMEM((GENES, VT, 128), BF16),
            pltpu.VMEM((2, TILE, 128), F32),
            pltpu.SMEM((2, GROUP, TILE), I32),
        ]
        + pdone
        + [pltpu.SemaphoreType.DMA((2,))]
        + four,
        out_specs=[HBM, VMEM, VMEM],
    )(addr, again, tile_gene, addr, block, dosages, weights.T)
    block = lax.all_to_all(block, FLAT, 0, 0, tiled=True)
    (block,) = call(
        back_kernel, [((NZ, ZB, 128), F32)], [SMEM, VMEM], buffers + zdone + four, out_specs=[HBM]
    )(table, block)
    block = lax.all_to_all(block, "z", 0, 0, tiled=True)
    projected, mark = call(
        sum_kernel,
        [((PROBES, ROWS), F32), ((1, 128), F32)],
        [VMEM] * 2,
        [pltpu.VMEM((2 * PROBES, ROWS), F32)],
    )(block, index)
    moments = jnp.stack([one[:, :PROBES], two[:, :PROBES]], axis=1)
    return projected, moments, mark[0, 0]


def exchange(rows):
    return lax.all_to_all(rows, ALL, 0, 0, tiled=True)


def whole(probes, dosages, weights, send_rows, tile_src, tile_gene):
    rows_sent = send_rows[0]
    high = lax.Precision.HIGHEST
    outgoing = probes.T[rows_sent].reshape(DEV, SLOTS * PROBES // 128, 128)
    incoming = exchange(outgoing).reshape(SRC, PROBES)
    fetched = jnp.concatenate([incoming, jnp.zeros((1, PROBES), F32)], axis=0)
    slab = fetched[tile_src]
    tile_scores = jnp.einsum("tcb,tvc->tbv", slab, dosages, precision=high, preferred_element_type=F32)
    member = (tile_gene[None, :] == jnp.arange(GENES, dtype=I32)[:, None]).astype(F32)
    scores = jnp.einsum("gt,tbv->gbv", member, tile_scores, precision=high) * weights[:, None, :]
    one = jnp.sum(scores * scores, axis=2) / VT
    weighted = jnp.einsum("gt,gbv->tbv", member, scores * weights[:, None, :], precision=high)
    returned = jnp.einsum("tbv,tvc->tcb", weighted, dosages, precision=high, preferred_element_type=F32)
    two = jnp.dot(member, jnp.sum(returned * returned, axis=1), precision=high) / TILE
    sums = jax.ops.segment_sum(returned.reshape(-1, PROBES), tile_src.reshape(-1), num_segments=SRC + 1)
    arrived = exchange(sums[:SRC].reshape(DEV, SLOTS * PROBES // 128, 128))
    projected = jax.ops.segment_sum(
        arrived.reshape(SRC, PROBES), rows_sent.reshape(-1), num_segments=ROWS
    ).T
    return projected, jnp.stack([one, two], axis=1)


def shards(*args):
    projected, moments, mark = packed(*args)
    projected, moments = lax.cond(mark > 0.5, lambda: whole(*args), lambda: (projected, moments))
    return projected, moments.transpose(1, 2, 0)


def solution(mesh):
    fine = Mesh(mesh.devices.reshape(NY, NZ, NC, NX), ALL)
    placed = (P(None, ALL), P(ALL, None, None), P(ALL, None), P(ALL, None, None), P(ALL, None), P(ALL))
    return jax.shard_map(
        shards,
        mesh=fine,
        in_specs=placed,
        out_specs=(P(None, ALL), P(None, None, ALL)),
        check_vma=False,
    )
```

```python
import jax
import jax.numpy as jnp
from jax import lax
from jax.experimental import pallas as pl
from jax.experimental.pallas import tpu as pltpu
from jax.sharding import Mesh, PartitionSpec as P

NY, NZ, NC, NX = 4, 16, 2, 4
PLANE = NY * NC * NX
DEV = NY * NZ * NC * NX
SLOTS = 24
LANE = 32
SRC = DEV * SLOTS
TILES = 40
TILE = 128
VT = 128
GENES = 20
GROUP = 4
GROUPS = TILES // GROUP
PROBES = 64
ROWS = 1024
ZB = 128
ZCAP = 2 * (ZB - 1)
PB = 96
PCAP = 2 * (PB - 1)
ZBUF = 280
PBUF = 216
HOLD = PLANE * 2 * PB
F32 = jnp.float32
BF16 = jnp.bfloat16
I32 = jnp.int32
ALL = ("y", "z", "c", "x")
FLAT = ("y", "c", "x")


def iota(shape, dim):
    return lax.broadcasted_iota(I32, shape, dim)


def dot(a, b, ca=1, cb=0, **kw):
    return lax.dot_general(a, b, (((ca,), (cb,)), ((), ())), preferred_element_type=F32, **kw)


def ones_where(mask):
    return jnp.where(mask, 1.0, 0.0).astype(BF16)


def ones16(mask):
    return jnp.where(mask, jnp.ones((), BF16), jnp.zeros((), BF16))


def short(v):
    return v.astype(I32).astype(jnp.int16)


def lanes64(shape):
    return iota(shape, 1) < PROBES


def split(v):
    high = v.astype(BF16)
    return jnp.concatenate([high, (v - high.astype(F32)).astype(BF16)], axis=0)


def both(block):
    turned = pltpu.roll(block, PROBES, 1)
    left = lanes64(block.shape)
    return jnp.where(left, block, turned), jnp.where(left, turned, block)


def source_parts(ref, t, n):
    highs, lows, empties = [], [], []
    for i in range(n):
        p = ref[pl.ds(t * n + i, 1), :]
        o = (p * 43691) >> 20
        highs.append(((o >> 7) * (NC * NX) + (o & 7)) * 4 + ((o >> 5) & 3))
        lows.append(((o >> 3) & 3) * LANE + p - o * SLOTS)
        empties.append(p >= SRC)
    return highs, lows, empties


def one_hots(rows):
    return jnp.concatenate([ones16(iota((128, 128), 0).astype(jnp.int16) == r.astype(jnp.int16)) for r in rows], axis=1)


def used_kernel(src_ref, used_ref, count_ref):
    count_ref[...] = jnp.zeros_like(count_ref)

    def step(t, carry):
        highs, lows, _ = source_parts(src_ref, t, 8)
        count_ref[...] += dot(one_hots(highs), one_hots(lows), 1, 1)
        return carry

    lax.fori_loop(0, TILES // 8, step, 0)
    used_ref[...] = jnp.minimum(count_ref[...], 1.0)


def place_kernel(src_ref, count_ref, addr_ref, again_ref):
    count = count_ref[...]
    again_ref[0, 0] = jnp.where(jnp.max(count) > 1.5, 1, 0)
    used = ones_where(count > 0.5)
    row, col = iota((128, 128), 0), iota((128, 128), 1)
    before = dot(used, ones_where(row < col))
    number = dot(used, jnp.ones((128, 128), BF16)).astype(BF16)
    earlier = ones_where(((row >> 2) == (col >> 2)) & (col < row))
    rank = jnp.minimum((dot(earlier, number) + before).astype(I32), PCAP)
    place = (row >> 2) * (2 * PB) + rank + jnp.where(rank >= PB - 1, 1, 0)
    turned = jnp.transpose(place)
    high = turned >> 6
    table = jnp.concatenate([high, turned - (high << 6)], axis=0).astype(F32).astype(BF16)

    def step(t, carry):
        highs, lows, empties = source_parts(src_ref, t, 8)
        found = dot(table, one_hots(highs))
        for i in range(8):
            part = found[:, i * 128 : (i + 1) * 128]
            value = part[:128] * 64.0 + part[128:]
            value = jnp.sum(jnp.where(row == lows[i], value, 0.0), axis=0, keepdims=True)
            addr_ref[pl.ds(t * 8 + i, 1), :] = jnp.where(empties[i], HOLD, value.astype(I32))
        return carry

    lax.fori_loop(0, TILES // 8, step, 0)


def meet_kernel(in_ref, out_ref):
    block = iota((8, 128), 1) >> 5
    for high in range(4):
        parts = [in_ref[pl.ds(x * 4 + high, 8, stride=16), :] for x in range(NX)]
        for low in range(4):
            turned = [pltpu.roll(parts[x], ((x - low) * LANE) % 128, 1) for x in range(NX)]
            result = turned[0]
            for x in range(1, NX):
                result = jnp.where(block == x, turned[x], result)
            out_ref[high * 4 + low] = result


def table_kernel(in_ref, table_ref, mark_ref):
    used = ones_where(in_ref[...] > 0.5)
    row, col = iota((128, 128), 0), iota((128, 128), 1)
    segment = dot(used, ones_where((row >> 5) == (col >> 5)))
    whole_row = dot(used, jnp.ones((128, 128), BF16))
    before = dot(used, ones_where((row >> 5) < (col >> 5)))
    owner = dot(ones_where(((row & 3) == (col & 3)) & (col < row)), segment.astype(BF16))
    holder = before + dot(ones_where(((row >> 2) == (col >> 2)) & (col < row)), whole_row.astype(BF16))
    over = jnp.maximum(
        jnp.where(owner + segment > ZCAP, 1.0, 0.0), jnp.where(holder + segment > PCAP, 1.0, 0.0)
    )
    mark_ref[...] = jnp.broadcast_to(jnp.max(over), (1, 128))
    owner = jnp.minimum(owner, float(ZCAP)).astype(I32) + ((row & 3) * 4 + (col >> 5)) * ZBUF
    holder = jnp.minimum(holder, float(PCAP + 1)).astype(I32) + (row >> 2) * PBUF
    table_ref[...] = jnp.where((col & 1) == 0, owner, holder)


def ready_kernel(rows_ref, probes_ref, value_ref, parts_ref, turned_ref):
    col = iota((128, 128), 1)
    high = probes_ref[...].astype(BF16).astype(F32)
    parts_ref[...] = jnp.concatenate([high, probes_ref[...] - high], axis=0).astype(BF16)
    turned_ref[...] = jnp.zeros_like(turned_ref)
    for k in range(DEV // 128):
        turned_ref[pl.ds(k * 128, 128), pl.ds(0, SLOTS)] = jnp.transpose(rows_ref[:, pl.ds(k * 128, 128)])
    value = turned_ref[pl.ds(0, 128, stride=NX), :]
    for x in range(1, NX):
        turned = pltpu.roll(turned_ref[pl.ds(x, 128, stride=NX), :], x * LANE, 1)
        value = jnp.where((col >> 5) == x, turned, value)
    value_ref[...] = value + 1


def send_kernel(used_ref, value_ref, parts_ref, out_ref, index_ref, high_ref, low_ref, done, sem):
    used = used_ref[...]
    flag = ones_where(used > 0.5)
    row, col = iota((128, 128), 0), iota((128, 128), 1)
    number = dot(flag, jnp.ones((128, 128), BF16))
    start = dot(ones_where(((row >> 3) == (col >> 3)) & (col < row)), number.astype(BF16))
    place = (start + dot(flag, ones_where(row < col))).astype(I32)
    place = place + jnp.where(place >= ZB - 1, 1, 0)
    high_ref[...] = jnp.where(used > 0.5, place >> 7, -1)
    low_ref[...] = place & (ZB - 1)
    which = iota((8, 128), 0)
    at = iota((ZB, 128), 0).astype(jnp.int16)
    subject = (iota((ROWS, 4 * ZB), 0) + 1).astype(jnp.int16)

    def list_of(z):
        values, places = [], []
        for y in range(NY):
            for c in range(NC):
                i = z * (NY * NC) + y * NC + c
                value = value_ref[pl.ds(y * (NZ * NC) + z * NC + c, 1), :]
                digit = jnp.where(which < 2, value >> 5, value & 31)
                match = ((which & 1) == high_ref[pl.ds(i, 1), :]) & (which < 4)
                values.append(jnp.where(match, digit, 0).astype(F32).astype(BF16))
                places.append(ones16(at == low_ref[pl.ds(i, 1), :].astype(jnp.int16)))
        listed = dot(jnp.concatenate(values, axis=1), jnp.concatenate(places, axis=1), 1, 1)
        index = listed[:2] * 32.0 + listed[2:4]
        index = jnp.concatenate([index[:1], index[1:]], axis=1)
        index_ref[pl.ds(z, 1), :] = index
        return index

    def lists_of(i):
        return jnp.concatenate([list_of(2 * i), list_of(2 * i + 1)], axis=1)

    def step(i, index):
        later = lists_of(jnp.minimum(i + 1, NZ // 2 - 1))
        rows = dot(parts_ref[...], ones16(subject == short(index)))
        rows = rows[:PROBES] + rows[PROBES:]
        for n in range(2):
            left, right = rows[:, 2 * n * ZB : (2 * n + 1) * ZB], rows[:, (2 * n + 1) * ZB : (2 * n + 2) * ZB]
            done[2 * i + n] = jnp.transpose(jnp.concatenate([left, right], axis=0))
        leave(i).start()
        return later

    def leave(i):
        part = pl.ds(2 * i, 2)
        return pltpu.make_async_copy(done.at[part], out_ref.at[part], sem.at[i])

    lax.fori_loop(0, NZ // 2, step, lists_of(0))
    for i in range(NZ // 2):
        leave(i).wait()


def relay_kernel(table, mark_ref, in_ref, out_ref, zbuf, pbuf, done, sem):
    for z in range(NZ):
        left, right = both(in_ref[z])
        zbuf[pl.ds(z * ZBUF, ZB), :] = left
        zbuf[pl.ds(z * ZBUF + ZB - 1, ZB), :] = right
    left = lanes64((PB, 128))
    copies = []
    for r in range(PLANE):
        for z in range(NZ):
            row, col = r * 4 + z // 4, (z % 4) * LANE
            pbuf[pl.ds(table[row, col + 1], SLOTS), :] = zbuf[pl.ds(table[row, col], SLOTS), :]
        done[r] = jnp.where(left, pbuf[pl.ds(r * PBUF, PB), :], pbuf[pl.ds(r * PBUF + PB - 1, PB), :])
        done[r, pl.ds(PB - 1, 1), :] = mark_ref[...]
        if r % 8 == 7:
            part = pl.ds(r - 7, 8)
            copies.append(pltpu.make_async_copy(done.at[part], out_ref.at[part], sem.at[r // 8]))
            copies[-1].start()
    for copy in copies:
        copy.wait()


def back_kernel(table, in_ref, out_ref, zbuf, pbuf, done, sem):
    mark = jnp.zeros((1, 128), F32)
    for r in range(PLANE):
        left, right = both(in_ref[r])
        pbuf[pl.ds(r * PBUF, PB), :] = left
        pbuf[pl.ds(r * PBUF + PB - 1, PB), :] = right
        mark = jnp.maximum(mark, in_ref[r, pl.ds(PB - 1, 1), :])
    left = lanes64((ZB, 128))
    copies = []
    for z in range(NZ):
        for r in range(PLANE):
            row, col = r * 4 + z // 4, (z % 4) * LANE
            zbuf[pl.ds(table[row, col], SLOTS), :] = pbuf[pl.ds(table[row, col + 1], SLOTS), :]
        done[z] = jnp.where(left, zbuf[pl.ds(z * ZBUF, ZB), :], zbuf[pl.ds(z * ZBUF + ZB - 1, ZB), :])
        done[z, pl.ds(ZB - 1, 1), :] = mark
        if z % 4 == 3:
            part = pl.ds(z - 3, 4)
            copies.append(pltpu.make_async_copy(done.at[part], out_ref.at[part], sem.at[z // 4]))
            copies[-1].start()
    for copy in copies:
        copy.wait()


def gene_kernel(
    addr,
    again,
    gene,
    addr_ref,
    in_ref,
    dose_ref,
    weight_ref,
    out_ref,
    one_ref,
    two_ref,
    held,
    total,
    weighted,
    work,
    near,
    done,
    sem,
    out_sem,
):
    def fetch(group, slot):
        return pltpu.make_async_copy(
            addr_ref.at[pl.ds(lax.rem(group, GROUPS) * GROUP, GROUP), :], near.at[slot], sem.at[slot]
        )

    fetch(0, 0).start()
    fetch(1, 1).start()
    mark = jnp.zeros((1, 128), F32)
    for m in range(PLANE):
        left, right = both(in_ref[m])
        held[pl.ds(m * 2 * PB, PB), :] = left
        held[pl.ds(m * 2 * PB + PB, PB), :] = right
        mark = jnp.maximum(mark, in_ref[m, pl.ds(PB - 1, 1), :])
    held[pl.ds(HOLD, 8), :] = jnp.zeros((8, 128), F32)
    total[...] = jnp.zeros_like(total)
    two_ref[...] = jnp.zeros_like(two_ref)

    def gather(slot, k):
        for c in range(TILE):
            work[k % 2, pl.ds(c, 1), :] = held[pl.ds(near[slot, k, c], 1), :]

    def score(t, k):
        dose = dose_ref[t]
        total[gene[t]] += dot(jnp.concatenate([dose, dose], axis=1), split(work[k % 2]))

    def scored(i, carry):
        for slot in range(2):
            group = i * 2 + slot
            fetch(group, slot).wait()
            for k in range(GROUP):
                gather(slot, k)
                score(jnp.maximum(group * GROUP + k - 1, 0), k + 1)
            fetch(group + 2, slot).start()
        return carry

    work[1] = jnp.zeros((TILE, 128), F32)
    lax.fori_loop(0, GROUPS // 2, scored, 0)
    score(TILES - 1, 1)
    for k in range(GENES):
        weight = weight_ref[k]
        scores = total[k] * weight
        one_ref[pl.ds(k, 1), :] = jnp.sum(scores * scores, axis=0, keepdims=True) * (1.0 / VT)
        weighted[k] = split(scores * weight)

    def returned(t, slot):
        scale = jnp.where(t < TILES, 1.0 / TILE, 0.0)
        t = jnp.minimum(t, TILES - 1)
        dose = dose_ref[t]
        rows = dot(jnp.concatenate([dose, dose], axis=0), weighted[gene[t]], 0, 0)
        two_ref[pl.ds(gene[t], 1), :] += jnp.sum(rows * rows, axis=0, keepdims=True) * scale
        work[slot] = rows

    def scatter(slot, k):
        for c in range(TILE):
            held[pl.ds(near[slot, k, c], 1), :] = work[k % 2, pl.ds(c, 1), :]

    @pl.when(again[0, 0] == 0)
    def _():
        def sent(i, carry):
            for slot in range(2):
                group = i * 2 + slot
                fetch(group, slot).wait()
                for k in range(GROUP):
                    returned(group * GROUP + k + 1, (k + 1) % 2)
                    scatter(slot, k)
                fetch(group + 2, slot).start()
            return carry

        returned(0, 0)
        lax.fori_loop(0, GROUPS // 2, sent, 0)

    @pl.when(again[0, 0] != 0)
    def _():
        held[...] = jnp.zeros_like(held)

        def summed(t, carry):
            returned(t, 0)

            def add(c, inner):
                held[pl.ds(addr[t, c], 1), :] += work[0, pl.ds(c, 1), :]
                return inner

            lax.fori_loop(0, TILE, add, 0)
            return carry

        lax.fori_loop(0, TILES, summed, 0)

    fetch(0, 0).wait()
    fetch(1, 1).wait()
    left = lanes64((PB, 128))
    copies = []
    for m in range(PLANE):
        done[m] = jnp.where(left, held[pl.ds(m * 2 * PB, PB), :], held[pl.ds(m * 2 * PB + PB, PB), :])
        done[m, pl.ds(PB - 1, 1), :] = mark
        if m % 8 == 7:
            part = pl.ds(m - 7, 8)
            copies.append(pltpu.make_async_copy(done.at[part], out_ref.at[part], out_sem.at[m // 8]))
            copies[-1].start()
    for copy in copies:
        copy.wait()


def sum_kernel(in_ref, index_ref, out_ref, mark_ref, total):
    total[...] = jnp.zeros_like(total)
    at = (iota((ROWS, 8 * ZB), 0) + 1).astype(jnp.int16)

    def step(i, mark):
        rows, indices = [], []
        for n in range(4):
            z = i * 4 + n
            turned = jnp.transpose(in_ref[z])
            rows += [turned[:PROBES], turned[PROBES:]]
            indices.append(index_ref[pl.ds(z, 1), :])
            mark = jnp.maximum(mark, in_ref[z, pl.ds(ZB - 1, 1), :])
        index = jnp.concatenate(indices, axis=1)
        rows = jnp.where(index > 0.5, jnp.concatenate(rows, axis=1), 0.0)
        high = rows.astype(BF16).astype(F32)
        parts = jnp.concatenate([high, rows - high], axis=0).astype(BF16)
        total[...] += dot(parts, ones16(at == short(index)), 1, 1)
        return mark

    mark_ref[...] = lax.fori_loop(0, NZ // 4, step, jnp.zeros((1, 128), F32))
    out_ref[...] = total[pl.ds(0, PROBES), :] + total[pl.ds(PROBES, PROBES), :]


VMEM = pl.BlockSpec(memory_space=pltpu.VMEM)
SMEM = pl.BlockSpec(memory_space=pltpu.SMEM)
HBM = pl.BlockSpec(memory_space=pl.ANY)


def call(kernel, outs, ins, scratch=(), out_specs=None, cost=2_000_000, limit=24):
    shapes = [jax.ShapeDtypeStruct(*o) for o in outs]
    return pl.pallas_call(
        kernel,
        out_shape=shapes,
        in_specs=ins,
        out_specs=[VMEM] * len(shapes) if out_specs is None else out_specs,
        scratch_shapes=list(scratch),
        cost_estimate=pl.CostEstimate(flops=cost * 100, bytes_accessed=cost, transcendentals=0),
        compiler_params=pltpu.CompilerParams(vmem_limit_bytes=limit << 20),
    )


def packed(probes, dosages, weights, send_rows, tile_src, tile_gene):
    zdone, pdone = [pltpu.VMEM((NZ, ZB, 128), F32)], [pltpu.VMEM((PLANE, PB, 128), F32)]
    four = [pltpu.SemaphoreType.DMA((4,))]
    used, count = call(used_kernel, [((128, 128), F32)] * 2, [VMEM])(tile_src)
    asked = lax.all_to_all(used.reshape(PLANE, 4, 128), FLAT, 0, 0, tiled=True).reshape(128, 128)
    (met,) = call(meet_kernel, [((NZ, 8, 128), F32)], [VMEM])(asked)
    met = lax.all_to_all(met, "z", 0, 0, tiled=True).reshape(128, 128)
    value, parts = call(
        ready_kernel,
        [((128, 128), I32), ((2 * PROBES, ROWS), BF16)],
        [VMEM] * 2,
        [pltpu.VMEM((DEV, 128), I32)],
    )(send_rows[0].T, probes)
    asked, count, met, spread = lax.optimization_barrier((asked, count, met, weights))
    spread = jnp.broadcast_to(spread[:, :, None], (GENES, VT, 128))
    table, mark = call(table_kernel, [((128, 128), I32), ((1, 128), F32)], [VMEM])(asked)
    addr, again = call(
        place_kernel, [((TILES, TILE), I32), ((1, 1), I32)], [VMEM, VMEM], out_specs=[VMEM, SMEM]
    )(tile_src, count)
    block, index = call(
        send_kernel,
        [((NZ, ZB, 128), F32), ((NZ, 2 * ZB), F32)],
        [VMEM] * 3,
        [pltpu.VMEM((128, 128), I32)] * 2 + zdone + [pltpu.SemaphoreType.DMA((NZ // 2,))],
        out_specs=[HBM, VMEM],
    )(met, value, parts)
    block = lax.all_to_all(block, "z", 0, 0, tiled=True)
    buffers = [pltpu.VMEM((NZ * ZBUF, 128), F32), pltpu.VMEM((PLANE * PBUF, 128), F32)]
    (block,) = call(relay_kernel, [((PLANE, PB, 128), F32)], [SMEM, VMEM, VMEM], buffers + pdone + four, out_specs=[HBM])(
        table, mark, block
    )
    block = lax.all_to_all(block, FLAT, 0, 0, tiled=True)
    block, one, two = call(
        gene_kernel,
        [((PLANE, PB, 128), F32), ((GENES, 128), F32), ((GENES, 128), F32)],
        [SMEM] * 3 + [VMEM] * 4,
        [
            pltpu.VMEM((HOLD + 8, 128), F32),
            pltpu.VMEM((GENES, VT, 128), F32),
            pltpu.VMEM((GENES, 2 * VT, 128), BF16),
            pltpu.VMEM((2, TILE, 128), F32),
            pltpu.SMEM((2, GROUP, TILE), I32),
        ]
        + pdone
        + [pltpu.SemaphoreType.DMA((2,))]
        + four,
        out_specs=[HBM, VMEM, VMEM],
    )(addr, again, tile_gene, addr, block, dosages, spread)
    block = lax.all_to_all(block, FLAT, 0, 0, tiled=True)
    (block,) = call(
        back_kernel, [((NZ, ZB, 128), F32)], [SMEM, VMEM], buffers + zdone + four, out_specs=[HBM]
    )(table, block)
    block = lax.all_to_all(block, "z", 0, 0, tiled=True)
    projected, mark = call(
        sum_kernel,
        [((PROBES, ROWS), F32), ((1, 128), F32)],
        [VMEM] * 2,
        [pltpu.VMEM((2 * PROBES, ROWS), F32)],
    )(block, index)
    moments = jnp.stack([one[:, :PROBES], two[:, :PROBES]], axis=1)
    return projected, moments, mark[0, 0]


def exchange(rows):
    return lax.all_to_all(rows, ALL, 0, 0, tiled=True)


def whole(probes, dosages, weights, send_rows, tile_src, tile_gene):
    rows_sent = send_rows[0]
    high = lax.Precision.HIGHEST
    outgoing = probes.T[rows_sent].reshape(DEV, SLOTS * PROBES // 128, 128)
    incoming = exchange(outgoing).reshape(SRC, PROBES)
    fetched = jnp.concatenate([incoming, jnp.zeros((1, PROBES), F32)], axis=0)
    slab = fetched[tile_src]
    tile_scores = jnp.einsum("tcb,tvc->tbv", slab, dosages, precision=high, preferred_element_type=F32)
    member = (tile_gene[None, :] == jnp.arange(GENES, dtype=I32)[:, None]).astype(F32)
    scores = jnp.einsum("gt,tbv->gbv", member, tile_scores, precision=high) * weights[:, None, :]
    one = jnp.sum(scores * scores, axis=2) / VT
    weighted = jnp.einsum("gt,gbv->tbv", member, scores * weights[:, None, :], precision=high)
    returned = jnp.einsum("tbv,tvc->tcb", weighted, dosages, precision=high, preferred_element_type=F32)
    two = jnp.dot(member, jnp.sum(returned * returned, axis=1), precision=high) / TILE
    sums = jax.ops.segment_sum(returned.reshape(-1, PROBES), tile_src.reshape(-1), num_segments=SRC + 1)
    arrived = exchange(sums[:SRC].reshape(DEV, SLOTS * PROBES // 128, 128))
    projected = jax.ops.segment_sum(
        arrived.reshape(SRC, PROBES), rows_sent.reshape(-1), num_segments=ROWS
    ).T
    return projected, jnp.stack([one, two], axis=1)


def shards(*args):
    projected, moments, mark = packed(*args)
    projected, moments = lax.cond(mark > 0.5, lambda: whole(*args), lambda: (projected, moments))
    return projected, moments.transpose(1, 2, 0)


def solution(mesh):
    fine = Mesh(mesh.devices.reshape(NY, NZ, NC, NX), ALL)
    placed = (P(None, ALL), P(ALL, None, None), P(ALL, None), P(ALL, None, None), P(ALL, None), P(ALL))
    return jax.shard_map(
        shards,
        mesh=fine,
        in_specs=placed,
        out_specs=(P(None, ALL), P(None, None, ALL)),
        check_vma=False,
    )
```

```python
import jax
import jax.numpy as jnp
from jax import lax
from jax.experimental import pallas as pl
from jax.experimental.pallas import tpu as pltpu
from jax.sharding import Mesh, PartitionSpec as P

NY, NZ, NC, NX = 4, 16, 2, 4
PLANE = NY * NC * NX
DEV = NY * NZ * NC * NX
SLOTS = 24
LANE = 32
SRC = DEV * SLOTS
TILES = 40
TILE = 128
VT = 128
GENES = 20
GROUP = 4
GROUPS = TILES // GROUP
PROBES = 64
ROWS = 1024
ZB = 128
ZCAP = 2 * (ZB - 1)
PB = 96
PCAP = 2 * (PB - 1)
ZBUF = 280
PBUF = 216
HOLD = PLANE * 2 * PB
F32 = jnp.float32
BF16 = jnp.bfloat16
I32 = jnp.int32
ALL = ("y", "z", "c", "x")
FLAT = ("y", "c", "x")


def iota(shape, dim):
    return lax.broadcasted_iota(I32, shape, dim)


def dot(a, b, ca=1, cb=0, **kw):
    return lax.dot_general(a, b, (((ca,), (cb,)), ((), ())), preferred_element_type=F32, **kw)


def ones_where(mask):
    return jnp.where(mask, 1.0, 0.0).astype(BF16)


def ones16(mask):
    return jnp.where(mask, jnp.ones((), BF16), jnp.zeros((), BF16))


def short(v):
    return v.astype(I32).astype(jnp.int16)


def lanes64(shape):
    return iota(shape, 1) < PROBES


def split(v):
    high = v.astype(BF16)
    return jnp.concatenate([high, (v - high.astype(F32)).astype(BF16)], axis=0)


def both(block):
    turned = pltpu.roll(block, PROBES, 1)
    left = lanes64(block.shape)
    return jnp.where(left, block, turned), jnp.where(left, turned, block)


def source_parts(ref, t, n):
    highs, lows, empties = [], [], []
    for i in range(n):
        p = ref[pl.ds(t * n + i, 1), :]
        o = (p * 43691) >> 20
        highs.append(((o >> 7) * (NC * NX) + (o & 7)) * 4 + ((o >> 5) & 3))
        lows.append(((o >> 3) & 3) * LANE + p - o * SLOTS)
        empties.append(p >= SRC)
    return highs, lows, empties


def one_hots(rows):
    return jnp.concatenate([ones16(iota((128, 128), 0).astype(jnp.int16) == r.astype(jnp.int16)) for r in rows], axis=1)


def used_kernel(src_ref, used_ref, count_ref):
    count_ref[...] = jnp.zeros_like(count_ref)

    def step(t, carry):
        highs, lows, _ = source_parts(src_ref, t, 8)
        count_ref[...] += dot(one_hots(highs), one_hots(lows), 1, 1)
        return carry

    lax.fori_loop(0, TILES // 8, step, 0)
    used_ref[...] = jnp.minimum(count_ref[...], 1.0)


def place_kernel(src_ref, count_ref, addr_ref, again_ref):
    count = count_ref[...]
    again_ref[0, 0] = jnp.where(jnp.max(count) > 1.5, 1, 0)
    used = ones_where(count > 0.5)
    row, col = iota((128, 128), 0), iota((128, 128), 1)
    before = dot(used, ones_where(row < col))
    number = dot(used, jnp.ones((128, 128), BF16)).astype(BF16)
    earlier = ones_where(((row >> 2) == (col >> 2)) & (col < row))
    rank = jnp.minimum((dot(earlier, number) + before).astype(I32), PCAP)
    place = (row >> 2) * (2 * PB) + rank + jnp.where(rank >= PB - 1, 1, 0)
    turned = jnp.transpose(place)
    high = turned >> 6
    table = jnp.concatenate([high, turned - (high << 6)], axis=0).astype(F32).astype(BF16)

    def step(t, carry):
        highs, lows, empties = source_parts(src_ref, t, 8)
        found = dot(table, one_hots(highs))
        for i in range(8):
            part = found[:, i * 128 : (i + 1) * 128]
            value = part[:128] * 64.0 + part[128:]
            value = jnp.sum(jnp.where(row == lows[i], value, 0.0), axis=0, keepdims=True)
            addr_ref[pl.ds(t * 8 + i, 1), :] = jnp.where(empties[i], HOLD, value.astype(I32))
        return carry

    lax.fori_loop(0, TILES // 8, step, 0)


def meet_kernel(in_ref, out_ref):
    block = iota((8, 128), 1) >> 5
    for high in range(4):
        parts = [in_ref[pl.ds(x * 4 + high, 8, stride=16), :] for x in range(NX)]
        for low in range(4):
            turned = [pltpu.roll(parts[x], ((x - low) * LANE) % 128, 1) for x in range(NX)]
            result = turned[0]
            for x in range(1, NX):
                result = jnp.where(block == x, turned[x], result)
            out_ref[high * 4 + low] = result


def table_kernel(in_ref, weight_ref, table_ref, mark_ref, spread_ref):
    used = ones_where(in_ref[...] > 0.5)
    row, col = iota((128, 128), 0), iota((128, 128), 1)
    segment = dot(used, ones_where((row >> 5) == (col >> 5)))
    whole_row = dot(used, jnp.ones((128, 128), BF16))
    before = dot(used, ones_where((row >> 5) < (col >> 5)))
    owner = dot(ones_where(((row & 3) == (col & 3)) & (col < row)), segment.astype(BF16))
    holder = before + dot(ones_where(((row >> 2) == (col >> 2)) & (col < row)), whole_row.astype(BF16))
    over = jnp.maximum(
        jnp.where(owner + segment > ZCAP, 1.0, 0.0), jnp.where(holder + segment > PCAP, 1.0, 0.0)
    )
    mark_ref[...] = jnp.broadcast_to(jnp.max(over), (1, 128))
    owner = jnp.minimum(owner, float(ZCAP)).astype(I32) + ((row & 3) * 4 + (col >> 5)) * ZBUF
    holder = jnp.minimum(holder, float(PCAP + 1)).astype(I32) + (row >> 2) * PBUF
    table_ref[...] = jnp.where((col & 1) == 0, owner, holder)
    for k in range(GENES):
        spread_ref[k] = jnp.transpose(jnp.broadcast_to(weight_ref[pl.ds(k, 1), :], (128, VT)))


def ready_kernel(rows_ref, probes_ref, value_ref, parts_ref, turned_ref):
    col = iota((128, 128), 1)
    high = probes_ref[...].astype(BF16).astype(F32)
    parts_ref[...] = jnp.concatenate([high, probes_ref[...] - high], axis=0).astype(BF16)
    turned_ref[...] = jnp.zeros_like(turned_ref)
    for k in range(DEV // 128):
        turned_ref[pl.ds(k * 128, 128), pl.ds(0, SLOTS)] = jnp.transpose(rows_ref[:, pl.ds(k * 128, 128)])
    value = turned_ref[pl.ds(0, 128, stride=NX), :]
    for x in range(1, NX):
        turned = pltpu.roll(turned_ref[pl.ds(x, 128, stride=NX), :], x * LANE, 1)
        value = jnp.where((col >> 5) == x, turned, value)
    value_ref[...] = value + 1


def send_kernel(used_ref, value_ref, parts_ref, out_ref, index_ref, high_ref, low_ref, done, sem):
    used = used_ref[...]
    flag = ones_where(used > 0.5)
    row, col = iota((128, 128), 0), iota((128, 128), 1)
    number = dot(flag, jnp.ones((128, 128), BF16))
    start = dot(ones_where(((row >> 3) == (col >> 3)) & (col < row)), number.astype(BF16))
    place = (start + dot(flag, ones_where(row < col))).astype(I32)
    place = place + jnp.where(place >= ZB - 1, 1, 0)
    high_ref[...] = jnp.where(used > 0.5, place >> 7, -1)
    low_ref[...] = place & (ZB - 1)
    which = iota((8, 128), 0)
    at = iota((ZB, 128), 0).astype(jnp.int16)
    subject = (iota((ROWS, 4 * ZB), 0) + 1).astype(jnp.int16)

    def list_of(z):
        values, places = [], []
        for y in range(NY):
            for c in range(NC):
                i = z * (NY * NC) + y * NC + c
                value = value_ref[pl.ds(y * (NZ * NC) + z * NC + c, 1), :]
                digit = jnp.where(which < 2, value >> 5, value & 31)
                match = ((which & 1) == high_ref[pl.ds(i, 1), :]) & (which < 4)
                values.append(jnp.where(match, digit, 0).astype(F32).astype(BF16))
                places.append(ones16(at == low_ref[pl.ds(i, 1), :].astype(jnp.int16)))
        listed = dot(jnp.concatenate(values, axis=1), jnp.concatenate(places, axis=1), 1, 1)
        index = listed[:2] * 32.0 + listed[2:4]
        index = jnp.concatenate([index[:1], index[1:]], axis=1)
        index_ref[pl.ds(z, 1), :] = index
        return index

    def lists_of(i):
        return jnp.concatenate([list_of(2 * i), list_of(2 * i + 1)], axis=1)

    def step(i, index):
        later = lists_of(jnp.minimum(i + 1, NZ // 2 - 1))
        rows = dot(parts_ref[...], ones16(subject == short(index)))
        rows = rows[:PROBES] + rows[PROBES:]
        for n in range(2):
            left, right = rows[:, 2 * n * ZB : (2 * n + 1) * ZB], rows[:, (2 * n + 1) * ZB : (2 * n + 2) * ZB]
            done[2 * i + n] = jnp.transpose(jnp.concatenate([left, right], axis=0))
        leave(i).start()
        return later

    def leave(i):
        part = pl.ds(2 * i, 2)
        return pltpu.make_async_copy(done.at[part], out_ref.at[part], sem.at[i])

    lax.fori_loop(0, NZ // 2, step, lists_of(0))
    for i in range(NZ // 2):
        leave(i).wait()


def relay_kernel(table, mark_ref, in_ref, out_ref, zbuf, pbuf, done, sem):
    for z in range(NZ):
        left, right = both(in_ref[z])
        zbuf[pl.ds(z * ZBUF, ZB), :] = left
        zbuf[pl.ds(z * ZBUF + ZB - 1, ZB), :] = right
    left = lanes64((PB, 128))
    copies = []
    for r in range(PLANE):
        for z in range(NZ):
            row, col = r * 4 + z // 4, (z % 4) * LANE
            pbuf[pl.ds(table[row, col + 1], SLOTS), :] = zbuf[pl.ds(table[row, col], SLOTS), :]
        done[r] = jnp.where(left, pbuf[pl.ds(r * PBUF, PB), :], pbuf[pl.ds(r * PBUF + PB - 1, PB), :])
        done[r, pl.ds(PB - 1, 1), :] = mark_ref[...]
        if r % 8 == 7:
            part = pl.ds(r - 7, 8)
            copies.append(pltpu.make_async_copy(done.at[part], out_ref.at[part], sem.at[r // 8]))
            copies[-1].start()
    for copy in copies:
        copy.wait()


def back_kernel(table, in_ref, out_ref, zbuf, pbuf, done, sem):
    mark = jnp.zeros((1, 128), F32)
    for r in range(PLANE):
        left, right = both(in_ref[r])
        pbuf[pl.ds(r * PBUF, PB), :] = left
        pbuf[pl.ds(r * PBUF + PB - 1, PB), :] = right
        mark = jnp.maximum(mark, in_ref[r, pl.ds(PB - 1, 1), :])
    left = lanes64((ZB, 128))
    copies = []
    for z in range(NZ):
        for r in range(PLANE):
            row, col = r * 4 + z // 4, (z % 4) * LANE
            zbuf[pl.ds(table[row, col], SLOTS), :] = pbuf[pl.ds(table[row, col + 1], SLOTS), :]
        done[z] = jnp.where(left, zbuf[pl.ds(z * ZBUF, ZB), :], zbuf[pl.ds(z * ZBUF + ZB - 1, ZB), :])
        done[z, pl.ds(ZB - 1, 1), :] = mark
        if z % 4 == 3:
            part = pl.ds(z - 3, 4)
            copies.append(pltpu.make_async_copy(done.at[part], out_ref.at[part], sem.at[z // 4]))
            copies[-1].start()
    for copy in copies:
        copy.wait()


def gene_kernel(
    addr,
    again,
    gene,
    addr_ref,
    in_ref,
    dose_ref,
    weight_ref,
    out_ref,
    moment_ref,
    held,
    total,
    weighted,
    work,
    near,
    done,
    sem,
    out_sem,
):
    def fetch(group, slot):
        return pltpu.make_async_copy(
            addr_ref.at[pl.ds(lax.rem(group, GROUPS) * GROUP, GROUP), :], near.at[slot], sem.at[slot]
        )

    fetch(0, 0).start()
    fetch(1, 1).start()
    mark = jnp.zeros((1, 128), F32)
    for m in range(PLANE):
        left, right = both(in_ref[m])
        held[pl.ds(m * 2 * PB, PB), :] = left
        held[pl.ds(m * 2 * PB + PB, PB), :] = right
        mark = jnp.maximum(mark, in_ref[m, pl.ds(PB - 1, 1), :])
    held[pl.ds(HOLD, 8), :] = jnp.zeros((8, 128), F32)
    total[...] = jnp.zeros_like(total)
    moment_ref[...] = jnp.zeros_like(moment_ref)

    def gather(slot, k):
        for c in range(TILE):
            work[k % 2, pl.ds(c, 1), :] = held[pl.ds(near[slot, k, c], 1), :]

    def score(t, k):
        dose = dose_ref[t]
        total[gene[t]] += dot(jnp.concatenate([dose, dose], axis=1), split(work[k % 2]))

    def scored(i, carry):
        for slot in range(2):
            group = i * 2 + slot
            fetch(group, slot).wait()
            for k in range(GROUP):
                gather(slot, k)
                score(jnp.maximum(group * GROUP + k - 1, 0), k + 1)
            fetch(group + 2, slot).start()
        return carry

    work[1] = jnp.zeros((TILE, 128), F32)
    lax.fori_loop(0, GROUPS // 2, scored, 0)
    score(TILES - 1, 1)
    for k in range(GENES):
        weight = weight_ref[k]
        scores = total[k] * weight
        one = jnp.sum(scores * scores, axis=0, keepdims=True) * (1.0 / VT)
        moment_ref[k, pl.ds(0, 1), :] = one[:, :PROBES]
        weighted[k] = split(scores * weight)

    def returned(t, slot):
        scale = jnp.where(t < TILES, 1.0 / TILE, 0.0)
        t = jnp.minimum(t, TILES - 1)
        dose = dose_ref[t]
        rows = dot(jnp.concatenate([dose, dose], axis=0), weighted[gene[t]], 0, 0)
        two = jnp.sum(rows * rows, axis=0, keepdims=True) * scale
        moment_ref[gene[t], pl.ds(1, 1), :] += two[:, :PROBES]
        work[slot] = rows

    def scatter(slot, k):
        for c in range(TILE):
            held[pl.ds(near[slot, k, c], 1), :] = work[k % 2, pl.ds(c, 1), :]

    @pl.when(again[0, 0] == 0)
    def _():
        def sent(i, carry):
            for slot in range(2):
                group = i * 2 + slot
                fetch(group, slot).wait()
                for k in range(GROUP):
                    returned(group * GROUP + k + 1, (k + 1) % 2)
                    scatter(slot, k)
                fetch(group + 2, slot).start()
            return carry

        returned(0, 0)
        lax.fori_loop(0, GROUPS // 2, sent, 0)

    @pl.when(again[0, 0] != 0)
    def _():
        held[...] = jnp.zeros_like(held)

        def summed(t, carry):
            returned(t, 0)

            def add(c, inner):
                held[pl.ds(addr[t, c], 1), :] += work[0, pl.ds(c, 1), :]
                return inner

            lax.fori_loop(0, TILE, add, 0)
            return carry

        lax.fori_loop(0, TILES, summed, 0)

    fetch(0, 0).wait()
    fetch(1, 1).wait()
    left = lanes64((PB, 128))
    copies = []
    for m in range(PLANE):
        done[m] = jnp.where(left, held[pl.ds(m * 2 * PB, PB), :], held[pl.ds(m * 2 * PB + PB, PB), :])
        done[m, pl.ds(PB - 1, 1), :] = mark
        if m % 8 == 7:
            part = pl.ds(m - 7, 8)
            copies.append(pltpu.make_async_copy(done.at[part], out_ref.at[part], out_sem.at[m // 8]))
            copies[-1].start()
    for copy in copies:
        copy.wait()


def sum_kernel(in_ref, index_ref, out_ref, mark_ref, total):
    total[...] = jnp.zeros_like(total)
    at = (iota((ROWS, 8 * ZB), 0) + 1).astype(jnp.int16)

    def step(i, mark):
        rows, indices = [], []
        for n in range(4):
            z = i * 4 + n
            turned = jnp.transpose(in_ref[z])
            rows += [turned[:PROBES], turned[PROBES:]]
            indices.append(index_ref[pl.ds(z, 1), :])
            mark = jnp.maximum(mark, in_ref[z, pl.ds(ZB - 1, 1), :])
        index = jnp.concatenate(indices, axis=1)
        rows = jnp.where(index > 0.5, jnp.concatenate(rows, axis=1), 0.0)
        high = rows.astype(BF16).astype(F32)
        parts = jnp.concatenate([high, rows - high], axis=0).astype(BF16)
        total[...] += dot(parts, ones16(at == short(index)), 1, 1)
        return mark

    mark_ref[...] = lax.fori_loop(0, NZ // 4, step, jnp.zeros((1, 128), F32))
    out_ref[...] = total[pl.ds(0, PROBES), :] + total[pl.ds(PROBES, PROBES), :]


VMEM = pl.BlockSpec(memory_space=pltpu.VMEM)
SMEM = pl.BlockSpec(memory_space=pltpu.SMEM)
HBM = pl.BlockSpec(memory_space=pl.ANY)


def call(kernel, outs, ins, scratch=(), out_specs=None, cost=2_000_000, limit=24):
    shapes = [jax.ShapeDtypeStruct(*o) for o in outs]
    return pl.pallas_call(
        kernel,
        out_shape=shapes,
        in_specs=ins,
        out_specs=[VMEM] * len(shapes) if out_specs is None else out_specs,
        scratch_shapes=list(scratch),
        cost_estimate=pl.CostEstimate(flops=cost * 100, bytes_accessed=cost, transcendentals=0),
        compiler_params=pltpu.CompilerParams(vmem_limit_bytes=limit << 20),
    )


def packed(probes, dosages, weights, send_rows, tile_src, tile_gene):
    zdone, pdone = [pltpu.VMEM((NZ, ZB, 128), F32)], [pltpu.VMEM((PLANE, PB, 128), F32)]
    four = [pltpu.SemaphoreType.DMA((4,))]
    value, parts = call(
        ready_kernel,
        [((128, 128), I32), ((2 * PROBES, ROWS), BF16)],
        [VMEM] * 2,
        [pltpu.VMEM((DEV, 128), I32)],
    )(send_rows[0].T, probes)
    used, count = call(used_kernel, [((128, 128), F32)] * 2, [VMEM])(tile_src)
    used, count, value, parts = lax.optimization_barrier((used, count, value, parts))
    asked = lax.all_to_all(used.reshape(PLANE, 4, 128), FLAT, 0, 0, tiled=True).reshape(128, 128)
    (met,) = call(meet_kernel, [((NZ, 8, 128), F32)], [VMEM])(asked)
    met = lax.all_to_all(met, "z", 0, 0, tiled=True).reshape(128, 128)
    asked, count, met = lax.optimization_barrier((asked, count, met))
    table, mark, spread = call(
        table_kernel, [((128, 128), I32), ((1, 128), F32), ((GENES, VT, 128), F32)], [VMEM] * 2
    )(asked, weights)
    addr, again = call(
        place_kernel, [((TILES, TILE), I32), ((1, 1), I32)], [VMEM, VMEM], out_specs=[VMEM, SMEM]
    )(tile_src, count)
    block, index = call(
        send_kernel,
        [((NZ, ZB, 128), F32), ((NZ, 2 * ZB), F32)],
        [VMEM] * 3,
        [pltpu.VMEM((128, 128), I32)] * 2 + zdone + [pltpu.SemaphoreType.DMA((NZ // 2,))],
        out_specs=[HBM, VMEM],
    )(met, value, parts)
    block = lax.all_to_all(block, "z", 0, 0, tiled=True)
    block, addr, again, spread, table, mark = lax.optimization_barrier((block, addr, again, spread, table, mark))
    buffers = [pltpu.VMEM((NZ * ZBUF, 128), F32), pltpu.VMEM((PLANE * PBUF, 128), F32)]
    (block,) = call(relay_kernel, [((PLANE, PB, 128), F32)], [SMEM, VMEM, VMEM], buffers + pdone + four, out_specs=[HBM])(
        table, mark, block
    )
    block = lax.all_to_all(block, FLAT, 0, 0, tiled=True)
    block, moments = call(
        gene_kernel,
        [((PLANE, PB, 128), F32), ((GENES, 2, PROBES), F32)],
        [SMEM] * 3 + [VMEM] * 4,
        [
            pltpu.VMEM((HOLD + 8, 128), F32),
            pltpu.VMEM((GENES, VT, 128), F32),
            pltpu.VMEM((GENES, 2 * VT, 128), BF16),
            pltpu.VMEM((2, TILE, 128), F32),
            pltpu.SMEM((2, GROUP, TILE), I32),
        ]
        + pdone
        + [pltpu.SemaphoreType.DMA((2,))]
        + four,
        out_specs=[HBM, VMEM],
    )(addr, again, tile_gene, addr, block, dosages, spread)
    block = lax.all_to_all(block, FLAT, 0, 0, tiled=True)
    (block,) = call(
        back_kernel, [((NZ, ZB, 128), F32)], [SMEM, VMEM], buffers + zdone + four, out_specs=[HBM]
    )(table, block)
    block = lax.all_to_all(block, "z", 0, 0, tiled=True)
    projected, mark = call(
        sum_kernel,
        [((PROBES, ROWS), F32), ((1, 128), F32)],
        [VMEM] * 2,
        [pltpu.VMEM((2 * PROBES, ROWS), F32)],
    )(block, index)
    return projected, moments, mark[0, 0]


def exchange(rows):
    return lax.all_to_all(rows, ALL, 0, 0, tiled=True)


def whole(probes, dosages, weights, send_rows, tile_src, tile_gene):
    rows_sent = send_rows[0]
    high = lax.Precision.HIGHEST
    outgoing = probes.T[rows_sent].reshape(DEV, SLOTS * PROBES // 128, 128)
    incoming = exchange(outgoing).reshape(SRC, PROBES)
    fetched = jnp.concatenate([incoming, jnp.zeros((1, PROBES), F32)], axis=0)
    slab = fetched[tile_src]
    tile_scores = jnp.einsum("tcb,tvc->tbv", slab, dosages, precision=high, preferred_element_type=F32)
    member = (tile_gene[None, :] == jnp.arange(GENES, dtype=I32)[:, None]).astype(F32)
    scores = jnp.einsum("gt,tbv->gbv", member, tile_scores, precision=high) * weights[:, None, :]
    one = jnp.sum(scores * scores, axis=2) / VT
    weighted = jnp.einsum("gt,gbv->tbv", member, scores * weights[:, None, :], precision=high)
    returned = jnp.einsum("tbv,tvc->tcb", weighted, dosages, precision=high, preferred_element_type=F32)
    two = jnp.dot(member, jnp.sum(returned * returned, axis=1), precision=high) / TILE
    sums = jax.ops.segment_sum(returned.reshape(-1, PROBES), tile_src.reshape(-1), num_segments=SRC + 1)
    arrived = exchange(sums[:SRC].reshape(DEV, SLOTS * PROBES // 128, 128))
    projected = jax.ops.segment_sum(
        arrived.reshape(SRC, PROBES), rows_sent.reshape(-1), num_segments=ROWS
    ).T
    return projected, jnp.stack([one, two], axis=1)


def shards(*args):
    projected, moments, mark = packed(*args)
    projected, moments = lax.cond(mark > 0.5, lambda: whole(*args), lambda: (projected, moments))
    return projected, moments.transpose(1, 2, 0)


def solution(mesh):
    fine = Mesh(mesh.devices.reshape(NY, NZ, NC, NX), ALL)
    placed = (P(None, ALL), P(ALL, None, None), P(ALL, None), P(ALL, None, None), P(ALL, None), P(ALL))
    return jax.shard_map(
        shards,
        mesh=fine,
        in_specs=placed,
        out_specs=(P(None, ALL), P(None, None, ALL)),
        check_vma=False,
    )
```

```python
import jax
import jax.numpy as jnp
from jax import lax
from jax.experimental import pallas as pl
from jax.experimental.pallas import tpu as pltpu
from jax.sharding import Mesh, PartitionSpec as P

NY, NZ, NC, NX = 4, 16, 2, 4
PLANE = NY * NC * NX
DEV = NY * NZ * NC * NX
SLOTS = 24
LANE = 32
SRC = DEV * SLOTS
TILES = 40
TILE = 128
VT = 128
GENES = 20
GROUP = 4
GROUPS = TILES // GROUP
PROBES = 64
ROWS = 1024
ZB = 128
ZCAP = 2 * (ZB - 1)
PB = 96
PCAP = 2 * (PB - 1)
ZBUF = 280
PBUF = 216
HOLD = PLANE * 2 * PB
F32 = jnp.float32
BF16 = jnp.bfloat16
I32 = jnp.int32
ALL = ("y", "z", "c", "x")
FLAT = ("y", "c", "x")


def iota(shape, dim):
    return lax.broadcasted_iota(I32, shape, dim)


def dot(a, b, ca=1, cb=0, **kw):
    return lax.dot_general(a, b, (((ca,), (cb,)), ((), ())), preferred_element_type=F32, **kw)


def ones_where(mask):
    return jnp.where(mask, 1.0, 0.0).astype(BF16)


def ones16(mask):
    return jnp.where(mask, jnp.ones((), BF16), jnp.zeros((), BF16))


def short(v):
    return v.astype(I32).astype(jnp.int16)


def lanes64(shape):
    return iota(shape, 1) < PROBES


def split(v):
    high = v.astype(BF16)
    return jnp.concatenate([high, (v - high.astype(F32)).astype(BF16)], axis=0)


def both(block):
    turned = pltpu.roll(block, PROBES, 1)
    left = lanes64(block.shape)
    return jnp.where(left, block, turned), jnp.where(left, turned, block)


def source_parts(ref, t, n):
    highs, lows, empties = [], [], []
    for i in range(n):
        p = ref[pl.ds(t * n + i, 1), :]
        o = (p * 43691) >> 20
        highs.append(((o >> 7) * (NC * NX) + (o & 7)) * 4 + ((o >> 5) & 3))
        lows.append(((o >> 3) & 3) * LANE + p - o * SLOTS)
        empties.append(p >= SRC)
    return highs, lows, empties


def one_hots(rows):
    return jnp.concatenate([ones16(iota((128, 128), 0).astype(jnp.int16) == r.astype(jnp.int16)) for r in rows], axis=1)


def used_kernel(src_ref, used_ref, count_ref):
    count_ref[...] = jnp.zeros_like(count_ref)

    def step(t, carry):
        highs, lows, _ = source_parts(src_ref, t, 8)
        count_ref[...] += dot(one_hots(highs), one_hots(lows), 1, 1)
        return carry

    lax.fori_loop(0, TILES // 8, step, 0)
    used_ref[...] = jnp.minimum(count_ref[...], 1.0)


def place_kernel(src_ref, count_ref, addr_ref, again_ref):
    count = count_ref[...]
    again_ref[0, 0] = jnp.where(jnp.max(count) > 1.5, 1, 0)
    used = ones_where(count > 0.5)
    row, col = iota((128, 128), 0), iota((128, 128), 1)
    before = dot(used, ones_where(row < col))
    number = dot(used, jnp.ones((128, 128), BF16)).astype(BF16)
    earlier = ones_where(((row >> 2) == (col >> 2)) & (col < row))
    rank = jnp.minimum((dot(earlier, number) + before).astype(I32), PCAP)
    place = (row >> 2) * (2 * PB) + rank + jnp.where(rank >= PB - 1, 1, 0)
    turned = jnp.transpose(place)
    high = turned >> 6
    table = jnp.concatenate([high, turned - (high << 6)], axis=0).astype(F32).astype(BF16)

    def step(t, carry):
        highs, lows, empties = source_parts(src_ref, t, 8)
        found = dot(table, one_hots(highs))
        for i in range(8):
            part = found[:, i * 128 : (i + 1) * 128]
            value = part[:128] * 64.0 + part[128:]
            value = jnp.sum(jnp.where(row == lows[i], value, 0.0), axis=0, keepdims=True)
            addr_ref[pl.ds(t * 8 + i, 1), :] = jnp.where(empties[i], HOLD, value.astype(I32))
        return carry

    lax.fori_loop(0, TILES // 8, step, 0)


def meet_kernel(in_ref, out_ref):
    block = iota((8, 128), 1) >> 5
    for high in range(4):
        parts = [in_ref[pl.ds(x * 4 + high, 8, stride=16), :] for x in range(NX)]
        for low in range(4):
            turned = [pltpu.roll(parts[x], ((x - low) * LANE) % 128, 1) for x in range(NX)]
            result = turned[0]
            for x in range(1, NX):
                result = jnp.where(block == x, turned[x], result)
            out_ref[high * 4 + low] = result


def table_kernel(in_ref, weight_ref, table_ref, mark_ref, spread_ref):
    used = ones_where(in_ref[...] > 0.5)
    row, col = iota((128, 128), 0), iota((128, 128), 1)
    segment = dot(used, ones_where((row >> 5) == (col >> 5)))
    whole_row = dot(used, jnp.ones((128, 128), BF16))
    before = dot(used, ones_where((row >> 5) < (col >> 5)))
    owner = dot(ones_where(((row & 3) == (col & 3)) & (col < row)), segment.astype(BF16))
    holder = before + dot(ones_where(((row >> 2) == (col >> 2)) & (col < row)), whole_row.astype(BF16))
    over = jnp.maximum(
        jnp.where(owner + segment > ZCAP, 1.0, 0.0), jnp.where(holder + segment > PCAP, 1.0, 0.0)
    )
    mark_ref[...] = jnp.broadcast_to(jnp.max(over), (1, 128))
    owner = jnp.minimum(owner, float(ZCAP)).astype(I32) + ((row & 3) * 4 + (col >> 5)) * ZBUF
    holder = jnp.minimum(holder, float(PCAP + 1)).astype(I32) + (row >> 2) * PBUF
    table_ref[...] = jnp.where((col & 1) == 0, owner, holder)
    for k in range(GENES):
        spread_ref[k] = jnp.transpose(jnp.broadcast_to(weight_ref[pl.ds(k, 1), :], (128, VT)))


def ready_kernel(rows_ref, probes_ref, value_ref, parts_ref, turned_ref):
    col = iota((128, 128), 1)
    high = probes_ref[...].astype(BF16).astype(F32)
    parts_ref[...] = jnp.concatenate([high, probes_ref[...] - high], axis=0).astype(BF16)
    turned_ref[...] = jnp.zeros_like(turned_ref)
    for k in range(DEV // 128):
        turned_ref[pl.ds(k * 128, 128), pl.ds(0, SLOTS)] = jnp.transpose(rows_ref[:, pl.ds(k * 128, 128)])
    value = turned_ref[pl.ds(0, 128, stride=NX), :]
    for x in range(1, NX):
        turned = pltpu.roll(turned_ref[pl.ds(x, 128, stride=NX), :], x * LANE, 1)
        value = jnp.where((col >> 5) == x, turned, value)
    value_ref[...] = value + 1


def send_kernel(used_ref, value_ref, parts_ref, out_ref, index_ref, high_ref, low_ref, done, sem):
    used = used_ref[...]
    flag = ones_where(used > 0.5)
    row, col = iota((128, 128), 0), iota((128, 128), 1)
    number = dot(flag, jnp.ones((128, 128), BF16))
    start = dot(ones_where(((row >> 3) == (col >> 3)) & (col < row)), number.astype(BF16))
    place = (start + dot(flag, ones_where(row < col))).astype(I32)
    place = place + jnp.where(place >= ZB - 1, 1, 0)
    high_ref[...] = jnp.where(used > 0.5, place >> 7, -1)
    low_ref[...] = place & (ZB - 1)
    which = iota((8, 128), 0)
    at = iota((ZB, 128), 0).astype(jnp.int16)
    subject = (iota((ROWS, 4 * ZB), 0) + 1).astype(jnp.int16)

    def list_of(z):
        values, places = [], []
        for y in range(NY):
            for c in range(NC):
                i = z * (NY * NC) + y * NC + c
                value = value_ref[pl.ds(y * (NZ * NC) + z * NC + c, 1), :]
                digit = jnp.where(which < 2, value >> 5, value & 31)
                match = ((which & 1) == high_ref[pl.ds(i, 1), :]) & (which < 4)
                values.append(jnp.where(match, digit, 0).astype(F32).astype(BF16))
                places.append(ones16(at == low_ref[pl.ds(i, 1), :].astype(jnp.int16)))
        listed = dot(jnp.concatenate(values, axis=1), jnp.concatenate(places, axis=1), 1, 1)
        index = listed[:2] * 32.0 + listed[2:4]
        index = jnp.concatenate([index[:1], index[1:]], axis=1)
        index_ref[pl.ds(z, 1), :] = index
        return index

    def lists_of(i):
        return jnp.concatenate([list_of(2 * i), list_of(2 * i + 1)], axis=1)

    def step(i, index):
        later = lists_of(jnp.minimum(i + 1, NZ // 2 - 1))
        rows = dot(parts_ref[...], ones16(subject == short(index)))
        rows = rows[:PROBES] + rows[PROBES:]
        for n in range(2):
            left, right = rows[:, 2 * n * ZB : (2 * n + 1) * ZB], rows[:, (2 * n + 1) * ZB : (2 * n + 2) * ZB]
            done[2 * i + n] = jnp.transpose(jnp.concatenate([left, right], axis=0))
        leave(i).start()
        return later

    def leave(i):
        part = pl.ds(2 * i, 2)
        return pltpu.make_async_copy(done.at[part], out_ref.at[part], sem.at[i])

    lax.fori_loop(0, NZ // 2, step, lists_of(0))
    for i in range(NZ // 2):
        leave(i).wait()


def relay_kernel(table, mark_ref, in_ref, out_ref, zbuf, pbuf, done, sem):
    for z in range(NZ):
        left, right = both(in_ref[z])
        zbuf[pl.ds(z * ZBUF, ZB), :] = left
        zbuf[pl.ds(z * ZBUF + ZB - 1, ZB), :] = right
    left = lanes64((PB, 128))
    copies = []
    for r in range(PLANE):
        for z in range(NZ):
            row, col = r * 4 + z // 4, (z % 4) * LANE
            pbuf[pl.ds(table[row, col + 1], SLOTS), :] = zbuf[pl.ds(table[row, col], SLOTS), :]
        done[r] = jnp.where(left, pbuf[pl.ds(r * PBUF, PB), :], pbuf[pl.ds(r * PBUF + PB - 1, PB), :])
        done[r, pl.ds(PB - 1, 1), :] = mark_ref[...]
        if r % 8 == 7:
            part = pl.ds(r - 7, 8)
            copies.append(pltpu.make_async_copy(done.at[part], out_ref.at[part], sem.at[r // 8]))
            copies[-1].start()
    for copy in copies:
        copy.wait()


def back_kernel(table, in_ref, out_ref, zbuf, pbuf, done, sem):
    mark = jnp.zeros((1, 128), F32)
    for r in range(PLANE):
        left, right = both(in_ref[r])
        pbuf[pl.ds(r * PBUF, PB), :] = left
        pbuf[pl.ds(r * PBUF + PB - 1, PB), :] = right
        mark = jnp.maximum(mark, in_ref[r, pl.ds(PB - 1, 1), :])
    left = lanes64((ZB, 128))
    copies = []
    for z in range(NZ):
        for r in range(PLANE):
            row, col = r * 4 + z // 4, (z % 4) * LANE
            zbuf[pl.ds(table[row, col], SLOTS), :] = pbuf[pl.ds(table[row, col + 1], SLOTS), :]
        done[z] = jnp.where(left, zbuf[pl.ds(z * ZBUF, ZB), :], zbuf[pl.ds(z * ZBUF + ZB - 1, ZB), :])
        done[z, pl.ds(ZB - 1, 1), :] = mark
        if z % 4 == 3:
            part = pl.ds(z - 3, 4)
            copies.append(pltpu.make_async_copy(done.at[part], out_ref.at[part], sem.at[z // 4]))
            copies[-1].start()
    for copy in copies:
        copy.wait()


def gene_kernel(
    addr,
    again,
    gene,
    addr_ref,
    in_ref,
    dose_ref,
    turned_ref,
    weight_ref,
    out_ref,
    moment_ref,
    held,
    total,
    weighted,
    work,
    near,
    done,
    sem,
    out_sem,
):
    def fetch(group, slot):
        return pltpu.make_async_copy(
            addr_ref.at[pl.ds(lax.rem(group, GROUPS) * GROUP, GROUP), :], near.at[slot], sem.at[slot]
        )

    fetch(0, 0).start()
    fetch(1, 1).start()
    mark = jnp.zeros((1, 128), F32)
    for m in range(PLANE):
        left, right = both(in_ref[m])
        held[pl.ds(m * 2 * PB, PB), :] = left
        held[pl.ds(m * 2 * PB + PB, PB), :] = right
        mark = jnp.maximum(mark, in_ref[m, pl.ds(PB - 1, 1), :])
    held[pl.ds(HOLD, 8), :] = jnp.zeros((8, 128), F32)
    total[...] = jnp.zeros_like(total)
    moment_ref[...] = jnp.zeros_like(moment_ref)

    def gather(slot, k):
        for c in range(TILE):
            work[k % 2, pl.ds(c, 1), :] = held[pl.ds(near[slot, k, c], 1), :]

    def score(t, k):
        dose = dose_ref[t]
        total[gene[t]] += dot(jnp.concatenate([dose, dose], axis=1), split(work[k % 2]))

    def scored(i, carry):
        for slot in range(2):
            group = i * 2 + slot
            fetch(group, slot).wait()
            for k in range(GROUP):
                gather(slot, k)
                score(jnp.maximum(group * GROUP + k - 1, 0), k + 1)
            fetch(group + 2, slot).start()
        return carry

    work[1] = jnp.zeros((TILE, 128), F32)
    lax.fori_loop(0, GROUPS // 2, scored, 0)
    score(TILES - 1, 1)
    for k in range(GENES):
        weight = weight_ref[k]
        scores = total[k] * weight
        one = jnp.sum(scores * scores, axis=0, keepdims=True) * (1.0 / VT)
        moment_ref[k, pl.ds(0, 1), :] = one[:, :PROBES]
        weighted[k] = split(scores * weight)

    def returned(t, slot):
        scale = jnp.where(t < TILES, 1.0 / TILE, 0.0)
        t = jnp.minimum(t, TILES - 1)
        dose = turned_ref[t]
        rows = dot(jnp.concatenate([dose, dose], axis=1), weighted[gene[t]])
        two = jnp.sum(rows * rows, axis=0, keepdims=True) * scale
        moment_ref[gene[t], pl.ds(1, 1), :] += two[:, :PROBES]
        work[slot] = rows

    def scatter(slot, k):
        for c in range(TILE):
            held[pl.ds(near[slot, k, c], 1), :] = work[k % 2, pl.ds(c, 1), :]

    @pl.when(again[0, 0] == 0)
    def _():
        def sent(i, carry):
            for slot in range(2):
                group = i * 2 + slot
                fetch(group, slot).wait()
                for k in range(GROUP):
                    returned(group * GROUP + k + 1, (k + 1) % 2)
                    scatter(slot, k)
                fetch(group + 2, slot).start()
            return carry

        returned(0, 0)
        lax.fori_loop(0, GROUPS // 2, sent, 0)

    @pl.when(again[0, 0] != 0)
    def _():
        held[...] = jnp.zeros_like(held)

        def summed(t, carry):
            returned(t, 0)

            def add(c, inner):
                held[pl.ds(addr[t, c], 1), :] += work[0, pl.ds(c, 1), :]
                return inner

            lax.fori_loop(0, TILE, add, 0)
            return carry

        lax.fori_loop(0, TILES, summed, 0)

    fetch(0, 0).wait()
    fetch(1, 1).wait()
    left = lanes64((PB, 128))
    copies = []
    for m in range(PLANE):
        done[m] = jnp.where(left, held[pl.ds(m * 2 * PB, PB), :], held[pl.ds(m * 2 * PB + PB, PB), :])
        done[m, pl.ds(PB - 1, 1), :] = mark
        if m % 8 == 7:
            part = pl.ds(m - 7, 8)
            copies.append(pltpu.make_async_copy(done.at[part], out_ref.at[part], out_sem.at[m // 8]))
            copies[-1].start()
    for copy in copies:
        copy.wait()


def sum_kernel(in_ref, index_ref, out_ref, mark_ref, total):
    total[...] = jnp.zeros_like(total)
    at = (iota((ROWS, 8 * ZB), 0) + 1).astype(jnp.int16)

    def step(i, mark):
        rows, indices = [], []
        for n in range(4):
            z = i * 4 + n
            turned = jnp.transpose(in_ref[z])
            rows += [turned[:PROBES], turned[PROBES:]]
            indices.append(index_ref[pl.ds(z, 1), :])
            mark = jnp.maximum(mark, in_ref[z, pl.ds(ZB - 1, 1), :])
        index = jnp.concatenate(indices, axis=1)
        rows = jnp.where(index > 0.5, jnp.concatenate(rows, axis=1), 0.0)
        high = rows.astype(BF16).astype(F32)
        parts = jnp.concatenate([high, rows - high], axis=0).astype(BF16)
        total[...] += dot(parts, ones16(at == short(index)), 1, 1)
        return mark

    mark_ref[...] = lax.fori_loop(0, NZ // 4, step, jnp.zeros((1, 128), F32))
    out_ref[...] = total[pl.ds(0, PROBES), :] + total[pl.ds(PROBES, PROBES), :]


def turn_kernel(dose_ref, out_ref):
    def step(t, carry):
        out_ref[t] = jnp.transpose(dose_ref[t].astype(F32)).astype(BF16)
        return carry

    lax.fori_loop(0, TILES, step, 0)


VMEM = pl.BlockSpec(memory_space=pltpu.VMEM)
SMEM = pl.BlockSpec(memory_space=pltpu.SMEM)
HBM = pl.BlockSpec(memory_space=pl.ANY)


def call(kernel, outs, ins, scratch=(), out_specs=None, cost=2_000_000, limit=24):
    shapes = [jax.ShapeDtypeStruct(*o) for o in outs]
    return pl.pallas_call(
        kernel,
        out_shape=shapes,
        in_specs=ins,
        out_specs=[VMEM] * len(shapes) if out_specs is None else out_specs,
        scratch_shapes=list(scratch),
        cost_estimate=pl.CostEstimate(flops=cost * 100, bytes_accessed=cost, transcendentals=0),
        compiler_params=pltpu.CompilerParams(vmem_limit_bytes=limit << 20),
    )


def packed(probes, dosages, weights, send_rows, tile_src, tile_gene):
    zdone, pdone = [pltpu.VMEM((NZ, ZB, 128), F32)], [pltpu.VMEM((PLANE, PB, 128), F32)]
    four = [pltpu.SemaphoreType.DMA((4,))]
    value, parts = call(
        ready_kernel,
        [((128, 128), I32), ((2 * PROBES, ROWS), BF16)],
        [VMEM] * 2,
        [pltpu.VMEM((DEV, 128), I32)],
    )(send_rows[0].T, probes)
    used, count = call(used_kernel, [((128, 128), F32)] * 2, [VMEM])(tile_src)
    used, count, value, parts = lax.optimization_barrier((used, count, value, parts))
    asked = lax.all_to_all(used.reshape(PLANE, 4, 128), FLAT, 0, 0, tiled=True).reshape(128, 128)
    (met,) = call(meet_kernel, [((NZ, 8, 128), F32)], [VMEM])(asked)
    met = lax.all_to_all(met, "z", 0, 0, tiled=True).reshape(128, 128)
    asked, count, met, doses = lax.optimization_barrier((asked, count, met, dosages))
    (turned,) = call(turn_kernel, [((TILES, TILE, VT), BF16)], [VMEM])(doses)
    table, mark, spread = call(
        table_kernel, [((128, 128), I32), ((1, 128), F32), ((GENES, VT, 128), F32)], [VMEM] * 2
    )(asked, weights)
    addr, again = call(
        place_kernel, [((TILES, TILE), I32), ((1, 1), I32)], [VMEM, VMEM], out_specs=[VMEM, SMEM]
    )(tile_src, count)
    block, index = call(
        send_kernel,
        [((NZ, ZB, 128), F32), ((NZ, 2 * ZB), F32)],
        [VMEM] * 3,
        [pltpu.VMEM((128, 128), I32)] * 2 + zdone + [pltpu.SemaphoreType.DMA((NZ // 2,))],
        out_specs=[HBM, VMEM],
    )(met, value, parts)
    block = lax.all_to_all(block, "z", 0, 0, tiled=True)
    block, addr, again, spread, table, mark, turned = lax.optimization_barrier(
        (block, addr, again, spread, table, mark, turned)
    )
    buffers = [pltpu.VMEM((NZ * ZBUF, 128), F32), pltpu.VMEM((PLANE * PBUF, 128), F32)]
    (block,) = call(relay_kernel, [((PLANE, PB, 128), F32)], [SMEM, VMEM, VMEM], buffers + pdone + four, out_specs=[HBM])(
        table, mark, block
    )
    block = lax.all_to_all(block, FLAT, 0, 0, tiled=True)
    block, moments = call(
        gene_kernel,
        [((PLANE, PB, 128), F32), ((GENES, 2, PROBES), F32)],
        [SMEM] * 3 + [VMEM] * 5,
        [
            pltpu.VMEM((HOLD + 8, 128), F32),
            pltpu.VMEM((GENES, VT, 128), F32),
            pltpu.VMEM((GENES, 2 * VT, 128), BF16),
            pltpu.VMEM((2, TILE, 128), F32),
            pltpu.SMEM((2, GROUP, TILE), I32),
        ]
        + pdone
        + [pltpu.SemaphoreType.DMA((2,))]
        + four,
        out_specs=[HBM, VMEM],
    )(addr, again, tile_gene, addr, block, dosages, turned, spread)
    block = lax.all_to_all(block, FLAT, 0, 0, tiled=True)
    (block,) = call(
        back_kernel, [((NZ, ZB, 128), F32)], [SMEM, VMEM], buffers + zdone + four, out_specs=[HBM]
    )(table, block)
    block = lax.all_to_all(block, "z", 0, 0, tiled=True)
    projected, mark = call(
        sum_kernel,
        [((PROBES, ROWS), F32), ((1, 128), F32)],
        [VMEM] * 2,
        [pltpu.VMEM((2 * PROBES, ROWS), F32)],
    )(block, index)
    return projected, moments, mark[0, 0]


def exchange(rows):
    return lax.all_to_all(rows, ALL, 0, 0, tiled=True)


def whole(probes, dosages, weights, send_rows, tile_src, tile_gene):
    rows_sent = send_rows[0]
    high = lax.Precision.HIGHEST
    outgoing = probes.T[rows_sent].reshape(DEV, SLOTS * PROBES // 128, 128)
    incoming = exchange(outgoing).reshape(SRC, PROBES)
    fetched = jnp.concatenate([incoming, jnp.zeros((1, PROBES), F32)], axis=0)
    slab = fetched[tile_src]
    tile_scores = jnp.einsum("tcb,tvc->tbv", slab, dosages, precision=high, preferred_element_type=F32)
    member = (tile_gene[None, :] == jnp.arange(GENES, dtype=I32)[:, None]).astype(F32)
    scores = jnp.einsum("gt,tbv->gbv", member, tile_scores, precision=high) * weights[:, None, :]
    one = jnp.sum(scores * scores, axis=2) / VT
    weighted = jnp.einsum("gt,gbv->tbv", member, scores * weights[:, None, :], precision=high)
    returned = jnp.einsum("tbv,tvc->tcb", weighted, dosages, precision=high, preferred_element_type=F32)
    two = jnp.dot(member, jnp.sum(returned * returned, axis=1), precision=high) / TILE
    sums = jax.ops.segment_sum(returned.reshape(-1, PROBES), tile_src.reshape(-1), num_segments=SRC + 1)
    arrived = exchange(sums[:SRC].reshape(DEV, SLOTS * PROBES // 128, 128))
    projected = jax.ops.segment_sum(
        arrived.reshape(SRC, PROBES), rows_sent.reshape(-1), num_segments=ROWS
    ).T
    return projected, jnp.stack([one, two], axis=1)


def shards(*args):
    projected, moments, mark = packed(*args)
    projected, moments = lax.cond(mark > 0.5, lambda: whole(*args), lambda: (projected, moments))
    return projected, moments.transpose(1, 2, 0)


def solution(mesh):
    fine = Mesh(mesh.devices.reshape(NY, NZ, NC, NX), ALL)
    placed = (P(None, ALL), P(ALL, None, None), P(ALL, None), P(ALL, None, None), P(ALL, None), P(ALL))
    return jax.shard_map(
        shards,
        mesh=fine,
        in_specs=placed,
        out_specs=(P(None, ALL), P(None, None, ALL)),
        check_vma=False,
    )
```

```python
import jax
import jax.numpy as jnp
from jax import lax
from jax.experimental import pallas as pl
from jax.experimental.pallas import tpu as pltpu
from jax.sharding import Mesh, PartitionSpec as P

NY, NZ, NC, NX = 4, 16, 2, 4
PLANE = NY * NC * NX
DEV = NY * NZ * NC * NX
SLOTS = 24
LANE = 32
SRC = DEV * SLOTS
TILES = 40
TILE = 128
VT = 128
GENES = 20
GROUP = 4
GROUPS = TILES // GROUP
PROBES = 64
ROWS = 1024
ZB = 128
ZCAP = 2 * (ZB - 1)
PB = 96
PCAP = 2 * (PB - 1)
ZBUF = 280
PBUF = 216
HOLD = PLANE * 2 * PB
F32 = jnp.float32
BF16 = jnp.bfloat16
I32 = jnp.int32
ALL = ("y", "z", "c", "x")
FLAT = ("y", "c", "x")


def iota(shape, dim):
    return lax.broadcasted_iota(I32, shape, dim)


def dot(a, b, ca=1, cb=0, **kw):
    return lax.dot_general(a, b, (((ca,), (cb,)), ((), ())), preferred_element_type=F32, **kw)


def ones_where(mask):
    return jnp.where(mask, 1.0, 0.0).astype(BF16)


def ones16(mask):
    return jnp.where(mask, jnp.ones((), BF16), jnp.zeros((), BF16))


def short(v):
    return v.astype(I32).astype(jnp.int16)


def lanes64(shape):
    return iota(shape, 1) < PROBES


def split(v):
    high = v.astype(BF16)
    return jnp.concatenate([high, (v - high.astype(F32)).astype(BF16)], axis=0)


def both(block):
    turned = pltpu.roll(block, PROBES, 1)
    left = lanes64(block.shape)
    return jnp.where(left, block, turned), jnp.where(left, turned, block)


def source_parts(ref, t, n):
    highs, lows, empties = [], [], []
    for i in range(n):
        p = ref[pl.ds(t * n + i, 1), :]
        o = (p * 43691) >> 20
        highs.append(((o >> 7) * (NC * NX) + (o & 7)) * 4 + ((o >> 5) & 3))
        lows.append(((o >> 3) & 3) * LANE + p - o * SLOTS)
        empties.append(p >= SRC)
    return highs, lows, empties


def one_hots(rows):
    return jnp.concatenate([ones16(iota((128, 128), 0).astype(jnp.int16) == r.astype(jnp.int16)) for r in rows], axis=1)


def place_kernel(src_ref, count_ref, addr_ref, again_ref):
    count = count_ref[...]
    again_ref[0, 0] = jnp.where(jnp.max(count) > 1.5, 1, 0)
    used = ones_where(count > 0.5)
    row, col = iota((128, 128), 0), iota((128, 128), 1)
    before = dot(used, ones_where(row < col))
    number = dot(used, jnp.ones((128, 128), BF16)).astype(BF16)
    earlier = ones_where(((row >> 2) == (col >> 2)) & (col < row))
    rank = jnp.minimum((dot(earlier, number) + before).astype(I32), PCAP)
    place = (row >> 2) * (2 * PB) + rank + jnp.where(rank >= PB - 1, 1, 0)
    turned = jnp.transpose(place)
    high = turned >> 6
    table = jnp.concatenate([high, turned - (high << 6)], axis=0).astype(F32).astype(BF16)

    def step(t, carry):
        highs, lows, empties = source_parts(src_ref, t, 8)
        found = dot(table, one_hots(highs))
        for i in range(8):
            part = found[:, i * 128 : (i + 1) * 128]
            value = part[:128] * 64.0 + part[128:]
            value = jnp.sum(jnp.where(row == lows[i], value, 0.0), axis=0, keepdims=True)
            addr_ref[pl.ds(t * 8 + i, 1), :] = jnp.where(empties[i], HOLD, value.astype(I32))
        return carry

    lax.fori_loop(0, TILES // 8, step, 0)


def meet_kernel(in_ref, out_ref):
    block = iota((8, 128), 1) >> 5
    for high in range(4):
        parts = [in_ref[pl.ds(x * 4 + high, 8, stride=16), :] for x in range(NX)]
        for low in range(4):
            turned = [pltpu.roll(parts[x], ((x - low) * LANE) % 128, 1) for x in range(NX)]
            result = turned[0]
            for x in range(1, NX):
                result = jnp.where(block == x, turned[x], result)
            out_ref[high * 4 + low] = result


def table_kernel(in_ref, weight_ref, table_ref, mark_ref, spread_ref):
    used = ones_where(in_ref[...] > 0.5)
    row, col = iota((128, 128), 0), iota((128, 128), 1)
    segment = dot(used, ones_where((row >> 5) == (col >> 5)))
    whole_row = dot(used, jnp.ones((128, 128), BF16))
    before = dot(used, ones_where((row >> 5) < (col >> 5)))
    owner = dot(ones_where(((row & 3) == (col & 3)) & (col < row)), segment.astype(BF16))
    holder = before + dot(ones_where(((row >> 2) == (col >> 2)) & (col < row)), whole_row.astype(BF16))
    over = jnp.maximum(
        jnp.where(owner + segment > ZCAP, 1.0, 0.0), jnp.where(holder + segment > PCAP, 1.0, 0.0)
    )
    mark_ref[...] = jnp.broadcast_to(jnp.max(over), (1, 128))
    owner = jnp.minimum(owner, float(ZCAP)).astype(I32) + ((row & 3) * 4 + (col >> 5)) * ZBUF
    holder = jnp.minimum(holder, float(PCAP + 1)).astype(I32) + (row >> 2) * PBUF
    table_ref[...] = jnp.where((col & 1) == 0, owner, holder)
    for k in range(GENES):
        spread_ref[k] = jnp.transpose(jnp.broadcast_to(weight_ref[pl.ds(k, 1), :], (128, VT)))


def ready_kernel(
    src_ref, rows_ref, probes_ref, used_ref, count_ref, value_ref, parts_ref, turned_ref
):
    count = jnp.zeros((128, 128), F32)
    for t in range(TILES // 8):
        highs, lows, _ = source_parts(src_ref, t, 8)
        count += dot(one_hots(highs), one_hots(lows), 1, 1)
    count_ref[...] = count
    used_ref[...] = jnp.minimum(count, 1.0)
    col = iota((128, 128), 1)
    high = probes_ref[...].astype(BF16).astype(F32)
    parts_ref[...] = jnp.concatenate([high, probes_ref[...] - high], axis=0).astype(BF16)
    turned_ref[...] = jnp.zeros_like(turned_ref)
    for k in range(DEV // 128):
        turned_ref[pl.ds(k * 128, 128), pl.ds(0, SLOTS)] = jnp.transpose(rows_ref[:, pl.ds(k * 128, 128)])
    value = turned_ref[pl.ds(0, 128, stride=NX), :]
    for x in range(1, NX):
        turned = pltpu.roll(turned_ref[pl.ds(x, 128, stride=NX), :], x * LANE, 1)
        value = jnp.where((col >> 5) == x, turned, value)
    value_ref[...] = value + 1


def send_kernel(used_ref, value_ref, parts_ref, out_ref, index_ref, high_ref, low_ref, done, sem):
    used = used_ref[...]
    flag = ones_where(used > 0.5)
    row, col = iota((128, 128), 0), iota((128, 128), 1)
    number = dot(flag, jnp.ones((128, 128), BF16))
    start = dot(ones_where(((row >> 3) == (col >> 3)) & (col < row)), number.astype(BF16))
    place = (start + dot(flag, ones_where(row < col))).astype(I32)
    place = place + jnp.where(place >= ZB - 1, 1, 0)
    high_ref[...] = jnp.where(used > 0.5, place >> 7, -1)
    low_ref[...] = place & (ZB - 1)
    which = iota((8, 128), 0)
    at = iota((ZB, 128), 0).astype(jnp.int16)
    subject = (iota((ROWS, 4 * ZB), 0) + 1).astype(jnp.int16)

    def list_of(z):
        values, places = [], []
        for y in range(NY):
            for c in range(NC):
                i = z * (NY * NC) + y * NC + c
                value = value_ref[pl.ds(y * (NZ * NC) + z * NC + c, 1), :]
                digit = jnp.where(which < 2, value >> 5, value & 31)
                match = ((which & 1) == high_ref[pl.ds(i, 1), :]) & (which < 4)
                values.append(jnp.where(match, digit, 0).astype(F32).astype(BF16))
                places.append(ones16(at == low_ref[pl.ds(i, 1), :].astype(jnp.int16)))
        listed = dot(jnp.concatenate(values, axis=1), jnp.concatenate(places, axis=1), 1, 1)
        index = listed[:2] * 32.0 + listed[2:4]
        index = jnp.concatenate([index[:1], index[1:]], axis=1)
        index_ref[pl.ds(z, 1), :] = index
        return index

    def lists_of(i):
        return jnp.concatenate([list_of(2 * i), list_of(2 * i + 1)], axis=1)

    def step(i, index):
        later = lists_of(jnp.minimum(i + 1, NZ // 2 - 1))
        rows = dot(parts_ref[...], ones16(subject == short(index)))
        rows = rows[:PROBES] + rows[PROBES:]
        for n in range(2):
            left, right = rows[:, 2 * n * ZB : (2 * n + 1) * ZB], rows[:, (2 * n + 1) * ZB : (2 * n + 2) * ZB]
            done[2 * i + n] = jnp.transpose(jnp.concatenate([left, right], axis=0))
        leave(i).start()
        return later

    def leave(i):
        part = pl.ds(2 * i, 2)
        return pltpu.make_async_copy(done.at[part], out_ref.at[part], sem.at[i])

    lax.fori_loop(0, NZ // 2, step, lists_of(0))
    for i in range(NZ // 2):
        leave(i).wait()


def relay_kernel(table, mark_ref, in_ref, out_ref, zbuf, pbuf, done, sem):
    for z in range(NZ):
        left, right = both(in_ref[z])
        zbuf[pl.ds(z * ZBUF, ZB), :] = left
        zbuf[pl.ds(z * ZBUF + ZB - 1, ZB), :] = right
    left = lanes64((PB, 128))
    copies = []
    for r in range(PLANE):
        for z in range(NZ):
            row, col = r * 4 + z // 4, (z % 4) * LANE
            pbuf[pl.ds(table[row, col + 1], SLOTS), :] = zbuf[pl.ds(table[row, col], SLOTS), :]
        done[r] = jnp.where(left, pbuf[pl.ds(r * PBUF, PB), :], pbuf[pl.ds(r * PBUF + PB - 1, PB), :])
        done[r, pl.ds(PB - 1, 1), :] = mark_ref[...]
        if r % 8 == 7:
            part = pl.ds(r - 7, 8)
            copies.append(pltpu.make_async_copy(done.at[part], out_ref.at[part], sem.at[r // 8]))
            copies[-1].start()
    for copy in copies:
        copy.wait()


def back_kernel(table, in_ref, out_ref, zbuf, pbuf, done, sem):
    mark = jnp.zeros((1, 128), F32)
    for r in range(PLANE):
        left, right = both(in_ref[r])
        pbuf[pl.ds(r * PBUF, PB), :] = left
        pbuf[pl.ds(r * PBUF + PB - 1, PB), :] = right
        mark = jnp.maximum(mark, in_ref[r, pl.ds(PB - 1, 1), :])
    left = lanes64((ZB, 128))
    copies = []
    for z in range(NZ):
        for r in range(PLANE):
            row, col = r * 4 + z // 4, (z % 4) * LANE
            zbuf[pl.ds(table[row, col], SLOTS), :] = pbuf[pl.ds(table[row, col + 1], SLOTS), :]
        done[z] = jnp.where(left, zbuf[pl.ds(z * ZBUF, ZB), :], zbuf[pl.ds(z * ZBUF + ZB - 1, ZB), :])
        done[z, pl.ds(ZB - 1, 1), :] = mark
        if z % 4 == 3:
            part = pl.ds(z - 3, 4)
            copies.append(pltpu.make_async_copy(done.at[part], out_ref.at[part], sem.at[z // 4]))
            copies[-1].start()
    for copy in copies:
        copy.wait()


def gene_kernel(
    addr,
    again,
    gene,
    addr_ref,
    in_ref,
    dose_ref,
    turned_ref,
    weight_ref,
    out_ref,
    moment_ref,
    held,
    total,
    weighted,
    work,
    near,
    done,
    sem,
    out_sem,
):
    def fetch(group, slot):
        return pltpu.make_async_copy(
            addr_ref.at[pl.ds(lax.rem(group, GROUPS) * GROUP, GROUP), :], near.at[slot], sem.at[slot]
        )

    fetch(0, 0).start()
    fetch(1, 1).start()
    mark = jnp.zeros((1, 128), F32)
    for m in range(PLANE):
        left, right = both(in_ref[m])
        held[pl.ds(m * 2 * PB, PB), :] = left
        held[pl.ds(m * 2 * PB + PB, PB), :] = right
        mark = jnp.maximum(mark, in_ref[m, pl.ds(PB - 1, 1), :])
    held[pl.ds(HOLD, 8), :] = jnp.zeros((8, 128), F32)
    total[...] = jnp.zeros_like(total)
    moment_ref[...] = jnp.zeros_like(moment_ref)

    def gather(slot, k):
        for c in range(TILE):
            work[k % 2, pl.ds(c, 1), :] = held[pl.ds(near[slot, k, c], 1), :]

    def score(t, k):
        dose = dose_ref[t]
        total[gene[t]] += dot(jnp.concatenate([dose, dose], axis=1), split(work[k % 2]))

    def scored(i, carry):
        for slot in range(2):
            group = i * 2 + slot
            fetch(group, slot).wait()
            for k in range(GROUP):
                gather(slot, k)
                score(jnp.maximum(group * GROUP + k - 1, 0), k + 1)
            fetch(group + 2, slot).start()
        return carry

    work[1] = jnp.zeros((TILE, 128), F32)
    lax.fori_loop(0, GROUPS // 2, scored, 0)
    score(TILES - 1, 1)
    for k in range(GENES):
        weight = weight_ref[k]
        scores = total[k] * weight
        one = jnp.sum(scores * scores, axis=0, keepdims=True) * (1.0 / VT)
        moment_ref[k, pl.ds(0, 1), :] = one[:, :PROBES]
        weighted[k] = split(scores * weight)

    def returned(t, slot):
        scale = jnp.where(t < TILES, 1.0 / TILE, 0.0)
        t = jnp.minimum(t, TILES - 1)
        dose = turned_ref[t]
        rows = dot(jnp.concatenate([dose, dose], axis=1), weighted[gene[t]])
        two = jnp.sum(rows * rows, axis=0, keepdims=True) * scale
        moment_ref[gene[t], pl.ds(1, 1), :] += two[:, :PROBES]
        work[slot] = rows

    def scatter(slot, k):
        for c in range(TILE):
            held[pl.ds(near[slot, k, c], 1), :] = work[k % 2, pl.ds(c, 1), :]

    @pl.when(again[0, 0] == 0)
    def _():
        def sent(i, carry):
            for slot in range(2):
                group = i * 2 + slot
                fetch(group, slot).wait()
                for k in range(GROUP):
                    returned(group * GROUP + k + 1, (k + 1) % 2)
                    scatter(slot, k)
                fetch(group + 2, slot).start()
            return carry

        returned(0, 0)
        lax.fori_loop(0, GROUPS // 2, sent, 0)

    @pl.when(again[0, 0] != 0)
    def _():
        held[...] = jnp.zeros_like(held)

        def summed(t, carry):
            returned(t, 0)

            def add(c, inner):
                held[pl.ds(addr[t, c], 1), :] += work[0, pl.ds(c, 1), :]
                return inner

            lax.fori_loop(0, TILE, add, 0)
            return carry

        lax.fori_loop(0, TILES, summed, 0)

    fetch(0, 0).wait()
    fetch(1, 1).wait()
    left = lanes64((PB, 128))
    copies = []
    for m in range(PLANE):
        done[m] = jnp.where(left, held[pl.ds(m * 2 * PB, PB), :], held[pl.ds(m * 2 * PB + PB, PB), :])
        done[m, pl.ds(PB - 1, 1), :] = mark
        if m % 8 == 7:
            part = pl.ds(m - 7, 8)
            copies.append(pltpu.make_async_copy(done.at[part], out_ref.at[part], out_sem.at[m // 8]))
            copies[-1].start()
    for copy in copies:
        copy.wait()


def sum_kernel(in_ref, index_ref, out_ref, mark_ref, total):
    total[...] = jnp.zeros_like(total)
    at = (iota((ROWS, 8 * ZB), 0) + 1).astype(jnp.int16)

    def step(i, mark):
        rows, indices = [], []
        for n in range(4):
            z = i * 4 + n
            turned = jnp.transpose(in_ref[z])
            rows += [turned[:PROBES], turned[PROBES:]]
            indices.append(index_ref[pl.ds(z, 1), :])
            mark = jnp.maximum(mark, in_ref[z, pl.ds(ZB - 1, 1), :])
        index = jnp.concatenate(indices, axis=1)
        rows = jnp.where(index > 0.5, jnp.concatenate(rows, axis=1), 0.0)
        high = rows.astype(BF16).astype(F32)
        parts = jnp.concatenate([high, rows - high], axis=0).astype(BF16)
        total[...] += dot(parts, ones16(at == short(index)), 1, 1)
        return mark

    mark_ref[...] = lax.fori_loop(0, NZ // 4, step, jnp.zeros((1, 128), F32))
    out_ref[...] = total[pl.ds(0, PROBES), :] + total[pl.ds(PROBES, PROBES), :]


def turn_kernel(dose_ref, out_ref):
    def step(t, carry):
        out_ref[t] = jnp.transpose(dose_ref[t].astype(F32)).astype(BF16)
        return carry

    lax.fori_loop(0, TILES, step, 0)


VMEM = pl.BlockSpec(memory_space=pltpu.VMEM)
SMEM = pl.BlockSpec(memory_space=pltpu.SMEM)
HBM = pl.BlockSpec(memory_space=pl.ANY)


def call(kernel, outs, ins, scratch=(), out_specs=None, cost=2_000_000, limit=24):
    shapes = [jax.ShapeDtypeStruct(*o) for o in outs]
    return pl.pallas_call(
        kernel,
        out_shape=shapes,
        in_specs=ins,
        out_specs=[VMEM] * len(shapes) if out_specs is None else out_specs,
        scratch_shapes=list(scratch),
        cost_estimate=pl.CostEstimate(flops=cost * 100, bytes_accessed=cost, transcendentals=0),
        compiler_params=pltpu.CompilerParams(vmem_limit_bytes=limit << 20),
    )


def packed(probes, dosages, weights, send_rows, tile_src, tile_gene):
    zdone, pdone = [pltpu.VMEM((NZ, ZB, 128), F32)], [pltpu.VMEM((PLANE, PB, 128), F32)]
    four = [pltpu.SemaphoreType.DMA((4,))]
    used, count, value, parts = call(
        ready_kernel,
        [((128, 128), F32), ((128, 128), F32), ((128, 128), I32), ((2 * PROBES, ROWS), BF16)],
        [VMEM] * 3,
        [pltpu.VMEM((DEV, 128), I32)],
    )(tile_src, send_rows[0].T, probes)
    asked = lax.all_to_all(used.reshape(PLANE, 4, 128), FLAT, 0, 0, tiled=True).reshape(128, 128)
    (met,) = call(meet_kernel, [((NZ, 8, 128), F32)], [VMEM])(asked)
    met = lax.all_to_all(met, "z", 0, 0, tiled=True).reshape(128, 128)
    asked, count, met, doses = lax.optimization_barrier((asked, count, met, dosages))
    (turned,) = call(turn_kernel, [((TILES, TILE, VT), BF16)], [VMEM])(doses)
    table, mark, spread = call(
        table_kernel, [((128, 128), I32), ((1, 128), F32), ((GENES, VT, 128), F32)], [VMEM] * 2
    )(asked, weights)
    addr, again = call(
        place_kernel, [((TILES, TILE), I32), ((1, 1), I32)], [VMEM, VMEM], out_specs=[VMEM, SMEM]
    )(tile_src, count)
    block, index = call(
        send_kernel,
        [((NZ, ZB, 128), F32), ((NZ, 2 * ZB), F32)],
        [VMEM] * 3,
        [pltpu.VMEM((128, 128), I32)] * 2 + zdone + [pltpu.SemaphoreType.DMA((NZ // 2,))],
        out_specs=[HBM, VMEM],
    )(met, value, parts)
    block = lax.all_to_all(block, "z", 0, 0, tiled=True)
    block, addr, again, spread, table, mark, turned = lax.optimization_barrier(
        (block, addr, again, spread, table, mark, turned)
    )
    buffers = [pltpu.VMEM((NZ * ZBUF, 128), F32), pltpu.VMEM((PLANE * PBUF, 128), F32)]
    (block,) = call(relay_kernel, [((PLANE, PB, 128), F32)], [SMEM, VMEM, VMEM], buffers + pdone + four, out_specs=[HBM])(
        table, mark, block
    )
    block = lax.all_to_all(block, FLAT, 0, 0, tiled=True)
    block, moments = call(
        gene_kernel,
        [((PLANE, PB, 128), F32), ((GENES, 2, PROBES), F32)],
        [SMEM] * 3 + [VMEM] * 5,
        [
            pltpu.VMEM((HOLD + 8, 128), F32),
            pltpu.VMEM((GENES, VT, 128), F32),
            pltpu.VMEM((GENES, 2 * VT, 128), BF16),
            pltpu.VMEM((2, TILE, 128), F32),
            pltpu.SMEM((2, GROUP, TILE), I32),
        ]
        + pdone
        + [pltpu.SemaphoreType.DMA((2,))]
        + four,
        out_specs=[HBM, VMEM],
    )(addr, again, tile_gene, addr, block, dosages, turned, spread)
    block = lax.all_to_all(block, FLAT, 0, 0, tiled=True)
    (block,) = call(
        back_kernel, [((NZ, ZB, 128), F32)], [SMEM, VMEM], buffers + zdone + four, out_specs=[HBM]
    )(table, block)
    block = lax.all_to_all(block, "z", 0, 0, tiled=True)
    projected, mark = call(
        sum_kernel,
        [((PROBES, ROWS), F32), ((1, 128), F32)],
        [VMEM] * 2,
        [pltpu.VMEM((2 * PROBES, ROWS), F32)],
    )(block, index)
    return projected, moments, mark[0, 0]


def exchange(rows):
    return lax.all_to_all(rows, ALL, 0, 0, tiled=True)


def whole(probes, dosages, weights, send_rows, tile_src, tile_gene):
    rows_sent = send_rows[0]
    high = lax.Precision.HIGHEST
    outgoing = probes.T[rows_sent].reshape(DEV, SLOTS * PROBES // 128, 128)
    incoming = exchange(outgoing).reshape(SRC, PROBES)
    fetched = jnp.concatenate([incoming, jnp.zeros((1, PROBES), F32)], axis=0)
    slab = fetched[tile_src]
    tile_scores = jnp.einsum("tcb,tvc->tbv", slab, dosages, precision=high, preferred_element_type=F32)
    member = (tile_gene[None, :] == jnp.arange(GENES, dtype=I32)[:, None]).astype(F32)
    scores = jnp.einsum("gt,tbv->gbv", member, tile_scores, precision=high) * weights[:, None, :]
    one = jnp.sum(scores * scores, axis=2) / VT
    weighted = jnp.einsum("gt,gbv->tbv", member, scores * weights[:, None, :], precision=high)
    returned = jnp.einsum("tbv,tvc->tcb", weighted, dosages, precision=high, preferred_element_type=F32)
    two = jnp.dot(member, jnp.sum(returned * returned, axis=1), precision=high) / TILE
    sums = jax.ops.segment_sum(returned.reshape(-1, PROBES), tile_src.reshape(-1), num_segments=SRC + 1)
    arrived = exchange(sums[:SRC].reshape(DEV, SLOTS * PROBES // 128, 128))
    projected = jax.ops.segment_sum(
        arrived.reshape(SRC, PROBES), rows_sent.reshape(-1), num_segments=ROWS
    ).T
    return projected, jnp.stack([one, two], axis=1)


def shards(*args):
    projected, moments, mark = packed(*args)
    projected, moments = lax.cond(mark > 0.5, lambda: whole(*args), lambda: (projected, moments))
    return projected, moments.transpose(1, 2, 0)


def solution(mesh):
    fine = Mesh(mesh.devices.reshape(NY, NZ, NC, NX), ALL)
    placed = (P(None, ALL), P(ALL, None, None), P(ALL, None), P(ALL, None, None), P(ALL, None), P(ALL))
    return jax.shard_map(
        shards,
        mesh=fine,
        in_specs=placed,
        out_specs=(P(None, ALL), P(None, None, ALL)),
        check_vma=False,
    )
```

```python
import jax
import jax.numpy as jnp
from jax import lax
from jax.experimental import pallas as pl
from jax.experimental.pallas import tpu as pltpu
from jax.sharding import Mesh, PartitionSpec as P

NY, NZ, NC, NX = 4, 16, 2, 4
PLANE = NY * NC * NX
DEV = NY * NZ * NC * NX
SLOTS = 24
LANE = 32
SRC = DEV * SLOTS
TILES = 40
TILE = 128
VT = 128
GENES = 20
GROUP = 4
GROUPS = TILES // GROUP
PROBES = 64
ROWS = 1024
ZB = 128
ZCAP = 2 * (ZB - 1)
PB = 96
PCAP = 2 * (PB - 1)
ZBUF = 280
PBUF = 216
HOLD = PLANE * 2 * PB
F32 = jnp.float32
BF16 = jnp.bfloat16
I32 = jnp.int32
ALL = ("y", "z", "c", "x")
FLAT = ("y", "c", "x")


def iota(shape, dim):
    return lax.broadcasted_iota(I32, shape, dim)


def dot(a, b, ca=1, cb=0, **kw):
    return lax.dot_general(a, b, (((ca,), (cb,)), ((), ())), preferred_element_type=F32, **kw)


def ones_where(mask):
    return jnp.where(mask, 1.0, 0.0).astype(BF16)


def ones16(mask):
    return jnp.where(mask, jnp.ones((), BF16), jnp.zeros((), BF16))


def short(v):
    return v.astype(I32).astype(jnp.int16)


def lanes64(shape):
    return iota(shape, 1) < PROBES


def split(v):
    high = v.astype(BF16)
    return jnp.concatenate([high, (v - high.astype(F32)).astype(BF16)], axis=0)


def both(block):
    turned = pltpu.roll(block, PROBES, 1)
    left = lanes64(block.shape)
    return jnp.where(left, block, turned), jnp.where(left, turned, block)


def source_parts(ref, t, n):
    highs, lows, empties = [], [], []
    for i in range(n):
        p = ref[pl.ds(t * n + i, 1), :]
        o = (p * 43691) >> 20
        highs.append(((o >> 7) * (NC * NX) + (o & 7)) * 4 + ((o >> 5) & 3))
        lows.append(((o >> 3) & 3) * LANE + p - o * SLOTS)
        empties.append(p >= SRC)
    return highs, lows, empties


def one_hots(rows):
    return jnp.concatenate([ones16(iota((128, 128), 0).astype(jnp.int16) == r.astype(jnp.int16)) for r in rows], axis=1)


def place_kernel(src_ref, count_ref, addr_ref, again_ref):
    count = count_ref[...]
    again_ref[0, 0] = jnp.where(jnp.max(count) > 1.5, 1, 0)
    used = ones_where(count > 0.5)
    row, col = iota((128, 128), 0), iota((128, 128), 1)
    before = dot(used, ones_where(row < col))
    number = dot(used, jnp.ones((128, 128), BF16)).astype(BF16)
    earlier = ones_where(((row >> 2) == (col >> 2)) & (col < row))
    rank = jnp.minimum((dot(earlier, number) + before).astype(I32), PCAP)
    place = (row >> 2) * (2 * PB) + rank + jnp.where(rank >= PB - 1, 1, 0)
    turned = jnp.transpose(place)
    high = turned >> 6
    table = jnp.concatenate([high, turned - (high << 6)], axis=0).astype(F32).astype(BF16)

    def step(t, carry):
        highs, lows, empties = source_parts(src_ref, t, 8)
        found = dot(table, one_hots(highs))
        for i in range(8):
            part = found[:, i * 128 : (i + 1) * 128]
            value = part[:128] * 64.0 + part[128:]
            value = jnp.sum(jnp.where(row == lows[i], value, 0.0), axis=0, keepdims=True)
            addr_ref[pl.ds(t * 8 + i, 1), :] = jnp.where(empties[i], HOLD, value.astype(I32))
        return carry

    lax.fori_loop(0, TILES // 8, step, 0)


def meet_kernel(in_ref, out_ref):
    block = iota((8, 128), 1) >> 5
    for high in range(4):
        parts = [in_ref[pl.ds(x * 4 + high, 8, stride=16), :] for x in range(NX)]
        for low in range(4):
            turned = [pltpu.roll(parts[x], ((x - low) * LANE) % 128, 1) for x in range(NX)]
            result = turned[0]
            for x in range(1, NX):
                result = jnp.where(block == x, turned[x], result)
            out_ref[high * 4 + low] = result


def table_kernel(in_ref, weight_ref, table_ref, mark_ref, spread_ref):
    used = ones_where(in_ref[...] > 0.5)
    row, col = iota((128, 128), 0), iota((128, 128), 1)
    segment = dot(used, ones_where((row >> 5) == (col >> 5)))
    whole_row = dot(used, jnp.ones((128, 128), BF16))
    before = dot(used, ones_where((row >> 5) < (col >> 5)))
    owner = dot(ones_where(((row & 3) == (col & 3)) & (col < row)), segment.astype(BF16))
    holder = before + dot(ones_where(((row >> 2) == (col >> 2)) & (col < row)), whole_row.astype(BF16))
    over = jnp.maximum(
        jnp.where(owner + segment > ZCAP, 1.0, 0.0), jnp.where(holder + segment > PCAP, 1.0, 0.0)
    )
    mark_ref[...] = jnp.broadcast_to(jnp.max(over), (1, 128))
    owner = jnp.minimum(owner, float(ZCAP)).astype(I32) + ((row & 3) * 4 + (col >> 5)) * ZBUF
    holder = jnp.minimum(holder, float(PCAP + 1)).astype(I32) + (row >> 2) * PBUF
    table_ref[...] = jnp.where((col & 1) == 0, owner, holder)
    for k in range(GENES):
        spread_ref[k] = jnp.transpose(jnp.broadcast_to(weight_ref[pl.ds(k, 1), :], (128, VT)))


def ready_kernel(
    src_ref, rows_ref, probes_ref, used_ref, count_ref, value_ref, parts_ref, turned_ref
):
    count = jnp.zeros((128, 128), F32)
    for t in range(TILES // 8):
        highs, lows, _ = source_parts(src_ref, t, 8)
        count += dot(one_hots(highs), one_hots(lows), 1, 1)
    count_ref[...] = count
    used_ref[...] = jnp.minimum(count, 1.0)
    col = iota((128, 128), 1)
    high = probes_ref[...].astype(BF16).astype(F32)
    parts_ref[...] = jnp.concatenate([high, probes_ref[...] - high], axis=0).astype(BF16)
    turned_ref[...] = jnp.zeros_like(turned_ref)
    for k in range(DEV // 128):
        turned_ref[pl.ds(k * 128, 128), pl.ds(0, SLOTS)] = jnp.transpose(rows_ref[:, pl.ds(k * 128, 128)])
    value = turned_ref[pl.ds(0, 128, stride=NX), :]
    for x in range(1, NX):
        turned = pltpu.roll(turned_ref[pl.ds(x, 128, stride=NX), :], x * LANE, 1)
        value = jnp.where((col >> 5) == x, turned, value)
    value_ref[...] = value + 1


def send_kernel(used_ref, value_ref, parts_ref, out_ref, index_ref, high_ref, low_ref, done, sem):
    used = used_ref[...]
    flag = ones_where(used > 0.5)
    row, col = iota((128, 128), 0), iota((128, 128), 1)
    number = dot(flag, jnp.ones((128, 128), BF16))
    start = dot(ones_where(((row >> 3) == (col >> 3)) & (col < row)), number.astype(BF16))
    place = (start + dot(flag, ones_where(row < col))).astype(I32)
    place = place + jnp.where(place >= ZB - 1, 1, 0)
    high_ref[...] = jnp.where(used > 0.5, place >> 7, -1)
    low_ref[...] = place & (ZB - 1)
    which = iota((8, 128), 0)
    at = iota((ZB, 128), 0).astype(jnp.int16)
    subject = (iota((ROWS, 4 * ZB), 0) + 1).astype(jnp.int16)

    def list_of(z):
        values, places = [], []
        for y in range(NY):
            for c in range(NC):
                i = z * (NY * NC) + y * NC + c
                value = value_ref[pl.ds(y * (NZ * NC) + z * NC + c, 1), :]
                digit = jnp.where(which < 2, value >> 5, value & 31)
                match = ((which & 1) == high_ref[pl.ds(i, 1), :]) & (which < 4)
                values.append(jnp.where(match, digit, 0).astype(F32).astype(BF16))
                places.append(ones16(at == low_ref[pl.ds(i, 1), :].astype(jnp.int16)))
        listed = dot(jnp.concatenate(values, axis=1), jnp.concatenate(places, axis=1), 1, 1)
        index = listed[:2] * 32.0 + listed[2:4]
        index = jnp.concatenate([index[:1], index[1:]], axis=1)
        index_ref[pl.ds(z, 1), :] = index
        return index

    def lists_of(i):
        return jnp.concatenate([list_of(2 * i), list_of(2 * i + 1)], axis=1)

    def step(i, index):
        later = lists_of(jnp.minimum(i + 1, NZ // 2 - 1))
        rows = dot(parts_ref[...], ones16(subject == short(index)))
        rows = rows[:PROBES] + rows[PROBES:]
        for n in range(2):
            left, right = rows[:, 2 * n * ZB : (2 * n + 1) * ZB], rows[:, (2 * n + 1) * ZB : (2 * n + 2) * ZB]
            done[2 * i + n] = jnp.transpose(jnp.concatenate([left, right], axis=0))
        leave(i).start()
        return later

    def leave(i):
        part = pl.ds(2 * i, 2)
        return pltpu.make_async_copy(done.at[part], out_ref.at[part], sem.at[i])

    lax.fori_loop(0, NZ // 2, step, lists_of(0), unroll=2)
    for i in range(NZ // 2):
        leave(i).wait()


def relay_kernel(table, mark_ref, in_ref, out_ref, zbuf, pbuf, done, sem):
    for z in range(NZ):
        left, right = both(in_ref[z])
        zbuf[pl.ds(z * ZBUF, ZB), :] = left
        zbuf[pl.ds(z * ZBUF + ZB - 1, ZB), :] = right
    left = lanes64((PB, 128))
    copies = []
    for r in range(PLANE):
        for z in range(NZ):
            row, col = r * 4 + z // 4, (z % 4) * LANE
            pbuf[pl.ds(table[row, col + 1], SLOTS), :] = zbuf[pl.ds(table[row, col], SLOTS), :]
        done[r] = jnp.where(left, pbuf[pl.ds(r * PBUF, PB), :], pbuf[pl.ds(r * PBUF + PB - 1, PB), :])
        done[r, pl.ds(PB - 1, 1), :] = mark_ref[...]
        if r % 8 == 7:
            part = pl.ds(r - 7, 8)
            copies.append(pltpu.make_async_copy(done.at[part], out_ref.at[part], sem.at[r // 8]))
            copies[-1].start()
    for copy in copies:
        copy.wait()


def back_kernel(table, in_ref, out_ref, zbuf, pbuf, done, sem):
    mark = jnp.zeros((1, 128), F32)
    for r in range(PLANE):
        left, right = both(in_ref[r])
        pbuf[pl.ds(r * PBUF, PB), :] = left
        pbuf[pl.ds(r * PBUF + PB - 1, PB), :] = right
        mark = jnp.maximum(mark, in_ref[r, pl.ds(PB - 1, 1), :])
    left = lanes64((ZB, 128))
    copies = []
    for z in range(NZ):
        for r in range(PLANE):
            row, col = r * 4 + z // 4, (z % 4) * LANE
            zbuf[pl.ds(table[row, col], SLOTS), :] = pbuf[pl.ds(table[row, col + 1], SLOTS), :]
        done[z] = jnp.where(left, zbuf[pl.ds(z * ZBUF, ZB), :], zbuf[pl.ds(z * ZBUF + ZB - 1, ZB), :])
        done[z, pl.ds(ZB - 1, 1), :] = mark
        if z % 4 == 3:
            part = pl.ds(z - 3, 4)
            copies.append(pltpu.make_async_copy(done.at[part], out_ref.at[part], sem.at[z // 4]))
            copies[-1].start()
    for copy in copies:
        copy.wait()


def gene_kernel(
    addr,
    again,
    gene,
    addr_ref,
    in_ref,
    dose_ref,
    turned_ref,
    weight_ref,
    out_ref,
    moment_ref,
    held,
    total,
    weighted,
    work,
    near,
    done,
    sem,
    out_sem,
):
    def fetch(group, slot):
        return pltpu.make_async_copy(
            addr_ref.at[pl.ds(lax.rem(group, GROUPS) * GROUP, GROUP), :], near.at[slot], sem.at[slot]
        )

    fetch(0, 0).start()
    fetch(1, 1).start()
    mark = jnp.zeros((1, 128), F32)
    for m in range(PLANE):
        left, right = both(in_ref[m])
        held[pl.ds(m * 2 * PB, PB), :] = left
        held[pl.ds(m * 2 * PB + PB, PB), :] = right
        mark = jnp.maximum(mark, in_ref[m, pl.ds(PB - 1, 1), :])
    held[pl.ds(HOLD, 8), :] = jnp.zeros((8, 128), F32)
    total[...] = jnp.zeros_like(total)
    moment_ref[...] = jnp.zeros_like(moment_ref)

    def gather(slot, k):
        for c in range(TILE):
            work[k % 2, pl.ds(c, 1), :] = held[pl.ds(near[slot, k, c], 1), :]

    def score(t, k):
        dose = dose_ref[t]
        total[gene[t]] += dot(jnp.concatenate([dose, dose], axis=1), split(work[k % 2]))

    def scored(i, carry):
        for slot in range(2):
            group = i * 2 + slot
            fetch(group, slot).wait()
            for k in range(GROUP):
                gather(slot, k)
                score(jnp.maximum(group * GROUP + k - 1, 0), k + 1)
            fetch(group + 2, slot).start()
        return carry

    work[1] = jnp.zeros((TILE, 128), F32)
    lax.fori_loop(0, GROUPS // 2, scored, 0)
    score(TILES - 1, 1)
    for k in range(GENES):
        weight = weight_ref[k]
        scores = total[k] * weight
        one = jnp.sum(scores * scores, axis=0, keepdims=True) * (1.0 / VT)
        moment_ref[k, pl.ds(0, 1), :] = one[:, :PROBES]
        weighted[k] = split(scores * weight)

    def returned(t, slot):
        scale = jnp.where(t < TILES, 1.0 / TILE, 0.0)
        t = jnp.minimum(t, TILES - 1)
        dose = turned_ref[t]
        rows = dot(jnp.concatenate([dose, dose], axis=1), weighted[gene[t]])
        two = jnp.sum(rows * rows, axis=0, keepdims=True) * scale
        moment_ref[gene[t], pl.ds(1, 1), :] += two[:, :PROBES]
        work[slot] = rows

    def scatter(slot, k):
        for c in range(TILE):
            held[pl.ds(near[slot, k, c], 1), :] = work[k % 2, pl.ds(c, 1), :]

    @pl.when(again[0, 0] == 0)
    def _():
        def sent(i, carry):
            for slot in range(2):
                group = i * 2 + slot
                fetch(group, slot).wait()
                for k in range(GROUP):
                    returned(group * GROUP + k + 1, (k + 1) % 2)
                    scatter(slot, k)
                fetch(group + 2, slot).start()
            return carry

        returned(0, 0)
        lax.fori_loop(0, GROUPS // 2, sent, 0)

    @pl.when(again[0, 0] != 0)
    def _():
        held[...] = jnp.zeros_like(held)

        def summed(t, carry):
            returned(t, 0)

            def add(c, inner):
                held[pl.ds(addr[t, c], 1), :] += work[0, pl.ds(c, 1), :]
                return inner

            lax.fori_loop(0, TILE, add, 0)
            return carry

        lax.fori_loop(0, TILES, summed, 0)

    fetch(0, 0).wait()
    fetch(1, 1).wait()
    left = lanes64((PB, 128))
    copies = []
    for m in range(PLANE):
        done[m] = jnp.where(left, held[pl.ds(m * 2 * PB, PB), :], held[pl.ds(m * 2 * PB + PB, PB), :])
        done[m, pl.ds(PB - 1, 1), :] = mark
        if m % 8 == 7:
            part = pl.ds(m - 7, 8)
            copies.append(pltpu.make_async_copy(done.at[part], out_ref.at[part], out_sem.at[m // 8]))
            copies[-1].start()
    for copy in copies:
        copy.wait()


def sum_kernel(in_ref, index_ref, out_ref, mark_ref, total):
    at = (iota((ROWS, 8 * ZB), 0) + 1).astype(jnp.int16)

    def step(i, mark):
        rows, indices = [], []
        for n in range(4):
            z = i * 4 + n
            turned = jnp.transpose(in_ref[z])
            rows += [turned[:PROBES], turned[PROBES:]]
            indices.append(index_ref[pl.ds(z, 1), :])
            mark = jnp.maximum(mark, in_ref[z, pl.ds(ZB - 1, 1), :])
        index = jnp.concatenate(indices, axis=1)
        rows = jnp.where(index > 0.5, jnp.concatenate(rows, axis=1), 0.0)
        high = rows.astype(BF16).astype(F32)
        parts = jnp.concatenate([high, rows - high], axis=0).astype(BF16)
        sums = dot(parts, ones16(at == short(index)), 1, 1)
        total[...] = sums if i == 0 else total[...] + sums
        return mark

    mark = jnp.zeros((1, 128), F32)
    for i in range(NZ // 4):
        mark = step(i, mark)
    mark_ref[...] = mark
    out_ref[...] = total[pl.ds(0, PROBES), :] + total[pl.ds(PROBES, PROBES), :]


def turn_kernel(dose_ref, out_ref):
    def step(t, carry):
        out_ref[t] = jnp.transpose(dose_ref[t].astype(F32)).astype(BF16)
        return carry

    lax.fori_loop(0, TILES, step, 0)


VMEM = pl.BlockSpec(memory_space=pltpu.VMEM)
SMEM = pl.BlockSpec(memory_space=pltpu.SMEM)
HBM = pl.BlockSpec(memory_space=pl.ANY)


def call(kernel, outs, ins, scratch=(), out_specs=None, cost=2_000_000, limit=24):
    shapes = [jax.ShapeDtypeStruct(*o) for o in outs]
    return pl.pallas_call(
        kernel,
        out_shape=shapes,
        in_specs=ins,
        out_specs=[VMEM] * len(shapes) if out_specs is None else out_specs,
        scratch_shapes=list(scratch),
        cost_estimate=pl.CostEstimate(flops=cost * 100, bytes_accessed=cost, transcendentals=0),
        compiler_params=pltpu.CompilerParams(vmem_limit_bytes=limit << 20),
    )


def packed(probes, dosages, weights, send_rows, tile_src, tile_gene):
    zdone, pdone = [pltpu.VMEM((NZ, ZB, 128), F32)], [pltpu.VMEM((PLANE, PB, 128), F32)]
    four = [pltpu.SemaphoreType.DMA((4,))]
    used, count, value, parts = call(
        ready_kernel,
        [((128, 128), F32), ((128, 128), F32), ((128, 128), I32), ((2 * PROBES, ROWS), BF16)],
        [VMEM] * 3,
        [pltpu.VMEM((DEV, 128), I32)],
    )(tile_src, send_rows[0].T, probes)
    asked = lax.all_to_all(used.reshape(PLANE, 4, 128), FLAT, 0, 0, tiled=True).reshape(128, 128)
    (met,) = call(meet_kernel, [((NZ, 8, 128), F32)], [VMEM])(asked)
    met = lax.all_to_all(met, "z", 0, 0, tiled=True).reshape(128, 128)
    asked, count, met, doses = lax.optimization_barrier((asked, count, met, dosages))
    (turned,) = call(turn_kernel, [((TILES, TILE, VT), BF16)], [VMEM])(doses)
    table, mark, spread = call(
        table_kernel, [((128, 128), I32), ((1, 128), F32), ((GENES, VT, 128), F32)], [VMEM] * 2
    )(asked, weights)
    addr, again = call(
        place_kernel, [((TILES, TILE), I32), ((1, 1), I32)], [VMEM, VMEM], out_specs=[VMEM, SMEM]
    )(tile_src, count)
    block, index = call(
        send_kernel,
        [((NZ, ZB, 128), F32), ((NZ, 2 * ZB), F32)],
        [VMEM] * 3,
        [pltpu.VMEM((128, 128), I32)] * 2 + zdone + [pltpu.SemaphoreType.DMA((NZ // 2,))],
        out_specs=[HBM, VMEM],
    )(met, value, parts)
    block = lax.all_to_all(block, "z", 0, 0, tiled=True)
    block, addr, again, spread, table, mark, turned = lax.optimization_barrier(
        (block, addr, again, spread, table, mark, turned)
    )
    buffers = [pltpu.VMEM((NZ * ZBUF, 128), F32), pltpu.VMEM((PLANE * PBUF, 128), F32)]
    (block,) = call(relay_kernel, [((PLANE, PB, 128), F32)], [SMEM, VMEM, VMEM], buffers + pdone + four, out_specs=[HBM])(
        table, mark, block
    )
    block = lax.all_to_all(block, FLAT, 0, 0, tiled=True)
    block, moments = call(
        gene_kernel,
        [((PLANE, PB, 128), F32), ((GENES, 2, PROBES), F32)],
        [SMEM] * 3 + [VMEM] * 5,
        [
            pltpu.VMEM((HOLD + 8, 128), F32),
            pltpu.VMEM((GENES, VT, 128), F32),
            pltpu.VMEM((GENES, 2 * VT, 128), BF16),
            pltpu.VMEM((2, TILE, 128), F32),
            pltpu.SMEM((2, GROUP, TILE), I32),
        ]
        + pdone
        + [pltpu.SemaphoreType.DMA((2,))]
        + four,
        out_specs=[HBM, VMEM],
    )(addr, again, tile_gene, addr, block, dosages, turned, spread)
    block = lax.all_to_all(block, FLAT, 0, 0, tiled=True)
    (block,) = call(
        back_kernel, [((NZ, ZB, 128), F32)], [SMEM, VMEM], buffers + zdone + four, out_specs=[HBM]
    )(table, block)
    block = lax.all_to_all(block, "z", 0, 0, tiled=True)
    projected, mark = call(
        sum_kernel,
        [((PROBES, ROWS), F32), ((1, 128), F32)],
        [VMEM] * 2,
        [pltpu.VMEM((2 * PROBES, ROWS), F32)],
    )(block, index)
    return projected, moments, mark[0, 0]


def exchange(rows):
    return lax.all_to_all(rows, ALL, 0, 0, tiled=True)


def whole(probes, dosages, weights, send_rows, tile_src, tile_gene):
    rows_sent = send_rows[0]
    high = lax.Precision.HIGHEST
    outgoing = probes.T[rows_sent].reshape(DEV, SLOTS * PROBES // 128, 128)
    incoming = exchange(outgoing).reshape(SRC, PROBES)
    fetched = jnp.concatenate([incoming, jnp.zeros((1, PROBES), F32)], axis=0)
    slab = fetched[tile_src]
    tile_scores = jnp.einsum("tcb,tvc->tbv", slab, dosages, precision=high, preferred_element_type=F32)
    member = (tile_gene[None, :] == jnp.arange(GENES, dtype=I32)[:, None]).astype(F32)
    scores = jnp.einsum("gt,tbv->gbv", member, tile_scores, precision=high) * weights[:, None, :]
    one = jnp.sum(scores * scores, axis=2) / VT
    weighted = jnp.einsum("gt,gbv->tbv", member, scores * weights[:, None, :], precision=high)
    returned = jnp.einsum("tbv,tvc->tcb", weighted, dosages, precision=high, preferred_element_type=F32)
    two = jnp.dot(member, jnp.sum(returned * returned, axis=1), precision=high) / TILE
    sums = jax.ops.segment_sum(returned.reshape(-1, PROBES), tile_src.reshape(-1), num_segments=SRC + 1)
    arrived = exchange(sums[:SRC].reshape(DEV, SLOTS * PROBES // 128, 128))
    projected = jax.ops.segment_sum(
        arrived.reshape(SRC, PROBES), rows_sent.reshape(-1), num_segments=ROWS
    ).T
    return projected, jnp.stack([one, two], axis=1)


def shards(*args):
    projected, moments, mark = packed(*args)
    projected, moments = lax.cond(mark > 0.5, lambda: whole(*args), lambda: (projected, moments))
    return projected, moments.transpose(1, 2, 0)


def solution(mesh):
    fine = Mesh(mesh.devices.reshape(NY, NZ, NC, NX), ALL)
    placed = (P(None, ALL), P(ALL, None, None), P(ALL, None), P(ALL, None, None), P(ALL, None), P(ALL))
    return jax.shard_map(
        shards,
        mesh=fine,
        in_specs=placed,
        out_specs=(P(None, ALL), P(None, None, ALL)),
        check_vma=False,
    )
```

```python
import jax
import jax.numpy as jnp
from jax import lax
from jax.experimental import pallas as pl
from jax.experimental.pallas import tpu as pltpu
from jax.sharding import Mesh, PartitionSpec as P

NY, NZ, NC, NX = 4, 16, 2, 4
PLANE = NY * NC * NX
DEV = NY * NZ * NC * NX
SLOTS = 24
LANE = 32
SRC = DEV * SLOTS
TILES = 40
TILE = 128
VT = 128
GENES = 20
GROUP = 4
GROUPS = TILES // GROUP
PROBES = 64
ROWS = 1024
ZB = 128
ZCAP = 2 * (ZB - 1)
PB = 96
PCAP = 2 * (PB - 1)
ZBUF = 280
PBUF = 216
HOLD = PLANE * 2 * PB
F32 = jnp.float32
BF16 = jnp.bfloat16
I32 = jnp.int32
ALL = ("y", "z", "c", "x")
FLAT = ("y", "c", "x")


def iota(shape, dim):
    return lax.broadcasted_iota(I32, shape, dim)


def dot(a, b, ca=1, cb=0, **kw):
    return lax.dot_general(a, b, (((ca,), (cb,)), ((), ())), preferred_element_type=F32, **kw)


def ones_where(mask):
    return jnp.where(mask, 1.0, 0.0).astype(BF16)


def ones16(mask):
    return jnp.where(mask, jnp.ones((), BF16), jnp.zeros((), BF16))


def short(v):
    return v.astype(I32).astype(jnp.int16)


def lanes64(shape):
    return iota(shape, 1) < PROBES


def split(v):
    high = v.astype(BF16)
    return jnp.concatenate([high, (v - high.astype(F32)).astype(BF16)], axis=0)


def both(block):
    turned = pltpu.roll(block, PROBES, 1)
    left = lanes64(block.shape)
    return jnp.where(left, block, turned), jnp.where(left, turned, block)


def source_parts(ref, t, n):
    highs, lows, empties = [], [], []
    for i in range(n):
        p = ref[pl.ds(t * n + i, 1), :]
        o = (p * 43691) >> 20
        highs.append(((o >> 7) * (NC * NX) + (o & 7)) * 4 + ((o >> 5) & 3))
        lows.append(((o >> 3) & 3) * LANE + p - o * SLOTS)
        empties.append(p >= SRC)
    return highs, lows, empties


def one_hots(rows):
    return jnp.concatenate([ones16(iota((128, 128), 0).astype(jnp.int16) == r.astype(jnp.int16)) for r in rows], axis=1)


def place_kernel(src_ref, count_ref, addr_ref, again_ref):
    count = count_ref[...]
    again_ref[0, 0] = jnp.where(jnp.max(count) > 1.5, 1, 0)
    used = ones_where(count > 0.5)
    row, col = iota((128, 128), 0), iota((128, 128), 1)
    before = dot(used, ones_where(row < col))
    number = dot(used, jnp.ones((128, 128), BF16)).astype(BF16)
    earlier = ones_where(((row >> 2) == (col >> 2)) & (col < row))
    rank = jnp.minimum((dot(earlier, number) + before).astype(I32), PCAP)
    place = (row >> 2) * (2 * PB) + rank + jnp.where(rank >= PB - 1, 1, 0)
    turned = jnp.transpose(place)
    high = turned >> 6
    table = jnp.concatenate([high, turned - (high << 6)], axis=0).astype(F32).astype(BF16)

    def step(t, carry):
        highs, lows, empties = source_parts(src_ref, t, 8)
        found = dot(table, one_hots(highs))
        for i in range(8):
            part = found[:, i * 128 : (i + 1) * 128]
            value = part[:128] * 64.0 + part[128:]
            value = jnp.sum(jnp.where(row == lows[i], value, 0.0), axis=0, keepdims=True)
            addr_ref[pl.ds(t * 8 + i, 1), :] = jnp.where(empties[i], HOLD, value.astype(I32))
        return carry

    lax.fori_loop(0, TILES // 8, step, 0)


def meet_kernel(in_ref, out_ref):
    block = iota((8, 128), 1) >> 5
    for high in range(4):
        parts = [in_ref[pl.ds(x * 4 + high, 8, stride=16), :] for x in range(NX)]
        for low in range(4):
            turned = [pltpu.roll(parts[x], ((x - low) * LANE) % 128, 1) for x in range(NX)]
            result = turned[0]
            for x in range(1, NX):
                result = jnp.where(block == x, turned[x], result)
            out_ref[high * 4 + low] = result


def table_kernel(in_ref, weight_ref, table_ref, mark_ref, spread_ref):
    used = ones_where(in_ref[...] > 0.5)
    row, col = iota((128, 128), 0), iota((128, 128), 1)
    segment = dot(used, ones_where((row >> 5) == (col >> 5)))
    whole_row = dot(used, jnp.ones((128, 128), BF16))
    before = dot(used, ones_where((row >> 5) < (col >> 5)))
    owner = dot(ones_where(((row & 3) == (col & 3)) & (col < row)), segment.astype(BF16))
    holder = before + dot(ones_where(((row >> 2) == (col >> 2)) & (col < row)), whole_row.astype(BF16))
    over = jnp.maximum(
        jnp.where(owner + segment > ZCAP, 1.0, 0.0), jnp.where(holder + segment > PCAP, 1.0, 0.0)
    )
    mark_ref[...] = jnp.broadcast_to(jnp.max(over), (1, 128))
    owner = jnp.minimum(owner, float(ZCAP)).astype(I32) + ((row & 3) * 4 + (col >> 5)) * ZBUF
    holder = jnp.minimum(holder, float(PCAP + 1)).astype(I32) + (row >> 2) * PBUF
    table_ref[...] = jnp.where((col & 1) == 0, owner, holder)
    for k in range(GENES):
        spread_ref[k] = jnp.transpose(jnp.broadcast_to(weight_ref[pl.ds(k, 1), :], (128, VT)))


def ready_kernel(
    src_ref, rows_ref, probes_ref, used_ref, count_ref, value_ref, parts_ref, turned_ref
):
    count = jnp.zeros((128, 128), F32)
    for t in range(TILES // 8):
        highs, lows, _ = source_parts(src_ref, t, 8)
        count += dot(one_hots(highs), one_hots(lows), 1, 1)
    count_ref[...] = count
    used_ref[...] = jnp.minimum(count, 1.0)
    col = iota((128, 128), 1)
    high = probes_ref[...].astype(BF16).astype(F32)
    parts_ref[...] = jnp.concatenate([high, probes_ref[...] - high], axis=0).astype(BF16)
    turned_ref[...] = jnp.zeros_like(turned_ref)
    for k in range(DEV // 128):
        turned_ref[pl.ds(k * 128, 128), pl.ds(0, SLOTS)] = jnp.transpose(rows_ref[:, pl.ds(k * 128, 128)])
    value = turned_ref[pl.ds(0, 128, stride=NX), :]
    for x in range(1, NX):
        turned = pltpu.roll(turned_ref[pl.ds(x, 128, stride=NX), :], x * LANE, 1)
        value = jnp.where((col >> 5) == x, turned, value)
    value_ref[...] = value + 1


def send_kernel(used_ref, value_ref, parts_ref, out_ref, index_ref, high_ref, low_ref, done, sem):
    used = used_ref[...]
    flag = ones_where(used > 0.5)
    row, col = iota((128, 128), 0), iota((128, 128), 1)
    number = dot(flag, jnp.ones((128, 128), BF16))
    start = dot(ones_where(((row >> 3) == (col >> 3)) & (col < row)), number.astype(BF16))
    place = (start + dot(flag, ones_where(row < col))).astype(I32)
    place = place + jnp.where(place >= ZB - 1, 1, 0)
    high_ref[...] = jnp.where(used > 0.5, place >> 7, -1)
    low_ref[...] = place & (ZB - 1)
    which = iota((8, 128), 0)
    at = iota((ZB, 128), 0).astype(jnp.int16)
    subject = (iota((ROWS, 4 * ZB), 0) + 1).astype(jnp.int16)

    def list_of(z):
        values, places = [], []
        for y in range(NY):
            for c in range(NC):
                i = z * (NY * NC) + y * NC + c
                value = value_ref[pl.ds(y * (NZ * NC) + z * NC + c, 1), :]
                digit = jnp.where(which < 2, value >> 5, value & 31)
                match = ((which & 1) == high_ref[pl.ds(i, 1), :]) & (which < 4)
                values.append(jnp.where(match, digit, 0).astype(F32).astype(BF16))
                places.append(ones16(at == low_ref[pl.ds(i, 1), :].astype(jnp.int16)))
        listed = dot(jnp.concatenate(values, axis=1), jnp.concatenate(places, axis=1), 1, 1)
        index = listed[:2] * 32.0 + listed[2:4]
        index = jnp.concatenate([index[:1], index[1:]], axis=1)
        index_ref[pl.ds(z, 1), :] = index
        return index

    def lists_of(i):
        return jnp.concatenate([list_of(2 * i), list_of(2 * i + 1)], axis=1)

    def step(i, index):
        later = lists_of(jnp.minimum(i + 1, NZ // 2 - 1))
        rows = dot(parts_ref[...], ones16(subject == short(index)))
        rows = rows[:PROBES] + rows[PROBES:]
        for n in range(2):
            left, right = rows[:, 2 * n * ZB : (2 * n + 1) * ZB], rows[:, (2 * n + 1) * ZB : (2 * n + 2) * ZB]
            done[2 * i + n] = jnp.transpose(jnp.concatenate([left, right], axis=0))
        leave(i).start()
        return later

    def leave(i):
        part = pl.ds(2 * i, 2)
        return pltpu.make_async_copy(done.at[part], out_ref.at[part], sem.at[i])

    lax.fori_loop(0, NZ // 2, step, lists_of(0), unroll=4)
    for i in range(NZ // 2):
        leave(i).wait()


def relay_kernel(table, mark_ref, in_ref, out_ref, zbuf, pbuf, done, sem):
    for z in range(NZ):
        left, right = both(in_ref[z])
        zbuf[pl.ds(z * ZBUF, ZB), :] = left
        zbuf[pl.ds(z * ZBUF + ZB - 1, ZB), :] = right
    left = lanes64((PB, 128))
    copies = []
    for r in range(PLANE):
        for z in range(NZ):
            row, col = r * 4 + z // 4, (z % 4) * LANE
            pbuf[pl.ds(table[row, col + 1], SLOTS), :] = zbuf[pl.ds(table[row, col], SLOTS), :]
        done[r] = jnp.where(left, pbuf[pl.ds(r * PBUF, PB), :], pbuf[pl.ds(r * PBUF + PB - 1, PB), :])
        done[r, pl.ds(PB - 1, 1), :] = mark_ref[...]
        if r % 8 == 7:
            part = pl.ds(r - 7, 8)
            copies.append(pltpu.make_async_copy(done.at[part], out_ref.at[part], sem.at[r // 8]))
            copies[-1].start()
    for copy in copies:
        copy.wait()


def back_kernel(table, in_ref, out_ref, zbuf, pbuf, done, sem):
    mark = jnp.zeros((1, 128), F32)
    for r in range(PLANE):
        left, right = both(in_ref[r])
        pbuf[pl.ds(r * PBUF, PB), :] = left
        pbuf[pl.ds(r * PBUF + PB - 1, PB), :] = right
        mark = jnp.maximum(mark, in_ref[r, pl.ds(PB - 1, 1), :])
    left = lanes64((ZB, 128))
    copies = []
    for z in range(NZ):
        for r in range(PLANE):
            row, col = r * 4 + z // 4, (z % 4) * LANE
            zbuf[pl.ds(table[row, col], SLOTS), :] = pbuf[pl.ds(table[row, col + 1], SLOTS), :]
        done[z] = jnp.where(left, zbuf[pl.ds(z * ZBUF, ZB), :], zbuf[pl.ds(z * ZBUF + ZB - 1, ZB), :])
        done[z, pl.ds(ZB - 1, 1), :] = mark
        if z % 4 == 3:
            part = pl.ds(z - 3, 4)
            copies.append(pltpu.make_async_copy(done.at[part], out_ref.at[part], sem.at[z // 4]))
            copies[-1].start()
    for copy in copies:
        copy.wait()


def gene_kernel(
    addr,
    again,
    gene,
    addr_ref,
    in_ref,
    dose_ref,
    turned_ref,
    weight_ref,
    out_ref,
    moment_ref,
    held,
    total,
    weighted,
    work,
    near,
    done,
    sem,
    out_sem,
):
    def fetch(group, slot):
        return pltpu.make_async_copy(
            addr_ref.at[pl.ds(lax.rem(group, GROUPS) * GROUP, GROUP), :], near.at[slot], sem.at[slot]
        )

    fetch(0, 0).start()
    fetch(1, 1).start()
    mark = jnp.zeros((1, 128), F32)
    for m in range(PLANE):
        left, right = both(in_ref[m])
        held[pl.ds(m * 2 * PB, PB), :] = left
        held[pl.ds(m * 2 * PB + PB, PB), :] = right
        mark = jnp.maximum(mark, in_ref[m, pl.ds(PB - 1, 1), :])
    held[pl.ds(HOLD, 8), :] = jnp.zeros((8, 128), F32)
    total[...] = jnp.zeros_like(total)
    moment_ref[...] = jnp.zeros_like(moment_ref)

    def gather(slot, k):
        for c in range(TILE):
            work[k % 2, pl.ds(c, 1), :] = held[pl.ds(near[slot, k, c], 1), :]

    def score(t, k):
        dose = dose_ref[t]
        total[gene[t]] += dot(jnp.concatenate([dose, dose], axis=1), split(work[k % 2]))

    def scored(i, carry):
        for slot in range(2):
            group = i * 2 + slot
            fetch(group, slot).wait()
            for k in range(GROUP):
                gather(slot, k)
                score(jnp.maximum(group * GROUP + k - 1, 0), k + 1)
            fetch(group + 2, slot).start()
        return carry

    work[1] = jnp.zeros((TILE, 128), F32)
    lax.fori_loop(0, GROUPS // 2, scored, 0)
    score(TILES - 1, 1)
    for k in range(GENES):
        weight = weight_ref[k]
        scores = total[k] * weight
        one = jnp.sum(scores * scores, axis=0, keepdims=True) * (1.0 / VT)
        moment_ref[k, pl.ds(0, 1), :] = one[:, :PROBES]
        weighted[k] = split(scores * weight)

    def returned(t, slot):
        scale = jnp.where(t < TILES, 1.0 / TILE, 0.0)
        t = jnp.minimum(t, TILES - 1)
        dose = turned_ref[t]
        rows = dot(jnp.concatenate([dose, dose], axis=1), weighted[gene[t]])
        two = jnp.sum(rows * rows, axis=0, keepdims=True) * scale
        moment_ref[gene[t], pl.ds(1, 1), :] += two[:, :PROBES]
        work[slot] = rows

    def scatter(slot, k):
        for c in range(TILE):
            held[pl.ds(near[slot, k, c], 1), :] = work[k % 2, pl.ds(c, 1), :]

    @pl.when(again[0, 0] == 0)
    def _():
        def sent(i, carry):
            for slot in range(2):
                group = i * 2 + slot
                fetch(group, slot).wait()
                for k in range(GROUP):
                    returned(group * GROUP + k + 1, (k + 1) % 2)
                    scatter(slot, k)
                fetch(group + 2, slot).start()
            return carry

        returned(0, 0)
        lax.fori_loop(0, GROUPS // 2, sent, 0)

    @pl.when(again[0, 0] != 0)
    def _():
        held[...] = jnp.zeros_like(held)

        def summed(t, carry):
            returned(t, 0)

            def add(c, inner):
                held[pl.ds(addr[t, c], 1), :] += work[0, pl.ds(c, 1), :]
                return inner

            lax.fori_loop(0, TILE, add, 0)
            return carry

        lax.fori_loop(0, TILES, summed, 0)

    fetch(0, 0).wait()
    fetch(1, 1).wait()
    left = lanes64((PB, 128))
    copies = []
    for m in range(PLANE):
        done[m] = jnp.where(left, held[pl.ds(m * 2 * PB, PB), :], held[pl.ds(m * 2 * PB + PB, PB), :])
        done[m, pl.ds(PB - 1, 1), :] = mark
        if m % 8 == 7:
            part = pl.ds(m - 7, 8)
            copies.append(pltpu.make_async_copy(done.at[part], out_ref.at[part], out_sem.at[m // 8]))
            copies[-1].start()
    for copy in copies:
        copy.wait()


def sum_kernel(in_ref, index_ref, out_ref, mark_ref, total):
    at = (iota((ROWS, 8 * ZB), 0) + 1).astype(jnp.int16)

    def step(i, mark):
        rows, indices = [], []
        for n in range(4):
            z = i * 4 + n
            turned = jnp.transpose(in_ref[z])
            rows += [turned[:PROBES], turned[PROBES:]]
            indices.append(index_ref[pl.ds(z, 1), :])
            mark = jnp.maximum(mark, in_ref[z, pl.ds(ZB - 1, 1), :])
        index = jnp.concatenate(indices, axis=1)
        rows = jnp.where(index > 0.5, jnp.concatenate(rows, axis=1), 0.0)
        high = rows.astype(BF16).astype(F32)
        parts = jnp.concatenate([high, rows - high], axis=0).astype(BF16)
        sums = dot(parts, ones16(at == short(index)), 1, 1)
        total[...] = sums if i == 0 else total[...] + sums
        return mark

    mark = jnp.zeros((1, 128), F32)
    for i in range(NZ // 4):
        mark = step(i, mark)
    mark_ref[...] = mark
    out_ref[...] = total[pl.ds(0, PROBES), :] + total[pl.ds(PROBES, PROBES), :]


def turn_kernel(dose_ref, out_ref):
    def step(t, carry):
        out_ref[t] = jnp.transpose(dose_ref[t].astype(F32)).astype(BF16)
        return carry

    lax.fori_loop(0, TILES, step, 0)


VMEM = pl.BlockSpec(memory_space=pltpu.VMEM)
SMEM = pl.BlockSpec(memory_space=pltpu.SMEM)
HBM = pl.BlockSpec(memory_space=pl.ANY)


def call(kernel, outs, ins, scratch=(), out_specs=None, cost=2_000_000, limit=24):
    shapes = [jax.ShapeDtypeStruct(*o) for o in outs]
    return pl.pallas_call(
        kernel,
        out_shape=shapes,
        in_specs=ins,
        out_specs=[VMEM] * len(shapes) if out_specs is None else out_specs,
        scratch_shapes=list(scratch),
        cost_estimate=pl.CostEstimate(flops=cost * 100, bytes_accessed=cost, transcendentals=0),
        compiler_params=pltpu.CompilerParams(vmem_limit_bytes=limit << 20),
    )


def packed(probes, dosages, weights, send_rows, tile_src, tile_gene):
    zdone, pdone = [pltpu.VMEM((NZ, ZB, 128), F32)], [pltpu.VMEM((PLANE, PB, 128), F32)]
    four = [pltpu.SemaphoreType.DMA((4,))]
    used, count, value, parts = call(
        ready_kernel,
        [((128, 128), F32), ((128, 128), F32), ((128, 128), I32), ((2 * PROBES, ROWS), BF16)],
        [VMEM] * 3,
        [pltpu.VMEM((DEV, 128), I32)],
    )(tile_src, send_rows[0].T, probes)
    asked = lax.all_to_all(used.reshape(PLANE, 4, 128), FLAT, 0, 0, tiled=True).reshape(128, 128)
    (met,) = call(meet_kernel, [((NZ, 8, 128), F32)], [VMEM])(asked)
    met = lax.all_to_all(met, "z", 0, 0, tiled=True).reshape(128, 128)
    asked, count, met, doses = lax.optimization_barrier((asked, count, met, dosages))
    (turned,) = call(turn_kernel, [((TILES, TILE, VT), BF16)], [VMEM])(doses)
    table, mark, spread = call(
        table_kernel, [((128, 128), I32), ((1, 128), F32), ((GENES, VT, 128), F32)], [VMEM] * 2
    )(asked, weights)
    addr, again = call(
        place_kernel, [((TILES, TILE), I32), ((1, 1), I32)], [VMEM, VMEM], out_specs=[VMEM, SMEM]
    )(tile_src, count)
    block, index = call(
        send_kernel,
        [((NZ, ZB, 128), F32), ((NZ, 2 * ZB), F32)],
        [VMEM] * 3,
        [pltpu.VMEM((128, 128), I32)] * 2 + zdone + [pltpu.SemaphoreType.DMA((NZ // 2,))],
        out_specs=[HBM, VMEM],
    )(met, value, parts)
    block = lax.all_to_all(block, "z", 0, 0, tiled=True)
    block, addr, again, spread, table, mark, turned = lax.optimization_barrier(
        (block, addr, again, spread, table, mark, turned)
    )
    buffers = [pltpu.VMEM((NZ * ZBUF, 128), F32), pltpu.VMEM((PLANE * PBUF, 128), F32)]
    (block,) = call(relay_kernel, [((PLANE, PB, 128), F32)], [SMEM, VMEM, VMEM], buffers + pdone + four, out_specs=[HBM])(
        table, mark, block
    )
    block = lax.all_to_all(block, FLAT, 0, 0, tiled=True)
    block, moments = call(
        gene_kernel,
        [((PLANE, PB, 128), F32), ((GENES, 2, PROBES), F32)],
        [SMEM] * 3 + [VMEM] * 5,
        [
            pltpu.VMEM((HOLD + 8, 128), F32),
            pltpu.VMEM((GENES, VT, 128), F32),
            pltpu.VMEM((GENES, 2 * VT, 128), BF16),
            pltpu.VMEM((2, TILE, 128), F32),
            pltpu.SMEM((2, GROUP, TILE), I32),
        ]
        + pdone
        + [pltpu.SemaphoreType.DMA((2,))]
        + four,
        out_specs=[HBM, VMEM],
    )(addr, again, tile_gene, addr, block, dosages, turned, spread)
    block = lax.all_to_all(block, FLAT, 0, 0, tiled=True)
    (block,) = call(
        back_kernel, [((NZ, ZB, 128), F32)], [SMEM, VMEM], buffers + zdone + four, out_specs=[HBM]
    )(table, block)
    block = lax.all_to_all(block, "z", 0, 0, tiled=True)
    projected, mark = call(
        sum_kernel,
        [((PROBES, ROWS), F32), ((1, 128), F32)],
        [VMEM] * 2,
        [pltpu.VMEM((2 * PROBES, ROWS), F32)],
    )(block, index)
    return projected, moments, mark[0, 0]


def exchange(rows):
    return lax.all_to_all(rows, ALL, 0, 0, tiled=True)


def whole(probes, dosages, weights, send_rows, tile_src, tile_gene):
    rows_sent = send_rows[0]
    high = lax.Precision.HIGHEST
    outgoing = probes.T[rows_sent].reshape(DEV, SLOTS * PROBES // 128, 128)
    incoming = exchange(outgoing).reshape(SRC, PROBES)
    fetched = jnp.concatenate([incoming, jnp.zeros((1, PROBES), F32)], axis=0)
    slab = fetched[tile_src]
    tile_scores = jnp.einsum("tcb,tvc->tbv", slab, dosages, precision=high, preferred_element_type=F32)
    member = (tile_gene[None, :] == jnp.arange(GENES, dtype=I32)[:, None]).astype(F32)
    scores = jnp.einsum("gt,tbv->gbv", member, tile_scores, precision=high) * weights[:, None, :]
    one = jnp.sum(scores * scores, axis=2) / VT
    weighted = jnp.einsum("gt,gbv->tbv", member, scores * weights[:, None, :], precision=high)
    returned = jnp.einsum("tbv,tvc->tcb", weighted, dosages, precision=high, preferred_element_type=F32)
    two = jnp.dot(member, jnp.sum(returned * returned, axis=1), precision=high) / TILE
    sums = jax.ops.segment_sum(returned.reshape(-1, PROBES), tile_src.reshape(-1), num_segments=SRC + 1)
    arrived = exchange(sums[:SRC].reshape(DEV, SLOTS * PROBES // 128, 128))
    projected = jax.ops.segment_sum(
        arrived.reshape(SRC, PROBES), rows_sent.reshape(-1), num_segments=ROWS
    ).T
    return projected, jnp.stack([one, two], axis=1)


def shards(*args):
    projected, moments, mark = packed(*args)
    projected, moments = lax.cond(mark > 0.5, lambda: whole(*args), lambda: (projected, moments))
    return projected, moments.transpose(1, 2, 0)


def solution(mesh):
    fine = Mesh(mesh.devices.reshape(NY, NZ, NC, NX), ALL)
    placed = (P(None, ALL), P(ALL, None, None), P(ALL, None), P(ALL, None, None), P(ALL, None), P(ALL))
    return jax.shard_map(
        shards,
        mesh=fine,
        in_specs=placed,
        out_specs=(P(None, ALL), P(None, None, ALL)),
        check_vma=False,
    )
```

```python
import jax
import jax.numpy as jnp
from jax import lax
from jax.experimental import pallas as pl
from jax.experimental.pallas import tpu as pltpu
from jax.sharding import Mesh, PartitionSpec as P

NY, NZ, NC, NX = 4, 16, 2, 4
PLANE = NY * NC * NX
DEV = NY * NZ * NC * NX
SLOTS = 24
LANE = 32
SRC = DEV * SLOTS
TILES = 40
TILE = 128
VT = 128
GENES = 20
GROUP = 4
GROUPS = TILES // GROUP
PROBES = 64
ROWS = 1024
ZB = 128
ZCAP = 2 * (ZB - 1)
PB = 96
PCAP = 2 * (PB - 1)
ZBUF = 280
PBUF = 216
HOLD = PLANE * 2 * PB
F32 = jnp.float32
BF16 = jnp.bfloat16
I32 = jnp.int32
ALL = ("y", "z", "c", "x")
FLAT = ("y", "c", "x")


def iota(shape, dim):
    return lax.broadcasted_iota(I32, shape, dim)


def dot(a, b, ca=1, cb=0, **kw):
    return lax.dot_general(a, b, (((ca,), (cb,)), ((), ())), preferred_element_type=F32, **kw)


def ones_where(mask):
    return jnp.where(mask, 1.0, 0.0).astype(BF16)


def ones16(mask):
    return jnp.where(mask, jnp.ones((), BF16), jnp.zeros((), BF16))


def short(v):
    return v.astype(I32).astype(jnp.int16)


def lanes64(shape):
    return iota(shape, 1) < PROBES


def split(v):
    high = v.astype(BF16)
    return jnp.concatenate([high, (v - high.astype(F32)).astype(BF16)], axis=0)


def both(block):
    turned = pltpu.roll(block, PROBES, 1)
    left = lanes64(block.shape)
    return jnp.where(left, block, turned), jnp.where(left, turned, block)


def source_parts(ref, t, n):
    highs, lows, empties = [], [], []
    for i in range(n):
        p = ref[pl.ds(t * n + i, 1), :]
        o = (p * 43691) >> 20
        highs.append(((o >> 7) * (NC * NX) + (o & 7)) * 4 + ((o >> 5) & 3))
        lows.append(((o >> 3) & 3) * LANE + p - o * SLOTS)
        empties.append(p >= SRC)
    return highs, lows, empties


def one_hots(rows):
    return jnp.concatenate([ones16(iota((128, 128), 0).astype(jnp.int16) == r.astype(jnp.int16)) for r in rows], axis=1)


def place_kernel(src_ref, count_ref, addr_ref, again_ref):
    count = count_ref[...]
    again_ref[0, 0] = jnp.where(jnp.max(count) > 1.5, 1, 0)
    used = ones_where(count > 0.5)
    row, col = iota((128, 128), 0), iota((128, 128), 1)
    before = dot(used, ones_where(row < col))
    number = dot(used, jnp.ones((128, 128), BF16)).astype(BF16)
    earlier = ones_where(((row >> 2) == (col >> 2)) & (col < row))
    rank = jnp.minimum((dot(earlier, number) + before).astype(I32), PCAP)
    place = (row >> 2) * (2 * PB) + rank + jnp.where(rank >= PB - 1, 1, 0)
    turned = jnp.transpose(place)
    high = turned >> 6
    table = jnp.concatenate([high, turned - (high << 6)], axis=0).astype(F32).astype(BF16)

    def step(t, carry):
        highs, lows, empties = source_parts(src_ref, t, 8)
        found = dot(table, one_hots(highs))
        for i in range(8):
            part = found[:, i * 128 : (i + 1) * 128]
            value = part[:128] * 64.0 + part[128:]
            value = jnp.sum(jnp.where(row == lows[i], value, 0.0), axis=0, keepdims=True)
            addr_ref[pl.ds(t * 8 + i, 1), :] = jnp.where(empties[i], HOLD, value.astype(I32))
        return carry

    lax.fori_loop(0, TILES // 8, step, 0)


def meet_kernel(in_ref, out_ref):
    block = iota((8, 128), 1) >> 5
    for high in range(4):
        parts = [in_ref[pl.ds(x * 4 + high, 8, stride=16), :] for x in range(NX)]
        for low in range(4):
            turned = [pltpu.roll(parts[x], ((x - low) * LANE) % 128, 1) for x in range(NX)]
            result = turned[0]
            for x in range(1, NX):
                result = jnp.where(block == x, turned[x], result)
            out_ref[high * 4 + low] = result


def table_kernel(in_ref, weight_ref, table_ref, mark_ref, spread_ref):
    used = ones_where(in_ref[...] > 0.5)
    row, col = iota((128, 128), 0), iota((128, 128), 1)
    segment = dot(used, ones_where((row >> 5) == (col >> 5)))
    whole_row = dot(used, jnp.ones((128, 128), BF16))
    before = dot(used, ones_where((row >> 5) < (col >> 5)))
    owner = dot(ones_where(((row & 3) == (col & 3)) & (col < row)), segment.astype(BF16))
    holder = before + dot(ones_where(((row >> 2) == (col >> 2)) & (col < row)), whole_row.astype(BF16))
    over = jnp.maximum(
        jnp.where(owner + segment > ZCAP, 1.0, 0.0), jnp.where(holder + segment > PCAP, 1.0, 0.0)
    )
    mark_ref[...] = jnp.broadcast_to(jnp.max(over), (1, 128))
    owner = jnp.minimum(owner, float(ZCAP)).astype(I32) + ((row & 3) * 4 + (col >> 5)) * ZBUF
    holder = jnp.minimum(holder, float(PCAP + 1)).astype(I32) + (row >> 2) * PBUF
    table_ref[...] = jnp.where((col & 1) == 0, owner, holder)
    for k in range(GENES):
        spread_ref[k] = jnp.transpose(jnp.broadcast_to(weight_ref[pl.ds(k, 1), :], (128, VT)))


def ready_kernel(
    src_ref, rows_ref, probes_ref, used_ref, count_ref, value_ref, parts_ref, turned_ref
):
    count = jnp.zeros((128, 128), F32)
    for t in range(TILES // 8):
        highs, lows, _ = source_parts(src_ref, t, 8)
        count += dot(one_hots(highs), one_hots(lows), 1, 1)
    count_ref[...] = count
    used_ref[...] = jnp.minimum(count, 1.0)
    col = iota((128, 128), 1)
    high = probes_ref[...].astype(BF16).astype(F32)
    parts_ref[...] = jnp.concatenate([high, probes_ref[...] - high], axis=0).astype(BF16)
    turned_ref[...] = jnp.zeros_like(turned_ref)
    for k in range(DEV // 128):
        turned_ref[pl.ds(k * 128, 128), pl.ds(0, SLOTS)] = jnp.transpose(rows_ref[:, pl.ds(k * 128, 128)])
    value = turned_ref[pl.ds(0, 128, stride=NX), :]
    for x in range(1, NX):
        turned = pltpu.roll(turned_ref[pl.ds(x, 128, stride=NX), :], x * LANE, 1)
        value = jnp.where((col >> 5) == x, turned, value)
    value_ref[...] = value + 1


def send_kernel(used_ref, value_ref, parts_ref, out_ref, index_ref, high_ref, low_ref, done, sem):
    used = used_ref[...]
    flag = ones_where(used > 0.5)
    row, col = iota((128, 128), 0), iota((128, 128), 1)
    number = dot(flag, jnp.ones((128, 128), BF16))
    start = dot(ones_where(((row >> 3) == (col >> 3)) & (col < row)), number.astype(BF16))
    place = (start + dot(flag, ones_where(row < col))).astype(I32)
    place = place + jnp.where(place >= ZB - 1, 1, 0)
    high_ref[...] = jnp.where(used > 0.5, place >> 7, -1)
    low_ref[...] = place & (ZB - 1)
    which = iota((8, 128), 0)
    at = iota((ZB, 128), 0).astype(jnp.int16)
    subject = (iota((ROWS, 4 * ZB), 0) + 1).astype(jnp.int16)

    def list_of(z):
        values, places = [], []
        for y in range(NY):
            for c in range(NC):
                i = z * (NY * NC) + y * NC + c
                value = value_ref[pl.ds(y * (NZ * NC) + z * NC + c, 1), :]
                digit = jnp.where(which < 2, value >> 5, value & 31)
                match = ((which & 1) == high_ref[pl.ds(i, 1), :]) & (which < 4)
                values.append(jnp.where(match, digit, 0).astype(F32).astype(BF16))
                places.append(ones16(at == low_ref[pl.ds(i, 1), :].astype(jnp.int16)))
        listed = dot(jnp.concatenate(values, axis=1), jnp.concatenate(places, axis=1), 1, 1)
        index = listed[:2] * 32.0 + listed[2:4]
        index = jnp.concatenate([index[:1], index[1:]], axis=1)
        index_ref[pl.ds(z, 1), :] = index
        return index

    def lists_of(i):
        return jnp.concatenate([list_of(2 * i), list_of(2 * i + 1)], axis=1)

    def step(i, index):
        later = lists_of(jnp.minimum(i + 1, NZ // 2 - 1))
        rows = dot(parts_ref[...], ones16(subject == short(index)))
        rows = rows[:PROBES] + rows[PROBES:]
        for n in range(2):
            left, right = rows[:, 2 * n * ZB : (2 * n + 1) * ZB], rows[:, (2 * n + 1) * ZB : (2 * n + 2) * ZB]
            done[2 * i + n] = jnp.transpose(jnp.concatenate([left, right], axis=0))
        leave(i).start()
        return later

    def leave(i):
        part = pl.ds(2 * i, 2)
        return pltpu.make_async_copy(done.at[part], out_ref.at[part], sem.at[i])

    lax.fori_loop(0, NZ // 2, step, lists_of(0), unroll=True)
    for i in range(NZ // 2):
        leave(i).wait()


def relay_kernel(table, mark_ref, in_ref, out_ref, zbuf, pbuf, done, sem):
    for z in range(NZ):
        left, right = both(in_ref[z])
        zbuf[pl.ds(z * ZBUF, ZB), :] = left
        zbuf[pl.ds(z * ZBUF + ZB - 1, ZB), :] = right
    left = lanes64((PB, 128))
    copies = []
    for r in range(PLANE):
        for z in range(NZ):
            row, col = r * 4 + z // 4, (z % 4) * LANE
            pbuf[pl.ds(table[row, col + 1], SLOTS), :] = zbuf[pl.ds(table[row, col], SLOTS), :]
        done[r] = jnp.where(left, pbuf[pl.ds(r * PBUF, PB), :], pbuf[pl.ds(r * PBUF + PB - 1, PB), :])
        done[r, pl.ds(PB - 1, 1), :] = mark_ref[...]
        if r % 8 == 7:
            part = pl.ds(r - 7, 8)
            copies.append(pltpu.make_async_copy(done.at[part], out_ref.at[part], sem.at[r // 8]))
            copies[-1].start()
    for copy in copies:
        copy.wait()


def back_kernel(table, in_ref, out_ref, zbuf, pbuf, done, sem):
    mark = jnp.zeros((1, 128), F32)
    for r in range(PLANE):
        left, right = both(in_ref[r])
        pbuf[pl.ds(r * PBUF, PB), :] = left
        pbuf[pl.ds(r * PBUF + PB - 1, PB), :] = right
        mark = jnp.maximum(mark, in_ref[r, pl.ds(PB - 1, 1), :])
    left = lanes64((ZB, 128))
    copies = []
    for z in range(NZ):
        for r in range(PLANE):
            row, col = r * 4 + z // 4, (z % 4) * LANE
            zbuf[pl.ds(table[row, col], SLOTS), :] = pbuf[pl.ds(table[row, col + 1], SLOTS), :]
        done[z] = jnp.where(left, zbuf[pl.ds(z * ZBUF, ZB), :], zbuf[pl.ds(z * ZBUF + ZB - 1, ZB), :])
        done[z, pl.ds(ZB - 1, 1), :] = mark
        if z % 4 == 3:
            part = pl.ds(z - 3, 4)
            copies.append(pltpu.make_async_copy(done.at[part], out_ref.at[part], sem.at[z // 4]))
            copies[-1].start()
    for copy in copies:
        copy.wait()


def gene_kernel(
    addr,
    again,
    gene,
    addr_ref,
    in_ref,
    dose_ref,
    turned_ref,
    weight_ref,
    out_ref,
    moment_ref,
    held,
    total,
    weighted,
    work,
    near,
    done,
    sem,
    out_sem,
):
    def fetch(group, slot):
        return pltpu.make_async_copy(
            addr_ref.at[pl.ds(lax.rem(group, GROUPS) * GROUP, GROUP), :], near.at[slot], sem.at[slot]
        )

    fetch(0, 0).start()
    fetch(1, 1).start()
    mark = jnp.zeros((1, 128), F32)
    for m in range(PLANE):
        left, right = both(in_ref[m])
        held[pl.ds(m * 2 * PB, PB), :] = left
        held[pl.ds(m * 2 * PB + PB, PB), :] = right
        mark = jnp.maximum(mark, in_ref[m, pl.ds(PB - 1, 1), :])
    held[pl.ds(HOLD, 8), :] = jnp.zeros((8, 128), F32)
    total[...] = jnp.zeros_like(total)
    moment_ref[...] = jnp.zeros_like(moment_ref)

    def gather(slot, k):
        for c in range(TILE):
            work[k % 2, pl.ds(c, 1), :] = held[pl.ds(near[slot, k, c], 1), :]

    def score(t, k):
        dose = dose_ref[t]
        total[gene[t]] += dot(jnp.concatenate([dose, dose], axis=1), split(work[k % 2]))

    def scored(i, carry):
        for slot in range(2):
            group = i * 2 + slot
            fetch(group, slot).wait()
            for k in range(GROUP):
                gather(slot, k)
                score(jnp.maximum(group * GROUP + k - 1, 0), k + 1)
            fetch(group + 2, slot).start()
        return carry

    work[1] = jnp.zeros((TILE, 128), F32)
    lax.fori_loop(0, GROUPS // 2, scored, 0)
    score(TILES - 1, 1)
    for k in range(GENES):
        weight = weight_ref[k]
        scores = total[k] * weight
        one = jnp.sum(scores * scores, axis=0, keepdims=True) * (1.0 / VT)
        moment_ref[k, pl.ds(0, 1), :] = one[:, :PROBES]
        weighted[k] = split(scores * weight)

    def returned(t, slot):
        scale = jnp.where(t < TILES, 1.0 / TILE, 0.0)
        t = jnp.minimum(t, TILES - 1)
        dose = turned_ref[t]
        rows = dot(jnp.concatenate([dose, dose], axis=1), weighted[gene[t]])
        two = jnp.sum(rows * rows, axis=0, keepdims=True) * scale
        moment_ref[gene[t], pl.ds(1, 1), :] += two[:, :PROBES]
        work[slot] = rows

    def scatter(slot, k):
        for c in range(TILE):
            held[pl.ds(near[slot, k, c], 1), :] = work[k % 2, pl.ds(c, 1), :]

    @pl.when(again[0, 0] == 0)
    def _():
        def sent(i, carry):
            for slot in range(2):
                group = i * 2 + slot
                fetch(group, slot).wait()
                for k in range(GROUP):
                    returned(group * GROUP + k + 1, (k + 1) % 2)
                    scatter(slot, k)
                fetch(group + 2, slot).start()
            return carry

        returned(0, 0)
        lax.fori_loop(0, GROUPS // 2, sent, 0)

    @pl.when(again[0, 0] != 0)
    def _():
        held[...] = jnp.zeros_like(held)

        def summed(t, carry):
            returned(t, 0)

            def add(c, inner):
                held[pl.ds(addr[t, c], 1), :] += work[0, pl.ds(c, 1), :]
                return inner

            lax.fori_loop(0, TILE, add, 0)
            return carry

        lax.fori_loop(0, TILES, summed, 0)

    fetch(0, 0).wait()
    fetch(1, 1).wait()
    left = lanes64((PB, 128))
    copies = []
    for m in range(PLANE):
        done[m] = jnp.where(left, held[pl.ds(m * 2 * PB, PB), :], held[pl.ds(m * 2 * PB + PB, PB), :])
        done[m, pl.ds(PB - 1, 1), :] = mark
        if m % 8 == 7:
            part = pl.ds(m - 7, 8)
            copies.append(pltpu.make_async_copy(done.at[part], out_ref.at[part], out_sem.at[m // 8]))
            copies[-1].start()
    for copy in copies:
        copy.wait()


def sum_kernel(in_ref, index_ref, out_ref, mark_ref, total):
    at = (iota((ROWS, 8 * ZB), 0) + 1).astype(jnp.int16)

    def step(i, mark):
        rows, indices = [], []
        for n in range(4):
            z = i * 4 + n
            turned = jnp.transpose(in_ref[z])
            rows += [turned[:PROBES], turned[PROBES:]]
            indices.append(index_ref[pl.ds(z, 1), :])
            mark = jnp.maximum(mark, in_ref[z, pl.ds(ZB - 1, 1), :])
        index = jnp.concatenate(indices, axis=1)
        rows = jnp.where(index > 0.5, jnp.concatenate(rows, axis=1), 0.0)
        high = rows.astype(BF16).astype(F32)
        parts = jnp.concatenate([high, rows - high], axis=0).astype(BF16)
        sums = dot(parts, ones16(at == short(index)), 1, 1)
        total[...] = sums if i == 0 else total[...] + sums
        return mark

    mark = jnp.zeros((1, 128), F32)
    for i in range(NZ // 4):
        mark = step(i, mark)
    mark_ref[...] = mark
    out_ref[...] = total[pl.ds(0, PROBES), :] + total[pl.ds(PROBES, PROBES), :]


def turn_kernel(dose_ref, out_ref):
    def step(t, carry):
        out_ref[t] = jnp.transpose(dose_ref[t].astype(F32)).astype(BF16)
        return carry

    lax.fori_loop(0, TILES, step, 0)


VMEM = pl.BlockSpec(memory_space=pltpu.VMEM)
SMEM = pl.BlockSpec(memory_space=pltpu.SMEM)
HBM = pl.BlockSpec(memory_space=pl.ANY)


def call(kernel, outs, ins, scratch=(), out_specs=None, cost=2_000_000, limit=24):
    shapes = [jax.ShapeDtypeStruct(*o) for o in outs]
    return pl.pallas_call(
        kernel,
        out_shape=shapes,
        in_specs=ins,
        out_specs=[VMEM] * len(shapes) if out_specs is None else out_specs,
        scratch_shapes=list(scratch),
        cost_estimate=pl.CostEstimate(flops=cost * 100, bytes_accessed=cost, transcendentals=0),
        compiler_params=pltpu.CompilerParams(vmem_limit_bytes=limit << 20),
    )


def packed(probes, dosages, weights, send_rows, tile_src, tile_gene):
    zdone, pdone = [pltpu.VMEM((NZ, ZB, 128), F32)], [pltpu.VMEM((PLANE, PB, 128), F32)]
    four = [pltpu.SemaphoreType.DMA((4,))]
    used, count, value, parts = call(
        ready_kernel,
        [((128, 128), F32), ((128, 128), F32), ((128, 128), I32), ((2 * PROBES, ROWS), BF16)],
        [VMEM] * 3,
        [pltpu.VMEM((DEV, 128), I32)],
    )(tile_src, send_rows[0].T, probes)
    asked = lax.all_to_all(used.reshape(PLANE, 4, 128), FLAT, 0, 0, tiled=True).reshape(128, 128)
    (met,) = call(meet_kernel, [((NZ, 8, 128), F32)], [VMEM])(asked)
    met = lax.all_to_all(met, "z", 0, 0, tiled=True).reshape(128, 128)
    asked, count, met, doses = lax.optimization_barrier((asked, count, met, dosages))
    (turned,) = call(turn_kernel, [((TILES, TILE, VT), BF16)], [VMEM])(doses)
    table, mark, spread = call(
        table_kernel, [((128, 128), I32), ((1, 128), F32), ((GENES, VT, 128), F32)], [VMEM] * 2
    )(asked, weights)
    addr, again = call(
        place_kernel, [((TILES, TILE), I32), ((1, 1), I32)], [VMEM, VMEM], out_specs=[VMEM, SMEM]
    )(tile_src, count)
    block, index = call(
        send_kernel,
        [((NZ, ZB, 128), F32), ((NZ, 2 * ZB), F32)],
        [VMEM] * 3,
        [pltpu.VMEM((128, 128), I32)] * 2 + zdone + [pltpu.SemaphoreType.DMA((NZ // 2,))],
        out_specs=[HBM, VMEM],
    )(met, value, parts)
    block = lax.all_to_all(block, "z", 0, 0, tiled=True)
    block, addr, again, spread, table, mark, turned = lax.optimization_barrier(
        (block, addr, again, spread, table, mark, turned)
    )
    buffers = [pltpu.VMEM((NZ * ZBUF, 128), F32), pltpu.VMEM((PLANE * PBUF, 128), F32)]
    (block,) = call(relay_kernel, [((PLANE, PB, 128), F32)], [SMEM, VMEM, VMEM], buffers + pdone + four, out_specs=[HBM])(
        table, mark, block
    )
    block = lax.all_to_all(block, FLAT, 0, 0, tiled=True)
    block, moments = call(
        gene_kernel,
        [((PLANE, PB, 128), F32), ((GENES, 2, PROBES), F32)],
        [SMEM] * 3 + [VMEM] * 5,
        [
            pltpu.VMEM((HOLD + 8, 128), F32),
            pltpu.VMEM((GENES, VT, 128), F32),
            pltpu.VMEM((GENES, 2 * VT, 128), BF16),
            pltpu.VMEM((2, TILE, 128), F32),
            pltpu.SMEM((2, GROUP, TILE), I32),
        ]
        + pdone
        + [pltpu.SemaphoreType.DMA((2,))]
        + four,
        out_specs=[HBM, VMEM],
    )(addr, again, tile_gene, addr, block, dosages, turned, spread)
    block = lax.all_to_all(block, FLAT, 0, 0, tiled=True)
    (block,) = call(
        back_kernel, [((NZ, ZB, 128), F32)], [SMEM, VMEM], buffers + zdone + four, out_specs=[HBM]
    )(table, block)
    block = lax.all_to_all(block, "z", 0, 0, tiled=True)
    projected, mark = call(
        sum_kernel,
        [((PROBES, ROWS), F32), ((1, 128), F32)],
        [VMEM] * 2,
        [pltpu.VMEM((2 * PROBES, ROWS), F32)],
    )(block, index)
    return projected, moments, mark[0, 0]


def exchange(rows):
    return lax.all_to_all(rows, ALL, 0, 0, tiled=True)


def whole(probes, dosages, weights, send_rows, tile_src, tile_gene):
    rows_sent = send_rows[0]
    high = lax.Precision.HIGHEST
    outgoing = probes.T[rows_sent].reshape(DEV, SLOTS * PROBES // 128, 128)
    incoming = exchange(outgoing).reshape(SRC, PROBES)
    fetched = jnp.concatenate([incoming, jnp.zeros((1, PROBES), F32)], axis=0)
    slab = fetched[tile_src]
    tile_scores = jnp.einsum("tcb,tvc->tbv", slab, dosages, precision=high, preferred_element_type=F32)
    member = (tile_gene[None, :] == jnp.arange(GENES, dtype=I32)[:, None]).astype(F32)
    scores = jnp.einsum("gt,tbv->gbv", member, tile_scores, precision=high) * weights[:, None, :]
    one = jnp.sum(scores * scores, axis=2) / VT
    weighted = jnp.einsum("gt,gbv->tbv", member, scores * weights[:, None, :], precision=high)
    returned = jnp.einsum("tbv,tvc->tcb", weighted, dosages, precision=high, preferred_element_type=F32)
    two = jnp.dot(member, jnp.sum(returned * returned, axis=1), precision=high) / TILE
    sums = jax.ops.segment_sum(returned.reshape(-1, PROBES), tile_src.reshape(-1), num_segments=SRC + 1)
    arrived = exchange(sums[:SRC].reshape(DEV, SLOTS * PROBES // 128, 128))
    projected = jax.ops.segment_sum(
        arrived.reshape(SRC, PROBES), rows_sent.reshape(-1), num_segments=ROWS
    ).T
    return projected, jnp.stack([one, two], axis=1)


def shards(*args):
    projected, moments, mark = packed(*args)
    projected, moments = lax.cond(mark > 0.5, lambda: whole(*args), lambda: (projected, moments))
    return projected, moments.transpose(1, 2, 0)


def solution(mesh):
    fine = Mesh(mesh.devices.reshape(NY, NZ, NC, NX), ALL)
    placed = (P(None, ALL), P(ALL, None, None), P(ALL, None), P(ALL, None, None), P(ALL, None), P(ALL))
    return jax.shard_map(
        shards,
        mesh=fine,
        in_specs=placed,
        out_specs=(P(None, ALL), P(None, None, ALL)),
        check_vma=False,
    )
```
